256 devices in a mesh: shot: 2 (over x_lo), space: 128 (over z, x_hi, y, core).
Axes of the slice: x: 4 (x_hi: 2, x_lo: 2; x = x_hi * 2 + x_lo), y: 4, z: 8, core: 2. Of those that a mesh axis runs over, the one named last changes fastest.
Arguments:
- pressure_now: float32 [4, 128, 4, 128, 128], P('shot', 'space'), may hold values from -6 to 6
- pressure_old: float32 [4, 128, 4, 128, 128], P('shot', 'space'), may hold values from -6 to 6
- auxiliary_now: float32 [4, 128, 4, 128, 128], P('shot', 'space'), may hold values from -6 to 6
- auxiliary_old: float32 [4, 128, 4, 128, 128], P('shot', 'space'), may hold values from -6 to 6
- velocity: float32 [128, 4, 128, 128], P('space', 'shot'), may hold values from 1.5 to 4
- epsilon_field: float32 [128, 4, 128, 128], P('space', 'shot'), may hold values from 0.1 to 0.3
- delta_field: float32 [128, 4, 128, 128], P('space', 'shot'), may hold values from 0 to 0.1
- active_blocks: int32 [4, 128], P('shot', 'space'), may hold values 0 or 1
- source_cells: int32 [4], P('shot'), may hold values from 0 to 8388607
- receiver_cells: int32 [4, 256], P('shot'), may hold values from 0 to 8388607
- wavelet: float32 [4, 4], P('shot'), may hold values from -4 to 4
Outputs:
- pressure_final: float32 [4, 128, 4, 128, 128], P('shot', 'space')
- auxiliary_final: float32 [4, 128, 4, 128, 128], P('shot', 'space')
- traces: float32 [4, 4, 256], P('shot')
The draws below stay inside these ranges and needn't reach their ends.
Inputs may be any that keep to these rules, and one draw needn't show every extreme that they name: `source_cells`: cell numbers of the aperture. `receiver_cells`: cell numbers of the aperture.
All inputs are finite; a program needn't handle non-finite values. No bound on the sum of `active_blocks` on one device may be relied on, other than what follows from the above.
Results may differ from the reference program's by a relative error of at most 0.00002.
Values sent between devices are 32-bit elements; how exact they have to be, the bound alone decides.
No kernel may reach another device: no remote copies, remote signals or barrier semaphores. Data moves between devices by JAX's collectives and lax.ppermute only.
A program may use at most 64 MiB of HBM per device.

```python
import jax
import jax.numpy as jnp
from jax import lax

CX = 4
CY = 128
CZ = 128
GX = 128
BLOCKS = 128
NCELL = 8388608
SHOTS = 4
STEPS = 4
RECV = 256


def set_ends(array, rng, smallest, largest):
    extent = array.shape
    place = [jax.random.randint(jax.random.fold_in(rng, axis), (), 0, extent[axis]) for axis in range(len(extent))]
    array = array.at[tuple(place)].set(smallest)
    longest = extent.index(max(extent))
    place[longest] = (place[longest] + 1) % extent[longest]
    return array.at[tuple(place)].set(largest)


def block_scale(rng, extent, split, smallest, top_value):
    loudness = 1.0
    for axis_at, blocks in split:
        draws = jax.random.uniform(jax.random.fold_in(jax.random.fold_in(rng, 6), axis_at), (blocks,), jnp.float32, smallest / len(split), top_value / len(split))
        loudness = loudness * jnp.repeat(jnp.exp(draws), extent[axis_at] // blocks).reshape((-1,) + (1,) * (len(extent) - 1 - axis_at))
    return loudness


def normal_values(rng, extent, spread, most, cuts=(), kind=jnp.bfloat16):
    gain = block_scale(rng, extent, cuts, -0.22, 0.18) if cuts else 1.0
    drawn = jax.random.normal(rng, extent, jnp.float32) * spread * gain
    return jnp.minimum(jnp.maximum(drawn, -most), most).astype(kind)


def setup_inputs(seed: int = 0) -> dict:
    splits = jax.random.split(jax.random.key(seed), 12)
    pressure_now = normal_values(splits[0], (SHOTS, BLOCKS, CX, CY, CZ), 1.0, 6.0, ((0, 2), (1, 128)), jnp.float32)
    pressure_old = normal_values(splits[1], (SHOTS, BLOCKS, CX, CY, CZ), 1.0, 6.0, ((0, 2), (1, 128)), jnp.float32)
    auxiliary_now = normal_values(splits[2], (SHOTS, BLOCKS, CX, CY, CZ), 1.0, 6.0, ((0, 2), (1, 128)), jnp.float32)
    auxiliary_old = normal_values(splits[3], (SHOTS, BLOCKS, CX, CY, CZ), 1.0, 6.0, ((0, 2), (1, 128)), jnp.float32)
    velocity = jnp.clip(1.5 + 2.5 * jax.random.uniform(splits[4], (BLOCKS, CX, CY, CZ), jnp.float32) ** block_scale(splits[4], (BLOCKS, CX, CY, CZ), ((0, 128), (1, 2)), -0.2, 0.2), 1.5, 4.0)
    epsilon_field = jnp.clip(0.1 + 0.20000001043081284 * jax.random.uniform(splits[5], (BLOCKS, CX, CY, CZ), jnp.float32) ** block_scale(splits[5], (BLOCKS, CX, CY, CZ), ((0, 128), (1, 2)), -0.2, 0.2), 0.1, 0.3)
    delta_field = jnp.clip(0.1 * jax.random.uniform(splits[6], (BLOCKS, CX, CY, CZ), jnp.float32) ** block_scale(splits[6], (BLOCKS, CX, CY, CZ), ((0, 128), (1, 2)), -0.2, 0.2), 0.0, 0.1)
    active_blocks = set_ends((jax.random.randint(splits[7], (SHOTS, BLOCKS), 0, 4) < 3).astype(jnp.int32), jax.random.fold_in(splits[7], 1), 0, 1)
    source_cells = set_ends(jax.random.randint(splits[8], (SHOTS,), 0, NCELL), jax.random.fold_in(splits[8], 1), 0, NCELL - 1).astype(jnp.int32)
    receiver_cells = set_ends(jax.random.randint(splits[9], (SHOTS, RECV), 0, NCELL), jax.random.fold_in(splits[9], 1), 0, NCELL - 1).astype(jnp.int32)
    wavelet = normal_values(splits[10], (SHOTS, STEPS), 1.0, 4.0, ((0, 2),), jnp.float32)
    return {"pressure_now": pressure_now, "pressure_old": pressure_old, "auxiliary_now": auxiliary_now, "auxiliary_old": auxiliary_old, "velocity": velocity, "epsilon_field": epsilon_field, "delta_field": delta_field, "active_blocks": active_blocks, "source_cells": source_cells, "receiver_cells": receiver_cells, "wavelet": wavelet}


stencil_taps = (-205.0 / 72.0, 8.0 / 5.0, -1.0 / 5.0, 8.0 / 315.0, -1.0 / 560.0)
step_ratio = 0.08

def second_diff(padded, along, length):

    def window(offset):
        return lax.slice_in_dim(padded, 4 + offset, 4 + offset + length, axis=along)
    summed = stencil_taps[0] * window(0)
    for offset in range(1, 5):
        summed = summed + stencil_taps[offset] * (window(offset) + window(-offset))
    return summed

def to_grid(blocks):
    return blocks.reshape(GX * CX, CY, CZ)

def to_blocks(grid):
    return grid.reshape(GX, CX, CY, CZ)

def grid_coords(cell_ids):
    block = cell_ids // (CX * CY * CZ)
    inside = cell_ids % (CX * CY * CZ)
    coord_x = block * CX + inside // (CY * CZ)
    coord_y = inside // CZ % CY
    coord_z = inside % CZ
    return (coord_x, coord_y, coord_z)

def reference(pressure_now, pressure_old, auxiliary_now, auxiliary_old, velocity, epsilon_field, delta_field, active_blocks, source_cells, receiver_cells, wavelet):
    courant = (to_grid(velocity) * step_ratio) ** 2
    stretch = 1.0 + 2.0 * to_grid(epsilon_field)
    coupling = jnp.sqrt(1.0 + 2.0 * to_grid(delta_field))
    block_ids = jnp.arange(BLOCKS, dtype=jnp.int32)
    finals_p = []
    finals_q = []
    recorded = []
    for shot_index in range(SHOTS):
        source_block = source_cells[shot_index] // (CX * CY * CZ)
        live_blocks = jnp.maximum(active_blocks[shot_index], (block_ids == source_block).astype(jnp.int32)).astype(jnp.float32)
        live_mask = to_grid(jnp.broadcast_to(live_blocks[:, None, None, None], (BLOCKS, CX, CY, CZ)))
        pressure = to_grid(pressure_now[shot_index]) * live_mask
        pressure_prev = to_grid(pressure_old[shot_index]) * live_mask
        auxiliary = to_grid(auxiliary_now[shot_index]) * live_mask
        auxiliary_prev = to_grid(auxiliary_old[shot_index]) * live_mask
        source_x, source_y, source_z = grid_coords(source_cells[shot_index])
        recv_x, recv_y, recv_z = grid_coords(receiver_cells[shot_index])
        samples = []
        for time_step in range(STEPS):
            padded_x = jnp.pad(pressure, ((4, 4), (0, 0), (0, 0)))
            padded_y = jnp.pad(pressure, ((0, 0), (4, 4), (0, 0)))
            padded_z = jnp.pad(auxiliary, ((0, 0), (0, 0), (4, 4)))
            horizontal = second_diff(padded_x, 0, pressure.shape[0]) + second_diff(padded_y, 1, pressure.shape[1])
            vertical = second_diff(padded_z, 2, auxiliary.shape[2])
            new_p = 2.0 * pressure - pressure_prev + courant * (stretch * horizontal + coupling * vertical)
            new_q = 2.0 * auxiliary - auxiliary_prev + courant * (coupling * horizontal + vertical)
            new_p = new_p.at[source_x, source_y, source_z].add(wavelet[shot_index, time_step])
            new_q = new_q.at[source_x, source_y, source_z].add(wavelet[shot_index, time_step])
            new_p = new_p * live_mask
            new_q = new_q * live_mask
            samples.append(new_p[recv_x, recv_y, recv_z])
            pressure_prev, pressure = (pressure, new_p)
            auxiliary_prev, auxiliary = (auxiliary, new_q)
        finals_p.append(to_blocks(pressure))
        finals_q.append(to_blocks(auxiliary))
        recorded.append(jnp.stack(samples, axis=0))
    return (jnp.stack(finals_p, axis=0), jnp.stack(finals_q, axis=0), jnp.stack(recorded, axis=0))
```

```python
import functools

import jax
import jax.numpy as jnp
from jax import lax
from jax.experimental import pallas as pl
from jax.experimental.pallas import tpu as pltpu
from jax.sharding import PartitionSpec as P

STEPS = 4
CX, CY, CZ = 4, 128, 128
ROWS = CX * CY
CELLS = ROWS * CZ

taps = (-205.0 / 72.0, 8.0 / 5.0, -1.0 / 5.0, 8.0 / 315.0, -1.0 / 560.0)
step_ratio = 0.08

VMEM = pl.BlockSpec(memory_space=pltpu.VMEM)
SMEM = pl.BlockSpec(memory_space=pltpu.SMEM)
EXACT = lax.Precision.HIGHEST


def shape(*dims, dtype=jnp.float32):
    return jax.ShapeDtypeStruct(dims, dtype)


def call(kernel, ins, outs, flops, name):
    moved = 4 * sum(int(jnp.size(a)) for a in ins) + 4 * sum(o.size for o in outs)
    specs = [SMEM if a.size <= 64 else VMEM for a in ins]
    return pl.pallas_call(
        kernel,
        out_shape=tuple(outs),
        in_specs=specs,
        out_specs=tuple(VMEM for _ in outs),
        compiler_params=pltpu.CompilerParams(vmem_limit_bytes=24 << 20),
        cost_estimate=pl.CostEstimate(flops=flops, bytes_accessed=moved, transcendentals=0),
        name=name,
    )(*ins)


def live_of(at_ref, active_ref, source_ref, s):
    here = source_ref[s] // CELLS == at_ref[0]
    return jnp.where(here | (active_ref[s, 0] == 1), 1.0, 0.0)


def row(x):
    return pl.ds(x * CY, CY)


def begin_kernel(at_ref, active_ref, source_ref, p_ref, v_ref, e_ref, d_ref, p0_ref, own_ref, odd_ref):
    for s in range(2):
        p0_ref[s] = p_ref[s] * live_of(at_ref, active_ref, source_ref, s)
    courant = (v_ref[...] * step_ratio) * (v_ref[...] * step_ratio)
    coupling = jnp.sqrt(1.0 + 2.0 * d_ref[...])
    own_ref[0] = courant
    own_ref[1] = courant * (1.0 + 2.0 * e_ref[...])
    own_ref[2] = courant * coupling
    odd_ref[...] = jnp.full(odd_ref.shape, at_ref[0] & 1, jnp.int32)


def band():
    apart = jnp.abs(lax.broadcasted_iota(jnp.int32, (CZ, CZ), 0) - lax.broadcasted_iota(jnp.int32, (CZ, CZ), 1))
    out = jnp.zeros((CZ, CZ), jnp.float32)
    for k in range(5):
        out = jnp.where(apart == k, taps[k], out)
    return out


def local_part(s, at_ref, source_ref, wavelet_ref, step, p, po, q, qo, c_ref, cs_ref, ck_ref, pre_p, pre_q, mat):
    for x in range(CX):
        here = row(x)
        hor = jnp.dot(mat, p[s, here, :], precision=EXACT, preferred_element_type=jnp.float32)
        for other in range(CX):
            hor = hor + taps[abs(other - x)] * p[s, row(other), :]
        ver = jnp.dot(q[s, here, :], mat, precision=EXACT, preferred_element_type=jnp.float32)
        pre_p[s, here, :] = 2.0 * p[s, here, :] - po[s, here, :] + (cs_ref[s, here, :] * hor + ck_ref[s, here, :] * ver)
        pre_q[s, here, :] = 2.0 * q[s, here, :] - qo[s, here, :] + (ck_ref[s, here, :] * hor + c_ref[s, here, :] * ver)
    cell = source_ref[s] % CELLS
    gain = jnp.where(source_ref[s] // CELLS == at_ref[0], wavelet_ref[s, step], 0.0)
    lane = lax.broadcasted_iota(jnp.int32, (1, CZ), 1)
    add = jnp.where(lane == cell % CZ, gain, 0.0)
    line = pl.ds(cell // CZ, 1)
    pre_p[s, line, :] = pre_p[s, line, :] + add
    pre_q[s, line, :] = pre_q[s, line, :] + add


def first_kernel(at_ref, side_ref, active_ref, source_ref, wavelet_ref, p0, p_old, q_now, q_old, own, other,
                 pre_p, pre_q, po, q, c_ref, cs_ref, ck_ref):
    half = ROWS // 2
    mat = band()
    for s in range(2):
        live = live_of(at_ref, active_ref, source_ref, s)
        po[s] = p_old[s] * live
        q[s] = q_now[s] * live
        for k, ref in enumerate((c_ref, cs_ref, ck_ref)):
            mine = pl.ds(pl.multiple_of(side_ref[0] * half, half), half)
            theirs = pl.ds(pl.multiple_of((1 - side_ref[0]) * half, half), half)
            ref[s, mine, :] = own[k] * live
            ref[s, theirs, :] = other[k] * live
    for s in range(2):
        live = live_of(at_ref, active_ref, source_ref, s)
        pre_q[s] = q_old[s] * live
        local_part(s, at_ref, source_ref, wavelet_ref, 0, p0, po, q, pre_q, c_ref, cs_ref, ck_ref, pre_p, pre_q, mat)


def local_kernel(step, at_ref, source_ref, wavelet_ref, p, po, q, qo, c_ref, cs_ref, ck_ref, pre_p, pre_q):
    mat = band()
    for s in range(2):
        local_part(s, at_ref, source_ref, wavelet_ref, step, p, po, q, qo, c_ref, cs_ref, ck_ref, pre_p, pre_q, mat)


def halo_kernel(odd_ref, even_pair, odd_pair, pre_p, pre_q, cs_ref, ck_ref, p, q):
    odd = odd_ref[...] == 1
    for s in range(2):
        for tile in range(CY // 8):
            def at(x):
                return pl.ds(x * CY + tile * 8, 8)
            a = [even_pair[s, at(x), :] for x in range(CX)]
            b = [odd_pair[s, at(x), :] for x in range(CX)]
            lower = [jnp.where(odd, a[x], b[x]) for x in range(CX)]
            upper = [jnp.where(odd, b[x], a[x]) for x in range(CX)]
            for x in range(CX):
                hor = taps[4] * (lower[x] + upper[x])
                for k in range(1, 4):
                    if x + k < CX:
                        hor = hor + taps[4 - k] * lower[x + k]
                    if x - k >= 0:
                        hor = hor + taps[4 - k] * upper[x - k]
                p[s, at(x), :] = pre_p[s, at(x), :] + cs_ref[s, at(x), :] * hor
                q[s, at(x), :] = pre_q[s, at(x), :] + ck_ref[s, at(x), :] * hor


def samples(field, s, pick_z, pick_y):
    out = []
    for x in range(CX):
        spread = jnp.dot(field[s, row(x), :], pick_z, precision=EXACT, preferred_element_type=jnp.float32)
        out.append(jnp.sum(jnp.where(pick_y, spread, 0.0), axis=0, keepdims=True))
    return out


def picks(cells_ref, s):
    cells = cells_ref[pl.ds(s, 1), :]
    n = cells.shape[1]
    inside = cells % CELLS
    pick_z = jnp.where(lax.broadcasted_iota(jnp.int32, (CZ, n), 0) == inside % CZ, 1.0, 0.0)
    pick_y = lax.broadcasted_iota(jnp.int32, (CY, n), 0) == (inside // CZ) % CY
    return cells // CELLS, inside // (CY * CZ), pick_z, pick_y


def own_sample(values, block, x_at, me):
    out = jnp.zeros(block.shape, jnp.float32)
    for x in range(CX):
        out = jnp.where((x_at == x) & (block == me), values[x], out)
    return out


def sample_kernel(at_ref, cells_ref, *refs):
    fields, out_ref = refs[:-1], refs[-1]
    out_ref[...] = jnp.zeros(out_ref.shape, jnp.float32)
    for s in range(2):
        block, x_at, pick_z, pick_y = picks(cells_ref, s)
        for n, field in enumerate(fields):
            out_ref[s, pl.ds(n, 1), :] = own_sample(samples(field, s, pick_z, pick_y), block, x_at, at_ref[0])


def last_sample_kernel(at_ref, cells_ref, early_ref, p3, pre_p, out_ref):
    me = at_ref[0]
    out_ref[...] = early_ref[...]
    for s in range(2):
        block, x_at, pick_z, pick_y = picks(cells_ref, s)
        values = samples(p3, s, pick_z, pick_y)
        out_ref[s, pl.ds(3, 1), :] = own_sample(values, block, x_at, me)
        out_ref[s, pl.ds(4, 1), :] = own_sample(samples(pre_p, s, pick_z, pick_y), block, x_at, me)
        hor = jnp.zeros(block.shape, jnp.float32)
        for x in range(CX):
            apart = jnp.where(block == me + 1, x_at + 4 - x, jnp.where(block == me - 1, 4 + x - x_at, 9))
            for k in range(1, 5):
                hor = hor + jnp.where(apart == k, taps[k] * values[x], 0.0)
        out_ref[s, pl.ds(5, 1), :] = hor


def even_pairs(n):
    return [(i, i ^ 1) for i in range(n)]


def odd_pairs(n):
    up = [(i, i + 1) for i in range(1, n - 1, 2)]
    return up + [(b, a) for a, b in up]


def stages(n):
    if n != 128:
        bit, out = 1, []
        while bit < n:
            out.append([(i, i ^ bit) for i in range(n)])
            bit *= 2
        return out

    def device(z, xh, y, core):
        return ((z * 2 + xh) * 4 + y) * 2 + core

    def pairs(move):
        return [
            (device(z, xh, y, core), device(*move(z, xh, y, core)))
            for z in range(8) for xh in range(2) for y in range(4) for core in range(2)
        ]

    far = {0: 3, 3: 0, 4: 7, 7: 4, 1: 6, 6: 1, 2: 5, 5: 2}
    return [
        pairs(lambda z, xh, y, core: (z, xh, y, 1 - core)),
        pairs(lambda z, xh, y, core: (z, xh, y ^ 1, core)),
        pairs(lambda z, xh, y, core: (z, xh, 3 - y, core)),
        pairs(lambda z, xh, y, core: (z, 1 - xh, y, core)),
        pairs(lambda z, xh, y, core: (z ^ 1, xh, y, core)),
        pairs(lambda z, xh, y, core: ((z + 1 if z % 2 else z - 1) % 8, xh, y, core)),
        pairs(lambda z, xh, y, core: (far[z], xh, y, core)),
    ]


def per_device(pressure_now, pressure_old, auxiliary_now, auxiliary_old, velocity, epsilon_field, delta_field,
               active_blocks, source_cells, receiver_cells, wavelet):
    blocks = lax.axis_size("space")
    at = lax.axis_index("space").astype(jnp.int32).reshape(1)
    side = lax.axis_index("shot").astype(jnp.int32).reshape(1)
    fields = (2, ROWS, CZ)
    p_now, p_old, q_now, q_old = (a.reshape(fields) for a in (pressure_now, pressure_old, auxiliary_now, auxiliary_old))
    half = (ROWS // 2, CZ)
    speed, eps, delta = (a.reshape(half) for a in (velocity, epsilon_field, delta_field))
    field = shape(*fields)

    p, own, odd = call(
        begin_kernel, (at, active_blocks, source_cells, p_now, speed, eps, delta),
        (field, shape(3, *half), shape(8, CZ, dtype=jnp.int32)), 10**6, "begin")

    def exchange(values):
        return (lax.ppermute(values, "space", even_pairs(blocks)), lax.ppermute(values, "space", odd_pairs(blocks)))

    halos = exchange(p)
    other = lax.ppermute(own, "shot", [(0, 1), (1, 0)])
    pre_p, pre_q, po, q, c, cs, ck = call(
        first_kernel, (at, side, active_blocks, source_cells, wavelet, p, p_old, q_now, q_old, own, other),
        (field,) * 7, 10**8, "first")
    kept = []
    for step in range(STEPS):
        if step:
            pre_p, pre_q = call(
                functools.partial(local_kernel, step), (at, source_cells, wavelet, p, po, q, qo, c, cs, ck),
                (field, field), 10**8, f"local{step}")
        if step == 3:
            early, = call(
                sample_kernel, (at, receiver_cells, cs, kept[0], kept[1]),
                (shape(2, 8, receiver_cells.shape[1]),), 10**8, "sample_early")
            total, = call(
                last_sample_kernel, (at, receiver_cells, early, p, pre_p),
                (shape(2, 8, receiver_cells.shape[1]),), 10**8, "sample_late")
            for pairs in stages(blocks):
                total = total + lax.ppermute(total, "space", pairs)
        po, qo = p, q
        p, q = call(
            halo_kernel, (odd, *halos, pre_p, pre_q, cs, ck), (field, field), 10**6, f"halo{step}")
        kept.append(p)
        if step < STEPS - 1:
            halos = exchange(p)
    last = total[:, 4] + total[:, 0] * total[:, 5]
    traces = jnp.stack([total[:, 1], total[:, 2], total[:, 3], last], axis=1)
    return (p.reshape(pressure_now.shape), q.reshape(pressure_now.shape), traces)


def solution(mesh):
    grid = P("shot", "space", None, None, None)
    model = P("space", "shot", None, None)
    return jax.shard_map(
        per_device,
        mesh=mesh,
        in_specs=(grid, grid, grid, grid, model, model, model, P("shot", "space"), P("shot"), P("shot", None), P("shot", None)),
        out_specs=(grid, grid, P("shot", None, None)),
        check_vma=False,
    )
```

```python
import functools

import jax
import jax.numpy as jnp
from jax import lax
from jax.experimental import pallas as pl
from jax.experimental.pallas import tpu as pltpu
from jax.sharding import PartitionSpec as P

STEPS = 4
CX, CY, CZ = 4, 128, 128
ROWS = CX * CY
CELLS = ROWS * CZ

taps = (-205.0 / 72.0, 8.0 / 5.0, -1.0 / 5.0, 8.0 / 315.0, -1.0 / 560.0)
step_ratio = 0.08

VMEM = pl.BlockSpec(memory_space=pltpu.VMEM)
SMEM = pl.BlockSpec(memory_space=pltpu.SMEM)
FAR = pl.BlockSpec(memory_space=pltpu.HBM)
EXACT = lax.Precision.HIGHEST


def shape(*dims, dtype=jnp.float32):
    return jax.ShapeDtypeStruct(dims, dtype)


def call(kernel, ins, outs, flops, name, far=(), scratch=()):
    moved = 4 * sum(int(jnp.size(a)) for a in ins) + 4 * sum(o.size for o in outs)
    ins = [pltpu.with_memory_space_constraint(a, pltpu.HBM) if n in far else a for n, a in enumerate(ins)]
    specs = [FAR if n in far else SMEM if a.size <= 64 else VMEM for n, a in enumerate(ins)]
    return pl.pallas_call(
        kernel,
        out_shape=tuple(outs),
        in_specs=specs,
        out_specs=tuple(VMEM for _ in outs),
        scratch_shapes=scratch,
        compiler_params=pltpu.CompilerParams(vmem_limit_bytes=24 << 20),
        cost_estimate=pl.CostEstimate(flops=flops, bytes_accessed=moved, transcendentals=0),
        name=name,
    )(*ins)


def live_of(at_ref, active_ref, source_ref, s):
    here = source_ref[s] // CELLS == at_ref[0]
    return jnp.where(here | (active_ref[s] == 1), 1.0, 0.0)


def row(x):
    return pl.ds(x * CY, CY)


def model_kernel(v_far, e_far, d_far, own_ref, sems):
    copies = [pltpu.make_async_copy(src, own_ref.at[n], sems.at[n]) for n, src in enumerate((v_far, e_far, d_far))]
    for copy in copies:
        copy.start()
    for copy in copies:
        copy.wait()
    courant = (own_ref[0] * step_ratio) * (own_ref[0] * step_ratio)
    coupling = jnp.sqrt(1.0 + 2.0 * own_ref[2])
    own_ref[0] = courant
    own_ref[1] = courant * (1.0 + 2.0 * own_ref[1])
    own_ref[2] = courant * coupling


def begin_kernel(at_far, active_far, source_far, p_far, own_ref, p0_ref, odd_ref, live_ref, at_ref, active_ref, source_ref, sems):
    copies = [
        pltpu.make_async_copy(src, dst, sems.at[n])
        for n, (src, dst) in enumerate((
            (at_far, at_ref), (active_far, active_ref), (source_far, source_ref), (p_far, p0_ref)))
    ]
    for copy in copies:
        copy.start()
    for copy in copies:
        copy.wait()
    for s in range(2):
        live = live_of(at_ref, active_ref, source_ref, s)
        p0_ref[s] = p0_ref[s] * live
        live_ref[pl.ds(8 * s, 8), :] = jnp.full((8, CZ), live, jnp.float32)
    odd_ref[...] = jnp.full(odd_ref.shape, at_ref[0] & 1, jnp.int32)


def band():
    apart = jnp.abs(lax.broadcasted_iota(jnp.int32, (CZ, CZ), 0) - lax.broadcasted_iota(jnp.int32, (CZ, CZ), 1))
    out = jnp.zeros((CZ, CZ), jnp.float32)
    for k in range(5):
        out = jnp.where(apart == k, taps[k], out)
    return out


def second_diffs(s, x, p, q, mat):
    hor = jnp.dot(mat, p[s, row(x), :], precision=EXACT, preferred_element_type=jnp.float32)
    for other in range(CX):
        hor = hor + taps[abs(other - x)] * p[s, row(other), :]
    ver = jnp.dot(q[s, row(x), :], mat, precision=EXACT, preferred_element_type=jnp.float32)
    return hor, ver


def add_source(s, step, at_ref, source_ref, wavelet_ref, *refs):
    cell = source_ref[s] % CELLS
    gain = jnp.where(source_ref[s] // CELLS == at_ref[0], wavelet_ref[s, step], 0.0)
    lane = lax.broadcasted_iota(jnp.int32, (1, CZ), 1)
    add = jnp.where(lane == cell % CZ, gain, 0.0)
    line = pl.ds(cell // CZ, 1)
    for ref in refs:
        ref[s, line, :] = ref[s, line, :] + add


def ready_kernel(at_ref, active_ref, source_ref, wavelet_ref, p0, po_far, q_far, qo_far,
                 base_p, base_q, q, hor_ref, ver_ref, sems):
    copies = [
        pltpu.make_async_copy(src, dst, sems.at[n])
        for n, (src, dst) in enumerate(((q_far, q), (po_far, base_p), (qo_far, base_q)))
    ]
    for copy in copies:
        copy.start()
    mat = band()
    for copy in copies:
        copy.wait()
    for s in range(2):
        live = live_of(at_ref, active_ref, source_ref, s)
        q[s] = q[s] * live
        base_p[s] = 2.0 * p0[s] - base_p[s] * live
        base_q[s] = 2.0 * q[s] - base_q[s] * live
        for x in range(CX):
            hor_ref[s, row(x), :], ver_ref[s, row(x), :] = second_diffs(s, x, p0, q, mat)
        add_source(s, 0, at_ref, source_ref, wavelet_ref, base_p, base_q)


def halo_diff(x, lower, upper):
    hor = taps[4] * (lower[x] + upper[x])
    for k in range(1, 4):
        if x + k < CX:
            hor = hor + taps[4 - k] * lower[x + k]
        if x - k >= 0:
            hor = hor + taps[4 - k] * upper[x - k]
    return hor


def tile_at(x, tile):
    return pl.ds(x * CY + tile * 8, 8)


def halo_rows(s, tile, odd, even_pair, odd_pair):
    a = [even_pair[s, tile_at(x, tile), :] for x in range(CX)]
    b = [odd_pair[s, tile_at(x, tile), :] for x in range(CX)]
    return [jnp.where(odd, a[x], b[x]) for x in range(CX)], [jnp.where(odd, b[x], a[x]) for x in range(CX)]


def first_kernel(side_ref, live_ref, odd_ref, even_pair, odd_pair, own, other, base_p, base_q, hor_ref, ver_ref,
                 p, q, c_ref, cs_ref, ck_ref):
    odd = odd_ref[...] == 1

    def work(first, second):
        for tile in range(CY // 8):
            model = []
            for x in range(CX):
                half = (first, second)[x // 2]
                at = tile_at(x % 2, tile)
                model.append((half[0, at, :], half[1, at, :], half[2, at, :]))
            for s in range(2):
                live = live_ref[pl.ds(8 * s, 8), :]
                lower, upper = halo_rows(s, tile, odd, even_pair, odd_pair)
                for x in range(CX):
                    at = tile_at(x, tile)
                    c, cs, ck = (m * live for m in model[x])
                    c_ref[s, at, :], cs_ref[s, at, :], ck_ref[s, at, :] = c, cs, ck
                    hor = hor_ref[s, at, :] + halo_diff(x, lower, upper)
                    ver = ver_ref[s, at, :]
                    p[s, at, :] = base_p[s, at, :] + (cs * hor + ck * ver)
                    q[s, at, :] = base_q[s, at, :] + (ck * hor + c * ver)

    @pl.when(side_ref[0] == 0)
    def _():
        work(own, other)

    @pl.when(side_ref[0] == 1)
    def _():
        work(other, own)


def local_part(step, at_ref, source_ref, wavelet_ref, p, po, q, qo, c_ref, cs_ref, ck_ref, pre_p, pre_q):
    mat = band()
    for s in range(2):
        for x in range(CX):
            here = row(x)
            hor, ver = second_diffs(s, x, p, q, mat)
            pre_p[s, here, :] = 2.0 * p[s, here, :] - po[s, here, :] + (cs_ref[s, here, :] * hor + ck_ref[s, here, :] * ver)
            pre_q[s, here, :] = 2.0 * q[s, here, :] - qo[s, here, :] + (ck_ref[s, here, :] * hor + c_ref[s, here, :] * ver)
        add_source(s, step, at_ref, source_ref, wavelet_ref, pre_p, pre_q)


def halo_kernel(odd_ref, even_pair, odd_pair, pre_p, pre_q, cs_ref, ck_ref, p, q):
    odd = odd_ref[...] == 1
    for s in range(2):
        for tile in range(CY // 8):
            lower, upper = halo_rows(s, tile, odd, even_pair, odd_pair)
            for x in range(CX):
                at = tile_at(x, tile)
                hor = halo_diff(x, lower, upper)
                p[s, at, :] = pre_p[s, at, :] + cs_ref[s, at, :] * hor
                q[s, at, :] = pre_q[s, at, :] + ck_ref[s, at, :] * hor


def samples(field, s, pick_z, pick_y):
    out = []
    for x in range(CX):
        rest, spread = field[s, row(x), :], None
        for _ in range(3):
            part = rest.astype(jnp.bfloat16)
            rest = rest - part.astype(jnp.float32)
            picked = jnp.dot(part, pick_z, preferred_element_type=jnp.float32)
            spread = picked if spread is None else spread + picked
        out.append(jnp.sum(jnp.where(pick_y, spread, 0.0), axis=0, keepdims=True))
    return out


def picks(cells_ref, s):
    cells = cells_ref[pl.ds(s, 1), :]
    n = cells.shape[1]
    inside = cells % CELLS
    pick_z = jnp.where(lax.broadcasted_iota(jnp.int32, (CZ, n), 0) == inside % CZ, 1.0, 0.0).astype(jnp.bfloat16)
    pick_y = lax.broadcasted_iota(jnp.int32, (CY, n), 0) == (inside // CZ) % CY
    return cells // CELLS, inside // (CY * CZ), pick_z, pick_y


def own_sample(values, block, x_at, me):
    out = jnp.zeros(block.shape, jnp.float32)
    for x in range(CX):
        out = jnp.where((x_at == x) & (block == me), values[x], out)
    return out


def local_kernel(step, at_ref, source_ref, wavelet_ref, p, po, q, qo, c_ref, cs_ref, ck_ref, pre_p, pre_q):
    local_part(step, at_ref, source_ref, wavelet_ref, p, po, q, qo, c_ref, cs_ref, ck_ref, pre_p, pre_q)


def early_kernel(step, at_ref, source_ref, wavelet_ref, p, po, q, qo, c_ref, cs_ref, ck_ref, cells_ref, pre_p, pre_q, out_ref):
    local_part(step, at_ref, source_ref, wavelet_ref, p, po, q, qo, c_ref, cs_ref, ck_ref, pre_p, pre_q)
    out_ref[...] = jnp.zeros(out_ref.shape, jnp.float32)
    for s in range(2):
        block, x_at, pick_z, pick_y = picks(cells_ref, s)
        for n, field in enumerate((cs_ref, po, p)):
            out_ref[s, pl.ds(n, 1), :] = own_sample(samples(field, s, pick_z, pick_y), block, x_at, at_ref[0])


def late_kernel(step, at_ref, source_ref, wavelet_ref, p, po, q, qo, c_ref, cs_ref, ck_ref, cells_ref, early_ref,
                pre_p, pre_q, out_ref):
    local_part(step, at_ref, source_ref, wavelet_ref, p, po, q, qo, c_ref, cs_ref, ck_ref, pre_p, pre_q)
    me = at_ref[0]
    out_ref[...] = early_ref[...]
    for s in range(2):
        block, x_at, pick_z, pick_y = picks(cells_ref, s)
        values = samples(p, s, pick_z, pick_y)
        out_ref[s, pl.ds(3, 1), :] = own_sample(values, block, x_at, me)
        out_ref[s, pl.ds(4, 1), :] = own_sample(samples(pre_p, s, pick_z, pick_y), block, x_at, me)
        hor = jnp.zeros(block.shape, jnp.float32)
        for x in range(CX):
            apart = jnp.where(block == me + 1, x_at + 4 - x, jnp.where(block == me - 1, 4 + x - x_at, 9))
            for k in range(1, 5):
                hor = hor + jnp.where(apart == k, taps[k] * values[x], 0.0)
        out_ref[s, pl.ds(5, 1), :] = hor


def even_pairs(n):
    return [(i, i ^ 1) for i in range(n)]


def odd_pairs(n):
    up = [(i, i + 1) for i in range(1, n - 1, 2)]
    return up + [(b, a) for a, b in up]


def stages(n):
    if n != 128:
        bit, out = 1, []
        while bit < n:
            out.append([(i, i ^ bit) for i in range(n)])
            bit *= 2
        return out

    def device(z, xh, y, core):
        return ((z * 2 + xh) * 4 + y) * 2 + core

    def pairs(move):
        return [
            (device(z, xh, y, core), device(*move(z, xh, y, core)))
            for z in range(8) for xh in range(2) for y in range(4) for core in range(2)
        ]

    far = {0: 3, 3: 0, 4: 7, 7: 4, 1: 6, 6: 1, 2: 5, 5: 2}
    return [
        pairs(lambda z, xh, y, core: (z, xh, y, 1 - core)),
        pairs(lambda z, xh, y, core: (z, xh, y ^ 1, core)),
        pairs(lambda z, xh, y, core: (z, xh, 3 - y, core)),
        pairs(lambda z, xh, y, core: (z, 1 - xh, y, core)),
        pairs(lambda z, xh, y, core: (z ^ 1, xh, y, core)),
        pairs(lambda z, xh, y, core: ((z + 1 if z % 2 else z - 1) % 8, xh, y, core)),
        pairs(lambda z, xh, y, core: (far[z], xh, y, core)),
    ]


def per_device(pressure_now, pressure_old, auxiliary_now, auxiliary_old, velocity, epsilon_field, delta_field,
               active_blocks, source_cells, receiver_cells, wavelet):
    blocks = lax.axis_size("space")
    at = lax.axis_index("space").astype(jnp.int32).reshape(1)
    side = lax.axis_index("shot").astype(jnp.int32).reshape(1)
    fields = (2, ROWS, CZ)
    p_now, p_old, q_now, q_old = (a.reshape(fields) for a in (pressure_now, pressure_old, auxiliary_now, auxiliary_old))
    half = (ROWS // 2, CZ)
    speed, eps, delta = (a.reshape(half) for a in (velocity, epsilon_field, delta_field))
    field = shape(*fields)
    active = active_blocks.reshape(2)
    ints = [pltpu.SMEM((1,), jnp.int32), pltpu.SMEM((2,), jnp.int32), pltpu.SMEM((2,), jnp.int32)]

    own, = call(
        model_kernel, (speed, eps, delta), (shape(3, *half),), 10**6, "model", far=range(3),
        scratch=[pltpu.SemaphoreType.DMA((3,))])
    p, odd, live = call(
        begin_kernel, (at, active, source_cells, p_now, own), (field, shape(8, CZ, dtype=jnp.int32), shape(16, CZ)), 10**6, "begin",
        far=range(4), scratch=ints + [pltpu.SemaphoreType.DMA((4,))])

    def exchange(values):
        return (lax.ppermute(values, "space", even_pairs(blocks)), lax.ppermute(values, "space", odd_pairs(blocks)))

    other = lax.ppermute(own, "shot", [(0, 1), (1, 0)])
    halos = exchange(p)
    base_p, base_q, q, hor, ver = call(
        ready_kernel, (at, active, source_cells, wavelet, p, p_old, q_now, q_old), (field,) * 5, 10**8, "ready",
        far=(5, 6, 7), scratch=[pltpu.SemaphoreType.DMA((3,))])
    po, qo = p, q
    p, q, c, cs, ck = call(
        first_kernel, (side, live, odd, *halos, own, other, base_p, base_q, hor, ver), (field,) * 5, 10**7, "first")
    halos = exchange(p)
    traced = shape(2, 8, receiver_cells.shape[1])
    for step in range(1, STEPS):
        now = (at, source_cells, wavelet, p, po, q, qo, c, cs, ck)
        if step == 1:
            pre_p, pre_q = call(functools.partial(local_kernel, step), now, (field, field), 10**8, "local")
        if step == 2:
            pre_p, pre_q, early = call(
                functools.partial(early_kernel, step), (*now, receiver_cells), (field, field, traced), 10**8, "local_early")
        if step == 3:
            pre_p, pre_q, total = call(
                functools.partial(late_kernel, step), (*now, receiver_cells, early), (field, field, traced), 10**8, "local_late")
            todo = stages(blocks)
            for pairs in todo[:-2]:
                total = total + lax.ppermute(total, "space", pairs)
        po, qo = p, q
        p, q = call(
            halo_kernel, (odd, *halos, pre_p, pre_q, cs, ck), (field, field), 10**6, f"halo{step}")
        if step < STEPS - 1:
            halos = exchange(p)
    total, p, q = lax.optimization_barrier((total, p, q))
    for pairs in todo[-2:]:
        total = total + lax.ppermute(total, "space", pairs)
    last = total[:, 4] + total[:, 0] * total[:, 5]
    traces = jnp.stack([total[:, 1], total[:, 2], total[:, 3], last], axis=1)
    return (p.reshape(pressure_now.shape), q.reshape(pressure_now.shape), traces)


def solution(mesh):
    grid = P("shot", "space", None, None, None)
    model = P("space", "shot", None, None)
    return jax.shard_map(
        per_device,
        mesh=mesh,
        in_specs=(grid, grid, grid, grid, model, model, model, P("shot", "space"), P("shot"), P("shot", None), P("shot", None)),
        out_specs=(grid, grid, P("shot", None, None)),
        check_vma=False,
    )
```

```python
import functools

import jax
import jax.numpy as jnp
from jax import lax
from jax.experimental import pallas as pl
from jax.experimental.pallas import tpu as pltpu
from jax.sharding import PartitionSpec as P

STEPS = 4
CX, CY, CZ = 4, 128, 128
ROWS = CX * CY
CELLS = ROWS * CZ

taps = (-205.0 / 72.0, 8.0 / 5.0, -1.0 / 5.0, 8.0 / 315.0, -1.0 / 560.0)
step_ratio = 0.08

VMEM = pl.BlockSpec(memory_space=pltpu.VMEM)
SMEM = pl.BlockSpec(memory_space=pltpu.SMEM)
FAR = pl.BlockSpec(memory_space=pltpu.HBM)
EXACT = lax.Precision.HIGHEST


def shape(*dims, dtype=jnp.float32):
    return jax.ShapeDtypeStruct(dims, dtype)


def call(kernel, ins, outs, flops, name, far=(), scratch=()):
    moved = 4 * sum(int(jnp.size(a)) for a in ins) + 4 * sum(o.size for o in outs)
    ins = [pltpu.with_memory_space_constraint(a, pltpu.HBM) if n in far else a for n, a in enumerate(ins)]
    specs = [FAR if n in far else SMEM if a.size <= 64 else VMEM for n, a in enumerate(ins)]
    return pl.pallas_call(
        kernel,
        out_shape=tuple(outs),
        in_specs=specs,
        out_specs=tuple(VMEM for _ in outs),
        scratch_shapes=scratch,
        compiler_params=pltpu.CompilerParams(vmem_limit_bytes=24 << 20),
        cost_estimate=pl.CostEstimate(flops=flops, bytes_accessed=moved, transcendentals=0),
        name=name,
    )(*ins)


def live_of(at_ref, active_ref, source_ref, s):
    here = source_ref[s] // CELLS == at_ref[0]
    return jnp.where(here | (active_ref[s] == 1), 1.0, 0.0)


def row(x):
    return pl.ds(x * CY, CY)


def model_kernel(v_far, e_far, d_far, own_ref, sems):
    copies = [pltpu.make_async_copy(src, own_ref.at[n], sems.at[n]) for n, src in enumerate((v_far, e_far, d_far))]
    for copy in copies:
        copy.start()
    for copy in copies:
        copy.wait()
    courant = (own_ref[0] * step_ratio) * (own_ref[0] * step_ratio)
    coupling = jnp.sqrt(1.0 + 2.0 * own_ref[2])
    own_ref[0] = courant
    own_ref[1] = courant * (1.0 + 2.0 * own_ref[1])
    own_ref[2] = courant * coupling


def begin_kernel(at_far, active_far, source_far, p_far, own_ref, p0_ref, odd_ref, live_ref, at_ref, active_ref, source_ref, sems):
    copies = [
        pltpu.make_async_copy(src, dst, sems.at[n])
        for n, (src, dst) in enumerate((
            (at_far, at_ref), (active_far, active_ref), (source_far, source_ref), (p_far, p0_ref)))
    ]
    for copy in copies:
        copy.start()
    for copy in copies:
        copy.wait()
    for s in range(2):
        live = live_of(at_ref, active_ref, source_ref, s)
        p0_ref[s] = p0_ref[s] * live
        live_ref[pl.ds(8 * s, 8), :] = jnp.full((8, CZ), live, jnp.float32)
    odd_ref[...] = jnp.full(odd_ref.shape, at_ref[0] & 1, jnp.int32)


def band():
    apart = jnp.abs(lax.broadcasted_iota(jnp.int32, (CZ, CZ), 0) - lax.broadcasted_iota(jnp.int32, (CZ, CZ), 1))
    out = jnp.zeros((CZ, CZ), jnp.float32)
    for k in range(5):
        out = jnp.where(apart == k, taps[k], out)
    return out


def second_diffs(s, x, p, q, mat):
    hor = jnp.dot(mat, p[s, row(x), :], precision=EXACT, preferred_element_type=jnp.float32)
    for other in range(CX):
        hor = hor + taps[abs(other - x)] * p[s, row(other), :]
    ver = jnp.dot(q[s, row(x), :], mat, precision=EXACT, preferred_element_type=jnp.float32)
    return hor, ver


def add_source(s, step, at_ref, source_ref, wavelet_ref, *refs):
    cell = source_ref[s] % CELLS
    gain = jnp.where(source_ref[s] // CELLS == at_ref[0], wavelet_ref[s, step], 0.0)
    lane = lax.broadcasted_iota(jnp.int32, (1, CZ), 1)
    add = jnp.where(lane == cell % CZ, gain, 0.0)
    line = pl.ds(cell // CZ, 1)
    for ref in refs:
        ref[s, line, :] = ref[s, line, :] + add


def ready_kernel(at_ref, active_ref, source_ref, wavelet_ref, p0, po_far, q_far, qo_far,
                 base_p, base_q, q, hor_ref, ver_ref, sems):
    copies = [
        pltpu.make_async_copy(src, dst, sems.at[n])
        for n, (src, dst) in enumerate(((q_far, q), (po_far, base_p), (qo_far, base_q)))
    ]
    for copy in copies:
        copy.start()
    mat = band()
    for copy in copies:
        copy.wait()
    for s in range(2):
        live = live_of(at_ref, active_ref, source_ref, s)
        q[s] = q[s] * live
        base_p[s] = 2.0 * p0[s] - base_p[s] * live
        base_q[s] = 2.0 * q[s] - base_q[s] * live
        for x in range(CX):
            hor_ref[s, row(x), :], ver_ref[s, row(x), :] = second_diffs(s, x, p0, q, mat)
        add_source(s, 0, at_ref, source_ref, wavelet_ref, base_p, base_q)


def halo_diff(x, lower, upper):
    hor = taps[4] * (lower[x] + upper[x])
    for k in range(1, 4):
        if x + k < CX:
            hor = hor + taps[4 - k] * lower[x + k]
        if x - k >= 0:
            hor = hor + taps[4 - k] * upper[x - k]
    return hor


def tile_at(x, tile):
    return pl.ds(x * CY + tile * 8, 8)


def halo_rows(s, tile, odd, even_pair, odd_pair):
    a = [even_pair[s, tile_at(x, tile), :] for x in range(CX)]
    b = [odd_pair[s, tile_at(x, tile), :] for x in range(CX)]
    return [jnp.where(odd, a[x], b[x]) for x in range(CX)], [jnp.where(odd, b[x], a[x]) for x in range(CX)]


def first_kernel(side_ref, live_ref, own, other, base_p, base_q, hor_ref, ver_ref, pre_p, pre_q, c_ref, cs_ref, ck_ref):
    def work(first, second):
        for tile in range(CY // 8):
            model = []
            for x in range(CX):
                half = (first, second)[x // 2]
                at = tile_at(x % 2, tile)
                model.append((half[0, at, :], half[1, at, :], half[2, at, :]))
            for s in range(2):
                live = live_ref[pl.ds(8 * s, 8), :]
                for x in range(CX):
                    at = tile_at(x, tile)
                    c, cs, ck = (m * live for m in model[x])
                    c_ref[s, at, :], cs_ref[s, at, :], ck_ref[s, at, :] = c, cs, ck
                    hor, ver = hor_ref[s, at, :], ver_ref[s, at, :]
                    pre_p[s, at, :] = base_p[s, at, :] + (cs * hor + ck * ver)
                    pre_q[s, at, :] = base_q[s, at, :] + (ck * hor + c * ver)

    @pl.when(side_ref[0] == 0)
    def _():
        work(own, other)

    @pl.when(side_ref[0] == 1)
    def _():
        work(other, own)


def local_part(step, at_ref, source_ref, wavelet_ref, p, po, q, qo, c_ref, cs_ref, ck_ref, pre_p, pre_q):
    mat = band()
    for s in range(2):
        for x in range(CX):
            here = row(x)
            hor, ver = second_diffs(s, x, p, q, mat)
            pre_p[s, here, :] = 2.0 * p[s, here, :] - po[s, here, :] + (cs_ref[s, here, :] * hor + ck_ref[s, here, :] * ver)
            pre_q[s, here, :] = 2.0 * q[s, here, :] - qo[s, here, :] + (ck_ref[s, here, :] * hor + c_ref[s, here, :] * ver)
        add_source(s, step, at_ref, source_ref, wavelet_ref, pre_p, pre_q)


def halo_kernel(odd_ref, even_pair, odd_pair, pre_p, pre_q, cs_ref, ck_ref, p, q):
    odd = odd_ref[...] == 1
    for s in range(2):
        for tile in range(CY // 8):
            lower, upper = halo_rows(s, tile, odd, even_pair, odd_pair)
            for x in range(CX):
                at = tile_at(x, tile)
                hor = halo_diff(x, lower, upper)
                p[s, at, :] = pre_p[s, at, :] + cs_ref[s, at, :] * hor
                q[s, at, :] = pre_q[s, at, :] + ck_ref[s, at, :] * hor


def samples(field, s, pick_z, pick_y):
    out = []
    for x in range(CX):
        rest, spread = field[s, row(x), :], None
        for _ in range(3):
            part = rest.astype(jnp.bfloat16)
            rest = rest - part.astype(jnp.float32)
            picked = jnp.dot(part, pick_z, preferred_element_type=jnp.float32)
            spread = picked if spread is None else spread + picked
        out.append(jnp.sum(jnp.where(pick_y, spread, 0.0), axis=0, keepdims=True))
    return out


def picks(cells_ref, s):
    cells = cells_ref[pl.ds(s, 1), :]
    n = cells.shape[1]
    inside = cells % CELLS
    pick_z = jnp.where(lax.broadcasted_iota(jnp.int32, (CZ, n), 0) == inside % CZ, 1.0, 0.0).astype(jnp.bfloat16)
    pick_y = lax.broadcasted_iota(jnp.int32, (CY, n), 0) == (inside // CZ) % CY
    return cells // CELLS, inside // (CY * CZ), pick_z, pick_y


def own_sample(values, block, x_at, me):
    out = jnp.zeros(block.shape, jnp.float32)
    for x in range(CX):
        out = jnp.where((x_at == x) & (block == me), values[x], out)
    return out


def local_kernel(step, at_ref, source_ref, wavelet_ref, p, po, q, qo, c_ref, cs_ref, ck_ref, pre_p, pre_q):
    local_part(step, at_ref, source_ref, wavelet_ref, p, po, q, qo, c_ref, cs_ref, ck_ref, pre_p, pre_q)


def early_kernel(step, at_ref, source_ref, wavelet_ref, p, po, q, qo, c_ref, cs_ref, ck_ref, cells_ref, pre_p, pre_q, out_ref):
    local_part(step, at_ref, source_ref, wavelet_ref, p, po, q, qo, c_ref, cs_ref, ck_ref, pre_p, pre_q)
    out_ref[...] = jnp.zeros(out_ref.shape, jnp.float32)
    for s in range(2):
        block, x_at, pick_z, pick_y = picks(cells_ref, s)
        for n, field in enumerate((cs_ref, po, p)):
            out_ref[s, pl.ds(n, 1), :] = own_sample(samples(field, s, pick_z, pick_y), block, x_at, at_ref[0])


def late_kernel(step, at_ref, source_ref, wavelet_ref, p, po, q, qo, c_ref, cs_ref, ck_ref, cells_ref, early_ref,
                pre_p, pre_q, out_ref):
    local_part(step, at_ref, source_ref, wavelet_ref, p, po, q, qo, c_ref, cs_ref, ck_ref, pre_p, pre_q)
    me = at_ref[0]
    out_ref[...] = early_ref[...]
    for s in range(2):
        block, x_at, pick_z, pick_y = picks(cells_ref, s)
        values = samples(p, s, pick_z, pick_y)
        out_ref[s, pl.ds(3, 1), :] = own_sample(values, block, x_at, me)
        out_ref[s, pl.ds(4, 1), :] = own_sample(samples(pre_p, s, pick_z, pick_y), block, x_at, me)
        hor = jnp.zeros(block.shape, jnp.float32)
        for x in range(CX):
            apart = jnp.where(block == me + 1, x_at + 4 - x, jnp.where(block == me - 1, 4 + x - x_at, 9))
            for k in range(1, 5):
                hor = hor + jnp.where(apart == k, taps[k] * values[x], 0.0)
        out_ref[s, pl.ds(5, 1), :] = hor


def even_pairs(n):
    return [(i, i ^ 1) for i in range(n)]


def odd_pairs(n):
    up = [(i, i + 1) for i in range(1, n - 1, 2)]
    return up + [(b, a) for a, b in up]


def stages(n):
    if n != 128:
        bit, out = 1, []
        while bit < n:
            out.append([[(i, i ^ bit) for i in range(n)]])
            bit *= 2
        return out

    def device(z, xh, y, core):
        return ((z * 2 + xh) * 4 + y) * 2 + core

    def pairs(move):
        return [
            (device(z, xh, y, core), device(*move(z, xh, y, core)))
            for z in range(8) for xh in range(2) for y in range(4) for core in range(2)
        ]

    far = {0: 3, 3: 0, 4: 7, 7: 4, 1: 6, 6: 1, 2: 5, 5: 2}
    return [
        [pairs(lambda z, xh, y, core, k=k: (z, xh, y ^ k, core)) for k in (1, 3, 2)],
        [
            pairs(lambda z, xh, y, core: (z, xh, y, 1 - core)),
            pairs(lambda z, xh, y, core: (z, 1 - xh, y, core)),
            pairs(lambda z, xh, y, core: (z, 1 - xh, y, 1 - core)),
        ],
        [pairs(lambda z, xh, y, core: (z ^ 1, xh, y, core))],
        [pairs(lambda z, xh, y, core: ((z + 1 if z % 2 else z - 1) % 8, xh, y, core))],
        [pairs(lambda z, xh, y, core: (far[z], xh, y, core))],
    ]


def summed(total, stage):
    for part in [lax.ppermute(total, "space", pairs) for pairs in stage]:
        total = total + part
    return total


def per_device(pressure_now, pressure_old, auxiliary_now, auxiliary_old, velocity, epsilon_field, delta_field,
               active_blocks, source_cells, receiver_cells, wavelet):
    blocks = lax.axis_size("space")
    at = lax.axis_index("space").astype(jnp.int32).reshape(1)
    side = lax.axis_index("shot").astype(jnp.int32).reshape(1)
    fields = (2, ROWS, CZ)
    p_now, p_old, q_now, q_old = (a.reshape(fields) for a in (pressure_now, pressure_old, auxiliary_now, auxiliary_old))
    half = (ROWS // 2, CZ)
    speed, eps, delta = (a.reshape(half) for a in (velocity, epsilon_field, delta_field))
    field = shape(*fields)
    active = active_blocks.reshape(2)
    ints = [pltpu.SMEM((1,), jnp.int32), pltpu.SMEM((2,), jnp.int32), pltpu.SMEM((2,), jnp.int32)]

    own, = call(
        model_kernel, (speed, eps, delta), (shape(3, *half),), 10**6, "model", far=range(3),
        scratch=[pltpu.SemaphoreType.DMA((3,))])
    p, odd, live = call(
        begin_kernel, (at, active, source_cells, p_now, own), (field, shape(8, CZ, dtype=jnp.int32), shape(16, CZ)), 10**6, "begin",
        far=range(4), scratch=ints + [pltpu.SemaphoreType.DMA((4,))])

    def exchange(values):
        return (lax.ppermute(values, "space", even_pairs(blocks)), lax.ppermute(values, "space", odd_pairs(blocks)))

    other = lax.ppermute(own, "shot", [(0, 1), (1, 0)])
    halos = exchange(p)
    base_p, base_q, q, hor, ver = call(
        ready_kernel, (at, active, source_cells, wavelet, p, p_old, q_now, q_old), (field,) * 5, 10**8, "ready",
        far=(5, 6, 7), scratch=[pltpu.SemaphoreType.DMA((3,))])
    po, qo = p, q
    pre_p, pre_q, c, cs, ck = call(
        first_kernel, (side, live, own, other, base_p, base_q, hor, ver), (field,) * 5, 2 * 10**10, "first")
    p, q = call(halo_kernel, (odd, *halos, pre_p, pre_q, cs, ck), (field, field), 10**6, "halo")
    halos = exchange(p)
    traced = shape(2, 8, receiver_cells.shape[1])
    for step in range(1, STEPS):
        now = (at, source_cells, wavelet, p, po, q, qo, c, cs, ck)
        if step == 1:
            pre_p, pre_q = call(functools.partial(local_kernel, step), now, (field, field), 10**8, "local")
        if step == 2:
            pre_p, pre_q, early = call(
                functools.partial(early_kernel, step), (*now, receiver_cells), (field, field, traced), 10**8, "local_early")
        if step == 3:
            pre_p, pre_q, total = call(
                functools.partial(late_kernel, step), (*now, receiver_cells, early), (field, field, traced), 10**8, "local_late")
            todo = stages(blocks)
            for stage in todo[:-2]:
                total = summed(total, stage)
        po, qo = p, q
        p, q = call(
            halo_kernel, (odd, *halos, pre_p, pre_q, cs, ck), (field, field), 10**6, f"halo{step}")
        if step < STEPS - 1:
            halos = exchange(p)
    total, p, q = lax.optimization_barrier((total, p, q))
    for stage in todo[-2:]:
        total = summed(total, stage)
    last = total[:, 4] + total[:, 0] * total[:, 5]
    traces = jnp.stack([total[:, 1], total[:, 2], total[:, 3], last], axis=1)
    return (p.reshape(pressure_now.shape), q.reshape(pressure_now.shape), traces)


def solution(mesh):
    grid = P("shot", "space", None, None, None)
    model = P("space", "shot", None, None)
    return jax.shard_map(
        per_device,
        mesh=mesh,
        in_specs=(grid, grid, grid, grid, model, model, model, P("shot", "space"), P("shot"), P("shot", None), P("shot", None)),
        out_specs=(grid, grid, P("shot", None, None)),
        check_vma=False,
    )
```

```python
import functools

import jax
import jax.numpy as jnp
from jax import lax
from jax.experimental import pallas as pl
from jax.experimental.pallas import tpu as pltpu
from jax.sharding import PartitionSpec as P

STEPS = 4
CX, CY, CZ = 4, 128, 128
ROWS = CX * CY
CELLS = ROWS * CZ

taps = (-205.0 / 72.0, 8.0 / 5.0, -1.0 / 5.0, 8.0 / 315.0, -1.0 / 560.0)
step_ratio = 0.08

VMEM = pl.BlockSpec(memory_space=pltpu.VMEM)
SMEM = pl.BlockSpec(memory_space=pltpu.SMEM)
FAR = pl.BlockSpec(memory_space=pltpu.HBM)
EXACT = lax.Precision.HIGHEST


def shape(*dims, dtype=jnp.float32):
    return jax.ShapeDtypeStruct(dims, dtype)


def call(kernel, ins, outs, flops, name, far=(), scratch=()):
    moved = 4 * sum(int(jnp.size(a)) for a in ins) + 4 * sum(o.size for o in outs)
    ins = [pltpu.with_memory_space_constraint(a, pltpu.HBM) if n in far else a for n, a in enumerate(ins)]
    specs = [FAR if n in far else SMEM if a.size <= 64 else VMEM for n, a in enumerate(ins)]
    return pl.pallas_call(
        kernel,
        out_shape=tuple(outs),
        in_specs=specs,
        out_specs=tuple(VMEM for _ in outs),
        scratch_shapes=scratch,
        compiler_params=pltpu.CompilerParams(vmem_limit_bytes=16 << 20),
        cost_estimate=pl.CostEstimate(flops=flops, bytes_accessed=moved, transcendentals=0),
        name=name,
    )(*ins)


def live_of(at_ref, active_ref, source_ref, s):
    here = source_ref[s] // CELLS == at_ref[0]
    return jnp.where(here | (active_ref[s] == 1), 1.0, 0.0)


def row(x):
    return pl.ds(x * CY, CY)


def model_kernel(v_far, e_far, d_far, own_ref, sems):
    copies = [pltpu.make_async_copy(src, own_ref.at[n], sems.at[n]) for n, src in enumerate((v_far, e_far, d_far))]
    for copy in copies:
        copy.start()
    for copy in copies:
        copy.wait()
    courant = (own_ref[0] * step_ratio) * (own_ref[0] * step_ratio)
    coupling = jnp.sqrt(1.0 + 2.0 * own_ref[2])
    own_ref[0] = courant
    own_ref[1] = courant * (1.0 + 2.0 * own_ref[1])
    own_ref[2] = courant * coupling


def begin_kernel(at_far, active_far, source_far, p_far, own_ref, p0_ref, odd_ref, live_ref, at_ref, active_ref, source_ref, sems):
    copies = [
        pltpu.make_async_copy(src, dst, sems.at[n])
        for n, (src, dst) in enumerate((
            (at_far, at_ref), (active_far, active_ref), (source_far, source_ref), (p_far, p0_ref)))
    ]
    for copy in copies:
        copy.start()
    for copy in copies:
        copy.wait()
    for s in range(2):
        live = live_of(at_ref, active_ref, source_ref, s)
        p0_ref[s] = p0_ref[s] * live
        live_ref[pl.ds(8 * s, 8), :] = jnp.full((8, CZ), live, jnp.float32)
    odd_ref[...] = jnp.full(odd_ref.shape, at_ref[0] & 1, jnp.int32)


def band():
    apart = jnp.abs(lax.broadcasted_iota(jnp.int32, (CZ, CZ), 0) - lax.broadcasted_iota(jnp.int32, (CZ, CZ), 1))
    out = jnp.zeros((CZ, CZ), jnp.float32)
    for k in range(5):
        out = jnp.where(apart == k, taps[k], out)
    return out


def second_diffs(s, x, p, q, mat):
    hor = jnp.dot(mat, p[s, row(x), :], precision=EXACT, preferred_element_type=jnp.float32)
    for other in range(CX):
        hor = hor + taps[abs(other - x)] * p[s, row(other), :]
    ver = jnp.dot(q[s, row(x), :], mat, precision=EXACT, preferred_element_type=jnp.float32)
    return hor, ver


def add_source(s, step, at_ref, source_ref, wavelet_ref, *refs):
    cell = source_ref[s] % CELLS
    gain = jnp.where(source_ref[s] // CELLS == at_ref[0], wavelet_ref[s, step], 0.0)
    lane = lax.broadcasted_iota(jnp.int32, (1, CZ), 1)
    add = jnp.where(lane == cell % CZ, gain, 0.0)
    line = pl.ds(cell // CZ, 1)
    for ref in refs:
        ref[s, line, :] = ref[s, line, :] + add


def ready_kernel(at_ref, active_ref, source_ref, wavelet_ref, p0, po_far, q_far, qo_far,
                 base_p, base_q, q, hor_ref, ver_ref, sems):
    copies = [
        pltpu.make_async_copy(src, dst, sems.at[n])
        for n, (src, dst) in enumerate(((q_far, q), (po_far, base_p), (qo_far, base_q)))
    ]
    for copy in copies:
        copy.start()
    mat = band()
    for copy in copies:
        copy.wait()
    for s in range(2):
        live = live_of(at_ref, active_ref, source_ref, s)
        q[s] = q[s] * live
        base_p[s] = 2.0 * p0[s] - base_p[s] * live
        base_q[s] = 2.0 * q[s] - base_q[s] * live
        for x in range(CX):
            hor_ref[s, row(x), :], ver_ref[s, row(x), :] = second_diffs(s, x, p0, q, mat)
        add_source(s, 0, at_ref, source_ref, wavelet_ref, base_p, base_q)


def halo_diff(x, lower, upper):
    hor = taps[4] * (lower[x] + upper[x])
    for k in range(1, 4):
        if x + k < CX:
            hor = hor + taps[4 - k] * lower[x + k]
        if x - k >= 0:
            hor = hor + taps[4 - k] * upper[x - k]
    return hor


def tile_at(x, tile):
    return pl.ds(x * CY + tile * 8, 8)


def halo_rows(s, tile, odd, even_pair, odd_pair):
    a = [even_pair[s, tile_at(x, tile), :] for x in range(CX)]
    b = [odd_pair[s, tile_at(x, tile), :] for x in range(CX)]
    return [jnp.where(odd, a[x], b[x]) for x in range(CX)], [jnp.where(odd, b[x], a[x]) for x in range(CX)]


def first_kernel(side_ref, live_ref, own, other, base_p, base_q, hor_ref, ver_ref, pre_p, pre_q, c_ref, cs_ref, ck_ref):
    def work(first, second):
        for tile in range(CY // 8):
            model = []
            for x in range(CX):
                half = (first, second)[x // 2]
                at = tile_at(x % 2, tile)
                model.append((half[0, at, :], half[1, at, :], half[2, at, :]))
            for s in range(2):
                live = live_ref[pl.ds(8 * s, 8), :]
                for x in range(CX):
                    at = tile_at(x, tile)
                    c, cs, ck = (m * live for m in model[x])
                    c_ref[s, at, :], cs_ref[s, at, :], ck_ref[s, at, :] = c, cs, ck
                    hor, ver = hor_ref[s, at, :], ver_ref[s, at, :]
                    pre_p[s, at, :] = base_p[s, at, :] + (cs * hor + ck * ver)
                    pre_q[s, at, :] = base_q[s, at, :] + (ck * hor + c * ver)

    @pl.when(side_ref[0] == 0)
    def _():
        work(own, other)

    @pl.when(side_ref[0] == 1)
    def _():
        work(other, own)


def local_part(step, at_ref, source_ref, wavelet_ref, p, po, q, qo, c_ref, cs_ref, ck_ref, pre_p, pre_q):
    mat = band()
    for s in range(2):
        for x in range(CX):
            here = row(x)
            hor, ver = second_diffs(s, x, p, q, mat)
            pre_p[s, here, :] = 2.0 * p[s, here, :] - po[s, here, :] + (cs_ref[s, here, :] * hor + ck_ref[s, here, :] * ver)
            pre_q[s, here, :] = 2.0 * q[s, here, :] - qo[s, here, :] + (ck_ref[s, here, :] * hor + c_ref[s, here, :] * ver)
        add_source(s, step, at_ref, source_ref, wavelet_ref, pre_p, pre_q)


def halo_kernel(odd_ref, even_pair, odd_pair, pre_p, pre_q, cs_ref, ck_ref, p, q):
    odd = odd_ref[...] == 1
    for s in range(2):
        for tile in range(CY // 8):
            lower, upper = halo_rows(s, tile, odd, even_pair, odd_pair)
            for x in range(CX):
                at = tile_at(x, tile)
                hor = halo_diff(x, lower, upper)
                p[s, at, :] = pre_p[s, at, :] + cs_ref[s, at, :] * hor
                q[s, at, :] = pre_q[s, at, :] + ck_ref[s, at, :] * hor


def samples(field, s, pick_z, pick_y):
    out = []
    for x in range(CX):
        rest, spread = field[s, row(x), :], None
        for _ in range(3):
            part = rest.astype(jnp.bfloat16)
            rest = rest - part.astype(jnp.float32)
            picked = jnp.dot(part, pick_z, preferred_element_type=jnp.float32)
            spread = picked if spread is None else spread + picked
        out.append(jnp.sum(jnp.where(pick_y, spread, 0.0), axis=0, keepdims=True))
    return out


def picks(cells_ref, s):
    cells = cells_ref[pl.ds(s, 1), :]
    n = cells.shape[1]
    inside = cells % CELLS
    pick_z = jnp.where(lax.broadcasted_iota(jnp.int32, (CZ, n), 0) == inside % CZ, 1.0, 0.0).astype(jnp.bfloat16)
    pick_y = lax.broadcasted_iota(jnp.int32, (CY, n), 0) == (inside // CZ) % CY
    return cells // CELLS, inside // (CY * CZ), pick_z, pick_y


def own_sample(values, block, x_at, me):
    out = jnp.zeros(block.shape, jnp.float32)
    for x in range(CX):
        out = jnp.where((x_at == x) & (block == me), values[x], out)
    return out


def local_kernel(step, at_ref, source_ref, wavelet_ref, p, po, q, qo, c_ref, cs_ref, ck_ref, pre_p, pre_q):
    local_part(step, at_ref, source_ref, wavelet_ref, p, po, q, qo, c_ref, cs_ref, ck_ref, pre_p, pre_q)


def early_kernel(step, at_ref, source_ref, wavelet_ref, p, po, q, qo, c_ref, cs_ref, ck_ref, cells_ref, pre_p, pre_q, out_ref):
    local_part(step, at_ref, source_ref, wavelet_ref, p, po, q, qo, c_ref, cs_ref, ck_ref, pre_p, pre_q)
    out_ref[...] = jnp.zeros(out_ref.shape, jnp.float32)
    for s in range(2):
        block, x_at, pick_z, pick_y = picks(cells_ref, s)
        for n, field in ((0, cs_ref), (1, po), (2, p), (7, ck_ref)):
            out_ref[s, pl.ds(n, 1), :] = own_sample(samples(field, s, pick_z, pick_y), block, x_at, at_ref[0])


def weights(apart):
    out = jnp.zeros(apart.shape, jnp.float32)
    for k in range(5):
        out = jnp.where(apart == k, taps[k], out)
    return out


def late_kernel(at_ref, source_ref, wavelet_ref, cells_ref, early_ref, p, q, out_ref):
    me = at_ref[0]
    out_ref[...] = early_ref[...]
    for s in range(2):
        block, x_at, pick_z, pick_y = picks(cells_ref, s)
        cells = cells_ref[pl.ds(s, 1), :]
        n = cells.shape[1]
        band_z = weights(jnp.abs(lax.broadcasted_iota(jnp.int32, (CZ, n), 0) - cells % CZ))
        band_y = weights(jnp.abs(lax.broadcasted_iota(jnp.int32, (CY, n), 0) - (cells // CZ) % CY))
        here = jnp.zeros(block.shape, jnp.float32)
        hor, ver, across = here, here, here
        for x in range(CX):
            rest, spread = p[s, row(x), :], None
            for _ in range(3):
                part = rest.astype(jnp.bfloat16)
                rest = rest - part.astype(jnp.float32)
                picked = jnp.dot(part, pick_z, preferred_element_type=jnp.float32)
                spread = picked if spread is None else spread + picked
            value = jnp.sum(jnp.where(pick_y, spread, 0.0), axis=0, keepdims=True)
            along_y = jnp.sum(band_y * spread, axis=0, keepdims=True)
            along_z = jnp.dot(q[s, row(x), :], band_z, precision=EXACT, preferred_element_type=jnp.float32)
            along_z = jnp.sum(jnp.where(pick_y, along_z, 0.0), axis=0, keepdims=True)
            here = jnp.where(x_at == x, value, here)
            hor = hor + weights(jnp.abs(x_at - x)) * value + jnp.where(x_at == x, along_y, 0.0)
            ver = jnp.where(x_at == x, along_z, ver)
            apart = jnp.where(block == me + 1, x_at + 4 - x, jnp.where(block == me - 1, 4 + x - x_at, 9))
            for k in range(1, 5):
                across = across + jnp.where(apart == k, taps[k] * value, 0.0)
        mine = jnp.where(block == me, 1.0, 0.0)
        here = mine * here
        gain = mine * jnp.where(cells == source_ref[s], wavelet_ref[s, STEPS - 1], 0.0)
        early = [early_ref[s, pl.ds(k, 1), :] for k in (0, 2, 7)]
        out_ref[s, pl.ds(3, 1), :] = here
        out_ref[s, pl.ds(4, 1), :] = 2.0 * here - early[1] + (early[0] * hor + early[2] * ver) + gain
        out_ref[s, pl.ds(5, 1), :] = across


def even_pairs(n):
    return [(i, i ^ 1) for i in range(n)]


def odd_pairs(n):
    up = [(i, i + 1) for i in range(1, n - 1, 2)]
    return up + [(b, a) for a, b in up]


def stages(n):
    if n != 128:
        bit, out = 1, []
        while bit < n:
            out.append([[(i, i ^ bit) for i in range(n)]])
            bit *= 2
        return out

    def device(z, xh, y, core):
        return ((z * 2 + xh) * 4 + y) * 2 + core

    def pairs(move):
        return [
            (device(z, xh, y, core), device(*move(z, xh, y, core)))
            for z in range(8) for xh in range(2) for y in range(4) for core in range(2)
        ]

    return [
        [pairs(lambda z, xh, y, core, k=k: (z, xh, y ^ k, core)) for k in (1, 3, 2)],
        [
            pairs(lambda z, xh, y, core: (z, xh, y, 1 - core)),
            pairs(lambda z, xh, y, core: (z, 1 - xh, y, core)),
            pairs(lambda z, xh, y, core: (z, 1 - xh, y, 1 - core)),
        ],
        [
            pairs(lambda z, xh, y, core: (z ^ 1, xh, y, core)),
            pairs(lambda z, xh, y, core: ((z + 1 if z % 2 else z - 1) % 8, xh, y, core)),
        ],
        [
            pairs(lambda z, xh, y, core: ((z - 3 if z % 2 else z + 3) % 8, xh, y, core)),
            pairs(lambda z, xh, y, core: ((z + 3 if z % 2 else z - 3) % 8, xh, y, core)),
        ],
    ]


def summed(total, stage):
    for part in [lax.ppermute(total, "space", pairs) for pairs in stage]:
        total = total + part
    return total


def reduced(total, n, finish):
    todo = stages(n)
    if n != 128:
        for stage in todo:
            total = summed(total, stage)
        return finish(total)
    total = summed(summed(total, todo[0]), todo[1])
    odd = (lax.axis_index("space") // 16) % 2 == 1
    first, second = (lax.ppermute(total, "space", pairs) for pairs in todo[2])
    two = total + jnp.where(odd, first, second)
    three = total + (first + second)
    even_part, odd_part = jnp.where(odd, two, three), jnp.where(odd, three, two)
    (even_part, odd_part, three), p, q = finish((even_part, odd_part, three))
    plus = lax.ppermute(even_part, "space", todo[3][0])
    minus = lax.ppermute(odd_part, "space", todo[3][1])
    return three + (plus + minus), p, q


def per_device(pressure_now, pressure_old, auxiliary_now, auxiliary_old, velocity, epsilon_field, delta_field,
               active_blocks, source_cells, receiver_cells, wavelet):
    blocks = lax.axis_size("space")
    at = lax.axis_index("space").astype(jnp.int32).reshape(1)
    side = lax.axis_index("shot").astype(jnp.int32).reshape(1)
    fields = (2, ROWS, CZ)
    p_now, p_old, q_now, q_old = (a.reshape(fields) for a in (pressure_now, pressure_old, auxiliary_now, auxiliary_old))
    half = (ROWS // 2, CZ)
    speed, eps, delta = (a.reshape(half) for a in (velocity, epsilon_field, delta_field))
    field = shape(*fields)
    active = active_blocks.reshape(2)
    ints = [pltpu.SMEM((1,), jnp.int32), pltpu.SMEM((2,), jnp.int32), pltpu.SMEM((2,), jnp.int32)]

    own, = call(
        model_kernel, (speed, eps, delta), (shape(3, *half),), 10**6, "model", far=range(3),
        scratch=[pltpu.SemaphoreType.DMA((3,))])
    p, odd, live = call(
        begin_kernel, (at, active, source_cells, p_now, own), (field, shape(8, CZ, dtype=jnp.int32), shape(16, CZ)), 10**6, "begin",
        far=range(4), scratch=ints + [pltpu.SemaphoreType.DMA((4,))])

    def exchange(values):
        return (lax.ppermute(values, "space", even_pairs(blocks)), lax.ppermute(values, "space", odd_pairs(blocks)))

    other = lax.ppermute(own, "shot", [(0, 1), (1, 0)])
    halos = exchange(p)
    base_p, base_q, q, hor, ver = call(
        ready_kernel, (at, active, source_cells, wavelet, p, p_old, q_now, q_old), (field,) * 5, 10**8, "ready",
        far=(5, 6, 7), scratch=[pltpu.SemaphoreType.DMA((3,))])
    po, qo = p, q
    pre_p, pre_q, c, cs, ck = call(
        first_kernel, (side, live, own, other, base_p, base_q, hor, ver), (field,) * 5, 2 * 10**10, "first")
    p, q = call(halo_kernel, (odd, *halos, pre_p, pre_q, cs, ck), (field, field), 10**6, "halo")
    halos = exchange(p)
    traced = shape(2, 8, receiver_cells.shape[1])
    for step in range(1, STEPS):
        now = (at, source_cells, wavelet, p, po, q, qo, c, cs, ck)
        if step == 1:
            pre_p, pre_q = call(functools.partial(local_kernel, step), now, (field, field), 10**8, "local")
        if step == 2:
            pre_p, pre_q, early = call(
                functools.partial(early_kernel, step), (*now, receiver_cells), (field, field, traced), 10**8, "local_early")
        if step == 3:
            break
        po, qo = p, q
        p, q = call(
            halo_kernel, (odd, *halos, pre_p, pre_q, cs, ck), (field, field), 10**6, f"halo{step}")
        if step < 2:
            halos = exchange(p)
    total, = call(late_kernel, (at, source_cells, wavelet, receiver_cells, early, p, q), (traced,), 10**8, "late")
    sent, total = lax.optimization_barrier((p, total))
    halos = exchange(sent)

    def finish(total):
        pre_p, pre_q = call(functools.partial(local_kernel, 3), now, (field, field), 10**8, "local3")
        last = call(halo_kernel, (odd, *halos, pre_p, pre_q, cs, ck), (field, field), 10**6, "halo3")
        return lax.optimization_barrier((total, *last))

    total, p, q = reduced(total, blocks, finish)
    last = total[:, 4] + total[:, 0] * total[:, 5]
    traces = jnp.stack([total[:, 1], total[:, 2], total[:, 3], last], axis=1)
    return (p.reshape(pressure_now.shape), q.reshape(pressure_now.shape), traces)


def solution(mesh):
    grid = P("shot", "space", None, None, None)
    model = P("space", "shot", None, None)
    return jax.shard_map(
        per_device,
        mesh=mesh,
        in_specs=(grid, grid, grid, grid, model, model, model, P("shot", "space"), P("shot"), P("shot", None), P("shot", None)),
        out_specs=(grid, grid, P("shot", None, None)),
        check_vma=False,
    )
```

```python
import functools

import jax
import jax.numpy as jnp
from jax import lax
from jax.experimental import pallas as pl
from jax.experimental.pallas import tpu as pltpu
from jax.sharding import PartitionSpec as P

STEPS = 4
CX, CY, CZ = 4, 128, 128
ROWS = CX * CY
CELLS = ROWS * CZ

taps = (-205.0 / 72.0, 8.0 / 5.0, -1.0 / 5.0, 8.0 / 315.0, -1.0 / 560.0)
step_ratio = 0.08

VMEM = pl.BlockSpec(memory_space=pltpu.VMEM)
SMEM = pl.BlockSpec(memory_space=pltpu.SMEM)
FAR = pl.BlockSpec(memory_space=pltpu.HBM)
EXACT = lax.Precision.HIGHEST


def shape(*dims, dtype=jnp.float32):
    return jax.ShapeDtypeStruct(dims, dtype)


def call(kernel, ins, outs, flops, name, far=(), scratch=()):
    moved = 4 * sum(int(jnp.size(a)) for a in ins) + 4 * sum(o.size for o in outs)
    ins = [pltpu.with_memory_space_constraint(a, pltpu.HBM) if n in far else a for n, a in enumerate(ins)]
    specs = [FAR if n in far else SMEM if a.size <= 64 else VMEM for n, a in enumerate(ins)]
    return pl.pallas_call(
        kernel,
        out_shape=tuple(outs),
        in_specs=specs,
        out_specs=tuple(VMEM for _ in outs),
        scratch_shapes=scratch,
        compiler_params=pltpu.CompilerParams(vmem_limit_bytes=16 << 20),
        cost_estimate=pl.CostEstimate(flops=flops, bytes_accessed=moved, transcendentals=0),
        name=name,
    )(*ins)


def live_of(at_ref, active_ref, source_ref, s):
    here = source_ref[s] // CELLS == at_ref[0]
    return jnp.where(here | (active_ref[s] == 1), 1.0, 0.0)


def row(x):
    return pl.ds(x * CY, CY)


def model_kernel(v_far, e_far, d_far, own_ref, sems):
    copies = [pltpu.make_async_copy(src, own_ref.at[n], sems.at[n]) for n, src in enumerate((v_far, e_far, d_far))]
    for copy in copies:
        copy.start()
    for copy in copies:
        copy.wait()
    courant = (own_ref[0] * step_ratio) * (own_ref[0] * step_ratio)
    coupling = jnp.sqrt(1.0 + 2.0 * own_ref[2])
    own_ref[0] = courant
    own_ref[1] = courant * (1.0 + 2.0 * own_ref[1])
    own_ref[2] = courant * coupling


def begin_kernel(at_far, active_far, source_far, p_far, own_ref, p0_ref, odd_ref, live_ref, at_ref, active_ref, source_ref, sems):
    copies = [
        pltpu.make_async_copy(src, dst, sems.at[n])
        for n, (src, dst) in enumerate((
            (at_far, at_ref), (active_far, active_ref), (source_far, source_ref), (p_far, p0_ref)))
    ]
    for copy in copies:
        copy.start()
    for copy in copies:
        copy.wait()
    for s in range(2):
        live = live_of(at_ref, active_ref, source_ref, s)
        p0_ref[s] = p0_ref[s] * live
        live_ref[pl.ds(8 * s, 8), :] = jnp.full((8, CZ), live, jnp.float32)
    odd_ref[...] = jnp.full(odd_ref.shape, at_ref[0] & 1, jnp.int32)


def band():
    apart = jnp.abs(lax.broadcasted_iota(jnp.int32, (CZ, CZ), 0) - lax.broadcasted_iota(jnp.int32, (CZ, CZ), 1))
    out = jnp.zeros((CZ, CZ), jnp.float32)
    for k in range(5):
        out = jnp.where(apart == k, taps[k], out)
    return out


def second_diffs(s, x, p, q, mat):
    hor = jnp.dot(mat, p[s, row(x), :], precision=EXACT, preferred_element_type=jnp.float32)
    for other in range(CX):
        hor = hor + taps[abs(other - x)] * p[s, row(other), :]
    ver = jnp.dot(q[s, row(x), :], mat, precision=EXACT, preferred_element_type=jnp.float32)
    return hor, ver


def add_source(s, step, at_ref, source_ref, wavelet_ref, *refs):
    cell = source_ref[s] % CELLS
    gain = jnp.where(source_ref[s] // CELLS == at_ref[0], wavelet_ref[s, step], 0.0)
    lane = lax.broadcasted_iota(jnp.int32, (1, CZ), 1)
    add = jnp.where(lane == cell % CZ, gain, 0.0)
    line = pl.ds(cell // CZ, 1)
    for ref in refs:
        ref[s, line, :] = ref[s, line, :] + add


def ready_kernel(at_ref, active_ref, source_ref, wavelet_ref, p0, po_far, q_far, qo_far,
                 base_p, base_q, q, hor_ref, ver_ref, sems):
    copies = [
        pltpu.make_async_copy(src, dst, sems.at[n])
        for n, (src, dst) in enumerate(((q_far, q), (po_far, base_p), (qo_far, base_q)))
    ]
    for copy in copies:
        copy.start()
    mat = band()
    for copy in copies:
        copy.wait()
    for s in range(2):
        live = live_of(at_ref, active_ref, source_ref, s)
        q[s] = q[s] * live
        base_p[s] = 2.0 * p0[s] - base_p[s] * live
        base_q[s] = 2.0 * q[s] - base_q[s] * live
        for x in range(CX):
            hor_ref[s, row(x), :], ver_ref[s, row(x), :] = second_diffs(s, x, p0, q, mat)
        add_source(s, 0, at_ref, source_ref, wavelet_ref, base_p, base_q)


def halo_diff(x, lower, upper):
    hor = taps[4] * (lower[x] + upper[x])
    for k in range(1, 4):
        if x + k < CX:
            hor = hor + taps[4 - k] * lower[x + k]
        if x - k >= 0:
            hor = hor + taps[4 - k] * upper[x - k]
    return hor


def tile_at(x, tile):
    return pl.ds(x * CY + tile * 8, 8)


def halo_rows(s, tile, odd, even_pair, odd_pair):
    a = [even_pair[s, tile_at(x, tile), :] for x in range(CX)]
    b = [odd_pair[s, tile_at(x, tile), :] for x in range(CX)]
    return [jnp.where(odd, a[x], b[x]) for x in range(CX)], [jnp.where(odd, b[x], a[x]) for x in range(CX)]


def first_kernel(side_ref, live_ref, own, other, base_p, base_q, hor_ref, ver_ref, pre_p, pre_q, c_ref, cs_ref, ck_ref):
    def work(first, second):
        for tile in range(CY // 8):
            model = []
            for x in range(CX):
                half = (first, second)[x // 2]
                at = tile_at(x % 2, tile)
                model.append((half[0, at, :], half[1, at, :], half[2, at, :]))
            for s in range(2):
                live = live_ref[pl.ds(8 * s, 8), :]
                for x in range(CX):
                    at = tile_at(x, tile)
                    c, cs, ck = (m * live for m in model[x])
                    c_ref[s, at, :], cs_ref[s, at, :], ck_ref[s, at, :] = c, cs, ck
                    hor, ver = hor_ref[s, at, :], ver_ref[s, at, :]
                    pre_p[s, at, :] = base_p[s, at, :] + (cs * hor + ck * ver)
                    pre_q[s, at, :] = base_q[s, at, :] + (ck * hor + c * ver)

    @pl.when(side_ref[0] == 0)
    def _():
        work(own, other)

    @pl.when(side_ref[0] == 1)
    def _():
        work(other, own)


def local_part(step, at_ref, source_ref, wavelet_ref, p, po, q, qo, c_ref, cs_ref, ck_ref, pre_p, pre_q):
    mat = band()
    for s in range(2):
        for x in range(CX):
            here = row(x)
            hor, ver = second_diffs(s, x, p, q, mat)
            pre_p[s, here, :] = 2.0 * p[s, here, :] - po[s, here, :] + (cs_ref[s, here, :] * hor + ck_ref[s, here, :] * ver)
            pre_q[s, here, :] = 2.0 * q[s, here, :] - qo[s, here, :] + (ck_ref[s, here, :] * hor + c_ref[s, here, :] * ver)
        add_source(s, step, at_ref, source_ref, wavelet_ref, pre_p, pre_q)


def halo_kernel(odd_ref, even_pair, odd_pair, pre_p, pre_q, cs_ref, ck_ref, p, q):
    odd = odd_ref[...] == 1
    for s in range(2):
        for tile in range(CY // 8):
            lower, upper = halo_rows(s, tile, odd, even_pair, odd_pair)
            for x in range(CX):
                at = tile_at(x, tile)
                hor = halo_diff(x, lower, upper)
                p[s, at, :] = pre_p[s, at, :] + cs_ref[s, at, :] * hor
                q[s, at, :] = pre_q[s, at, :] + ck_ref[s, at, :] * hor


def samples(field, s, pick_z, pick_y):
    out = []
    for x in range(CX):
        rest, spread = field[s, row(x), :], None
        for _ in range(3):
            part = rest.astype(jnp.bfloat16)
            rest = rest - part.astype(jnp.float32)
            picked = jnp.dot(part, pick_z, preferred_element_type=jnp.float32)
            spread = picked if spread is None else spread + picked
        out.append(jnp.sum(jnp.where(pick_y, spread, 0.0), axis=0, keepdims=True))
    return out


def picks(cells_ref, s):
    cells = cells_ref[pl.ds(s, 1), :]
    n = cells.shape[1]
    inside = cells % CELLS
    pick_z = jnp.where(lax.broadcasted_iota(jnp.int32, (CZ, n), 0) == inside % CZ, 1.0, 0.0).astype(jnp.bfloat16)
    pick_y = lax.broadcasted_iota(jnp.int32, (CY, n), 0) == (inside // CZ) % CY
    return cells // CELLS, inside // (CY * CZ), pick_z, pick_y


def own_sample(values, block, x_at, me):
    out = jnp.zeros(block.shape, jnp.float32)
    for x in range(CX):
        out = jnp.where((x_at == x) & (block == me), values[x], out)
    return out


def local_kernel(step, at_ref, source_ref, wavelet_ref, p, po, q, qo, c_ref, cs_ref, ck_ref, pre_p, pre_q):
    local_part(step, at_ref, source_ref, wavelet_ref, p, po, q, qo, c_ref, cs_ref, ck_ref, pre_p, pre_q)


def early_kernel(step, at_ref, source_ref, wavelet_ref, p, po, q, qo, c_ref, cs_ref, ck_ref, cells_ref, pre_p, pre_q, out_ref):
    local_part(step, at_ref, source_ref, wavelet_ref, p, po, q, qo, c_ref, cs_ref, ck_ref, pre_p, pre_q)
    out_ref[...] = jnp.zeros(out_ref.shape, jnp.float32)
    for s in range(2):
        block, x_at, pick_z, pick_y = picks(cells_ref, s)
        for n, field in ((0, cs_ref), (1, po), (2, p), (7, ck_ref)):
            out_ref[s, pl.ds(n, 1), :] = own_sample(samples(field, s, pick_z, pick_y), block, x_at, at_ref[0])


def weights(apart):
    out = jnp.zeros(apart.shape, jnp.float32)
    for k in range(5):
        out = jnp.where(apart == k, taps[k], out)
    return out


def late_kernel(at_ref, source_ref, wavelet_ref, cells_ref, early_ref, p, q, out_ref):
    me = at_ref[0]
    out_ref[...] = early_ref[...]
    for s in range(2):
        block, x_at, pick_z, pick_y = picks(cells_ref, s)
        cells = cells_ref[pl.ds(s, 1), :]
        n = cells.shape[1]
        band_z = weights(jnp.abs(lax.broadcasted_iota(jnp.int32, (CZ, n), 0) - cells % CZ))
        band_y = weights(jnp.abs(lax.broadcasted_iota(jnp.int32, (CY, n), 0) - (cells // CZ) % CY))
        here = jnp.zeros(block.shape, jnp.float32)
        hor, ver, across = here, here, here
        for x in range(CX):
            rest, spread = p[s, row(x), :], None
            for _ in range(3):
                part = rest.astype(jnp.bfloat16)
                rest = rest - part.astype(jnp.float32)
                picked = jnp.dot(part, pick_z, preferred_element_type=jnp.float32)
                spread = picked if spread is None else spread + picked
            value = jnp.sum(jnp.where(pick_y, spread, 0.0), axis=0, keepdims=True)
            along_y = jnp.sum(band_y * spread, axis=0, keepdims=True)
            along_z = jnp.dot(q[s, row(x), :], band_z, precision=EXACT, preferred_element_type=jnp.float32)
            along_z = jnp.sum(jnp.where(pick_y, along_z, 0.0), axis=0, keepdims=True)
            here = jnp.where(x_at == x, value, here)
            hor = hor + weights(jnp.abs(x_at - x)) * value + jnp.where(x_at == x, along_y, 0.0)
            ver = jnp.where(x_at == x, along_z, ver)
            apart = jnp.where(block == me + 1, x_at + 4 - x, jnp.where(block == me - 1, 4 + x - x_at, 9))
            for k in range(1, 5):
                across = across + jnp.where(apart == k, taps[k] * value, 0.0)
        mine = jnp.where(block == me, 1.0, 0.0)
        here = mine * here
        gain = mine * jnp.where(cells == source_ref[s], wavelet_ref[s, STEPS - 1], 0.0)
        early = [early_ref[s, pl.ds(k, 1), :] for k in (0, 2, 7)]
        out_ref[s, pl.ds(3, 1), :] = here
        out_ref[s, pl.ds(4, 1), :] = 2.0 * here - early[1] + (early[0] * hor + early[2] * ver) + gain
        out_ref[s, pl.ds(5, 1), :] = across


def even_pairs(n):
    return [(i, i ^ 1) for i in range(n)]


def odd_pairs(n):
    up = [(i, i + 1) for i in range(1, n - 1, 2)]
    return up + [(b, a) for a, b in up]


def stages(n):
    if n != 128:
        bit, out = 1, []
        while bit < n:
            out.append([[(i, i ^ bit) for i in range(n)]])
            bit *= 2
        return out

    def device(z, xh, y, core):
        return ((z * 2 + xh) * 4 + y) * 2 + core

    def pairs(move):
        return [
            (device(z, xh, y, core), device(*move(z, xh, y, core)))
            for z in range(8) for xh in range(2) for y in range(4) for core in range(2)
        ]

    return [
        [pairs(lambda z, xh, y, core, k=k: (z, xh, y ^ k, core)) for k in (1, 3, 2)],
        [
            pairs(lambda z, xh, y, core: (z, xh, y, 1 - core)),
            pairs(lambda z, xh, y, core: (z, 1 - xh, y, core)),
            pairs(lambda z, xh, y, core: (z, 1 - xh, y, 1 - core)),
        ],
        [
            pairs(lambda z, xh, y, core: (z ^ 1, xh, y, core)),
            pairs(lambda z, xh, y, core: ((z + 1 if z % 2 else z - 1) % 8, xh, y, core)),
        ],
        [
            pairs(lambda z, xh, y, core: ((z - 3 if z % 2 else z + 3) % 8, xh, y, core)),
            pairs(lambda z, xh, y, core: ((z + 3 if z % 2 else z - 3) % 8, xh, y, core)),
        ],
    ]


def summed(total, stage):
    for part in [lax.ppermute(total, "space", pairs) for pairs in stage]:
        total = total + part
    return total


def reduced(total, n, gate, last_gate):
    todo = stages(n)
    if n != 128:
        total = gate(summed(total, todo[0]))
        for stage in todo[1:]:
            total = summed(total, stage)
        return last_gate(total)
    odd = (lax.axis_index("space") // 16) % 2 == 1
    first, second = (lax.ppermute(total, "space", pairs) for pairs in todo[2])
    two = total + jnp.where(odd, first, second)
    three = total + (first + second)
    even_part, odd_part, three = gate((jnp.where(odd, two, three), jnp.where(odd, three, two), three))
    plus = lax.ppermute(even_part, "space", todo[3][0])
    minus = lax.ppermute(odd_part, "space", todo[3][1])
    total = three + (plus + minus)
    return summed(last_gate(summed(total, todo[0])), todo[1])


def per_device(pressure_now, pressure_old, auxiliary_now, auxiliary_old, velocity, epsilon_field, delta_field,
               active_blocks, source_cells, receiver_cells, wavelet):
    blocks = lax.axis_size("space")
    at = lax.axis_index("space").astype(jnp.int32).reshape(1)
    side = lax.axis_index("shot").astype(jnp.int32).reshape(1)
    fields = (2, ROWS, CZ)
    p_now, p_old, q_now, q_old = (a.reshape(fields) for a in (pressure_now, pressure_old, auxiliary_now, auxiliary_old))
    half = (ROWS // 2, CZ)
    speed, eps, delta = (a.reshape(half) for a in (velocity, epsilon_field, delta_field))
    field = shape(*fields)
    active = active_blocks.reshape(2)
    ints = [pltpu.SMEM((1,), jnp.int32), pltpu.SMEM((2,), jnp.int32), pltpu.SMEM((2,), jnp.int32)]

    own, = call(
        model_kernel, (speed, eps, delta), (shape(3, *half),), 10**6, "model", far=range(3),
        scratch=[pltpu.SemaphoreType.DMA((3,))])
    p, odd, live = call(
        begin_kernel, (at, active, source_cells, p_now, own), (field, shape(8, CZ, dtype=jnp.int32), shape(16, CZ)), 10**6, "begin",
        far=range(4), scratch=ints + [pltpu.SemaphoreType.DMA((4,))])

    def exchange(values):
        return (lax.ppermute(values, "space", even_pairs(blocks)), lax.ppermute(values, "space", odd_pairs(blocks)))

    other = lax.ppermute(own, "shot", [(0, 1), (1, 0)])
    halos = exchange(p)
    base_p, base_q, q, hor, ver = call(
        ready_kernel, (at, active, source_cells, wavelet, p, p_old, q_now, q_old), (field,) * 5, 10**8, "ready",
        far=(5, 6, 7), scratch=[pltpu.SemaphoreType.DMA((3,))])
    po, qo = p, q
    pre_p, pre_q, c, cs, ck = call(
        first_kernel, (side, live, own, other, base_p, base_q, hor, ver), (field,) * 5, 2 * 10**10, "first")
    p, q = call(halo_kernel, (odd, *halos, pre_p, pre_q, cs, ck), (field, field), 10**6, "halo")
    halos = exchange(p)
    traced = shape(2, 8, receiver_cells.shape[1])
    for step in range(1, STEPS):
        now = (at, source_cells, wavelet, p, po, q, qo, c, cs, ck)
        if step == 1:
            pre_p, pre_q = call(functools.partial(local_kernel, step), now, (field, field), 10**8, "local")
        if step == 2:
            pre_p, pre_q, early = call(
                functools.partial(early_kernel, step), (*now, receiver_cells), (field, field, traced), 10**8, "local_early")
        if step == 3:
            break
        po, qo = p, q
        p, q = call(
            halo_kernel, (odd, *halos, pre_p, pre_q, cs, ck), (field, field), 10**6, f"halo{step}")
        if step < 2:
            halos = exchange(p)
    total, = call(late_kernel, (at, source_cells, wavelet, receiver_cells, early, p, q), (traced,), 10**8, "late")
    sent, total = lax.optimization_barrier((p, total))
    halos = exchange(sent)

    local = call(functools.partial(local_kernel, 3), now, (field, field), 10**8, "local3")

    def gate(total):
        nonlocal local
        total, local = lax.optimization_barrier((total, local))
        return total

    def last_gate(total):
        nonlocal halos
        total, halos = lax.optimization_barrier((total, halos))
        return total

    total = reduced(total, blocks, gate, last_gate)
    p, q = call(halo_kernel, (odd, *halos, *local, cs, ck), (field, field), 2 * 10**10, "halo3")
    last = total[:, 4] + total[:, 0] * total[:, 5]
    traces = jnp.stack([total[:, 1], total[:, 2], total[:, 3], last], axis=1)
    return (p.reshape(pressure_now.shape), q.reshape(pressure_now.shape), traces)


def solution(mesh):
    grid = P("shot", "space", None, None, None)
    model = P("space", "shot", None, None)
    return jax.shard_map(
        per_device,
        mesh=mesh,
        in_specs=(grid, grid, grid, grid, model, model, model, P("shot", "space"), P("shot"), P("shot", None), P("shot", None)),
        out_specs=(grid, grid, P("shot", None, None)),
        check_vma=False,
    )
```

```python
import functools

import jax
import jax.numpy as jnp
from jax import lax
from jax.experimental import pallas as pl
from jax.experimental.pallas import tpu as pltpu
from jax.sharding import PartitionSpec as P

STEPS = 4
CX, CY, CZ = 4, 128, 128
ROWS = CX * CY
CELLS = ROWS * CZ

taps = (-205.0 / 72.0, 8.0 / 5.0, -1.0 / 5.0, 8.0 / 315.0, -1.0 / 560.0)
step_ratio = 0.08

VMEM = pl.BlockSpec(memory_space=pltpu.VMEM)
SMEM = pl.BlockSpec(memory_space=pltpu.SMEM)
FAR = pl.BlockSpec(memory_space=pltpu.HBM)
EXACT = lax.Precision.HIGHEST


def shape(*dims, dtype=jnp.float32):
    return jax.ShapeDtypeStruct(dims, dtype)


def call(kernel, ins, outs, flops, name, far=(), scratch=()):
    moved = 4 * sum(int(jnp.size(a)) for a in ins) + 4 * sum(o.size for o in outs)
    ins = [pltpu.with_memory_space_constraint(a, pltpu.HBM) if n in far else a for n, a in enumerate(ins)]
    specs = [FAR if n in far else SMEM if a.size <= 64 else VMEM for n, a in enumerate(ins)]
    return pl.pallas_call(
        kernel,
        out_shape=tuple(outs),
        in_specs=specs,
        out_specs=tuple(VMEM for _ in outs),
        scratch_shapes=scratch,
        compiler_params=pltpu.CompilerParams(vmem_limit_bytes=16 << 20),
        cost_estimate=pl.CostEstimate(flops=flops, bytes_accessed=moved, transcendentals=0),
        name=name,
    )(*ins)


def live_of(at_ref, active_ref, source_ref, s):
    here = source_ref[s] // CELLS == at_ref[0]
    return jnp.where(here | (active_ref[s] == 1), 1.0, 0.0)


def row(x):
    return pl.ds(x * CY, CY)


def begin_kernel(at_far, side_far, active_far, source_far, v_far, e_far, d_far, p_far,
                 own_ref, p0_ref, odd_ref, live_ref, z_odd_ref, at_ref, active_ref, source_ref, sems):
    pairs = (
        (v_far, own_ref.at[0]), (e_far, own_ref.at[1]), (d_far, own_ref.at[2]),
        (at_far, at_ref), (active_far, active_ref), (source_far, source_ref), (p_far, p0_ref))
    copies = [pltpu.make_async_copy(src, dst, sems.at[n]) for n, (src, dst) in enumerate(pairs)]
    for copy in copies:
        copy.start()
    for copy in copies[:3]:
        copy.wait()
    courant = (own_ref[0] * step_ratio) * (own_ref[0] * step_ratio)
    coupling = jnp.sqrt(1.0 + 2.0 * own_ref[2])
    own_ref[0] = courant
    own_ref[1] = courant * (1.0 + 2.0 * own_ref[1])
    own_ref[2] = courant * coupling
    for copy in copies[3:]:
        copy.wait()
    for s in range(2):
        live = live_of(at_ref, active_ref, source_ref, s)
        p0_ref[s] = p0_ref[s] * live
        live_ref[pl.ds(8 * s, 8), :] = jnp.full((8, CZ), live, jnp.float32)
    odd_ref[...] = jnp.full(odd_ref.shape, at_ref[0] & 1, jnp.int32)
    z_odd_ref[...] = jnp.full(z_odd_ref.shape, (at_ref[0] // 16) & 1, jnp.int32)


def band():
    apart = jnp.abs(lax.broadcasted_iota(jnp.int32, (CZ, CZ), 0) - lax.broadcasted_iota(jnp.int32, (CZ, CZ), 1))
    out = jnp.zeros((CZ, CZ), jnp.float32)
    for k in range(5):
        out = jnp.where(apart == k, taps[k], out)
    return out


def second_diffs(s, x, p, q, mat):
    hor = jnp.dot(mat, p[s, row(x), :], precision=EXACT, preferred_element_type=jnp.float32)
    for other in range(CX):
        hor = hor + taps[abs(other - x)] * p[s, row(other), :]
    ver = jnp.dot(q[s, row(x), :], mat, precision=EXACT, preferred_element_type=jnp.float32)
    return hor, ver


def add_source(s, step, at_ref, source_ref, wavelet_ref, *refs):
    cell = source_ref[s] % CELLS
    gain = jnp.where(source_ref[s] // CELLS == at_ref[0], wavelet_ref[s, step], 0.0)
    lane = lax.broadcasted_iota(jnp.int32, (1, CZ), 1)
    add = jnp.where(lane == cell % CZ, gain, 0.0)
    line = pl.ds(cell // CZ, 1)
    for ref in refs:
        ref[s, line, :] = ref[s, line, :] + add


def ready_kernel(at_ref, active_ref, source_ref, wavelet_ref, p0, po_far, q_far, qo_far,
                 base_p, base_q, q, hor_ref, ver_ref, sems):
    copies = [
        pltpu.make_async_copy(src, dst, sems.at[n])
        for n, (src, dst) in enumerate(((q_far, q), (po_far, base_p), (qo_far, base_q)))
    ]
    for copy in copies:
        copy.start()
    mat = band()
    for copy in copies:
        copy.wait()
    for s in range(2):
        live = live_of(at_ref, active_ref, source_ref, s)
        q[s] = q[s] * live
        base_p[s] = 2.0 * p0[s] - base_p[s] * live
        base_q[s] = 2.0 * q[s] - base_q[s] * live
        for x in range(CX):
            hor_ref[s, row(x), :], ver_ref[s, row(x), :] = second_diffs(s, x, p0, q, mat)
        add_source(s, 0, at_ref, source_ref, wavelet_ref, base_p, base_q)


def halo_diff(x, lower, upper):
    hor = taps[4] * (lower[x] + upper[x])
    for k in range(1, 4):
        if x + k < CX:
            hor = hor + taps[4 - k] * lower[x + k]
        if x - k >= 0:
            hor = hor + taps[4 - k] * upper[x - k]
    return hor


def tile_at(x, tile):
    return pl.ds(x * CY + tile * 8, 8)


def halo_rows(s, tile, odd, even_pair, odd_pair):
    a = [even_pair[s, tile_at(x, tile), :] for x in range(CX)]
    b = [odd_pair[s, tile_at(x, tile), :] for x in range(CX)]
    return [jnp.where(odd, a[x], b[x]) for x in range(CX)], [jnp.where(odd, b[x], a[x]) for x in range(CX)]


def first_kernel(side_ref, live_ref, own, other, base_p, base_q, hor_ref, ver_ref, pre_p, pre_q, c_ref, cs_ref, ck_ref):
    def work(first, second):
        for tile in range(CY // 8):
            model = []
            for x in range(CX):
                half = (first, second)[x // 2]
                at = tile_at(x % 2, tile)
                model.append((half[0, at, :], half[1, at, :], half[2, at, :]))
            for s in range(2):
                live = live_ref[pl.ds(8 * s, 8), :]
                for x in range(CX):
                    at = tile_at(x, tile)
                    c, cs, ck = (m * live for m in model[x])
                    c_ref[s, at, :], cs_ref[s, at, :], ck_ref[s, at, :] = c, cs, ck
                    hor, ver = hor_ref[s, at, :], ver_ref[s, at, :]
                    pre_p[s, at, :] = base_p[s, at, :] + (cs * hor + ck * ver)
                    pre_q[s, at, :] = base_q[s, at, :] + (ck * hor + c * ver)

    @pl.when(side_ref[0] == 0)
    def _():
        work(own, other)

    @pl.when(side_ref[0] == 1)
    def _():
        work(other, own)


def local_part(step, at_ref, source_ref, wavelet_ref, p, po, q, qo, c_ref, cs_ref, ck_ref, pre_p, pre_q):
    mat = band()
    for s in range(2):
        for x in range(CX):
            here = row(x)
            hor, ver = second_diffs(s, x, p, q, mat)
            pre_p[s, here, :] = 2.0 * p[s, here, :] - po[s, here, :] + (cs_ref[s, here, :] * hor + ck_ref[s, here, :] * ver)
            pre_q[s, here, :] = 2.0 * q[s, here, :] - qo[s, here, :] + (ck_ref[s, here, :] * hor + c_ref[s, here, :] * ver)
        add_source(s, step, at_ref, source_ref, wavelet_ref, pre_p, pre_q)


def halo_kernel(odd_ref, even_pair, odd_pair, pre_p, pre_q, cs_ref, ck_ref, p, q):
    odd = odd_ref[...] == 1
    for s in range(2):
        for tile in range(CY // 8):
            lower, upper = halo_rows(s, tile, odd, even_pair, odd_pair)
            for x in range(CX):
                at = tile_at(x, tile)
                hor = halo_diff(x, lower, upper)
                p[s, at, :] = pre_p[s, at, :] + cs_ref[s, at, :] * hor
                q[s, at, :] = pre_q[s, at, :] + ck_ref[s, at, :] * hor


def samples(field, s, pick_z, pick_y):
    out = []
    for x in range(CX):
        rest, spread = field[s, row(x), :], None
        for _ in range(3):
            part = rest.astype(jnp.bfloat16)
            rest = rest - part.astype(jnp.float32)
            picked = jnp.dot(part, pick_z, preferred_element_type=jnp.float32)
            spread = picked if spread is None else spread + picked
        out.append(jnp.sum(jnp.where(pick_y, spread, 0.0), axis=0, keepdims=True))
    return out


def picks(cells_ref, s):
    cells = cells_ref[pl.ds(s, 1), :]
    n = cells.shape[1]
    inside = cells % CELLS
    pick_z = jnp.where(lax.broadcasted_iota(jnp.int32, (CZ, n), 0) == inside % CZ, 1.0, 0.0).astype(jnp.bfloat16)
    pick_y = lax.broadcasted_iota(jnp.int32, (CY, n), 0) == (inside // CZ) % CY
    return cells // CELLS, inside // (CY * CZ), pick_z, pick_y


def own_sample(values, block, x_at, me):
    out = jnp.zeros(block.shape, jnp.float32)
    for x in range(CX):
        out = jnp.where((x_at == x) & (block == me), values[x], out)
    return out


def local_kernel(step, at_ref, source_ref, wavelet_ref, p, po, q, qo, c_ref, cs_ref, ck_ref, pre_p, pre_q):
    local_part(step, at_ref, source_ref, wavelet_ref, p, po, q, qo, c_ref, cs_ref, ck_ref, pre_p, pre_q)


def early_kernel(step, at_ref, source_ref, wavelet_ref, p, po, q, qo, c_ref, cs_ref, ck_ref, cells_ref, pre_p, pre_q, out_ref):
    local_part(step, at_ref, source_ref, wavelet_ref, p, po, q, qo, c_ref, cs_ref, ck_ref, pre_p, pre_q)
    out_ref[...] = jnp.zeros(out_ref.shape, jnp.float32)
    for s in range(2):
        block, x_at, pick_z, pick_y = picks(cells_ref, s)
        for n, field in ((0, cs_ref), (1, po), (2, p), (7, ck_ref)):
            out_ref[s, pl.ds(n, 1), :] = own_sample(samples(field, s, pick_z, pick_y), block, x_at, at_ref[0])


def weights(apart):
    out = jnp.zeros(apart.shape, jnp.float32)
    for k in range(5):
        out = jnp.where(apart == k, taps[k], out)
    return out


def late_kernel(at_ref, source_ref, wavelet_ref, cells_ref, early_ref, p, q, out_ref):
    me = at_ref[0]
    out_ref[...] = early_ref[...]
    for s in range(2):
        block, x_at, pick_z, pick_y = picks(cells_ref, s)
        cells = cells_ref[pl.ds(s, 1), :]
        n = cells.shape[1]
        band_z = weights(jnp.abs(lax.broadcasted_iota(jnp.int32, (CZ, n), 0) - cells % CZ))
        band_y = weights(jnp.abs(lax.broadcasted_iota(jnp.int32, (CY, n), 0) - (cells // CZ) % CY))
        here = jnp.zeros(block.shape, jnp.float32)
        hor, ver, across = here, here, here
        for x in range(CX):
            rest, spread = p[s, row(x), :], None
            for _ in range(3):
                part = rest.astype(jnp.bfloat16)
                rest = rest - part.astype(jnp.float32)
                picked = jnp.dot(part, pick_z, preferred_element_type=jnp.float32)
                spread = picked if spread is None else spread + picked
            value = jnp.sum(jnp.where(pick_y, spread, 0.0), axis=0, keepdims=True)
            along_y = jnp.sum(band_y * spread, axis=0, keepdims=True)
            along_z = jnp.dot(q[s, row(x), :], band_z, precision=EXACT, preferred_element_type=jnp.float32)
            along_z = jnp.sum(jnp.where(pick_y, along_z, 0.0), axis=0, keepdims=True)
            here = jnp.where(x_at == x, value, here)
            hor = hor + weights(jnp.abs(x_at - x)) * value + jnp.where(x_at == x, along_y, 0.0)
            ver = jnp.where(x_at == x, along_z, ver)
            apart = jnp.where(block == me + 1, x_at + 4 - x, jnp.where(block == me - 1, 4 + x - x_at, 9))
            for k in range(1, 5):
                across = across + jnp.where(apart == k, taps[k] * value, 0.0)
        mine = jnp.where(block == me, 1.0, 0.0)
        here = mine * here
        gain = mine * jnp.where(cells == source_ref[s], wavelet_ref[s, STEPS - 1], 0.0)
        early = [early_ref[s, pl.ds(k, 1), :] for k in (0, 2, 7)]
        out_ref[s, pl.ds(3, 1), :] = here
        out_ref[s, pl.ds(4, 1), :] = 2.0 * here - early[1] + (early[0] * hor + early[2] * ver) + gain
        out_ref[s, pl.ds(5, 1), :] = across


def even_pairs(n):
    return [(i, i ^ 1) for i in range(n)]


def odd_pairs(n):
    up = [(i, i + 1) for i in range(1, n - 1, 2)]
    return up + [(b, a) for a, b in up]


def stages(n):
    if n != 128:
        bit, out = 1, []
        while bit < n:
            out.append([[(i, i ^ bit) for i in range(n)]])
            bit *= 2
        return out

    def device(z, xh, y, core):
        return ((z * 2 + xh) * 4 + y) * 2 + core

    def pairs(move):
        return [
            (device(z, xh, y, core), device(*move(z, xh, y, core)))
            for z in range(8) for xh in range(2) for y in range(4) for core in range(2)
        ]

    return [
        [pairs(lambda z, xh, y, core, k=k: (z, xh, y ^ k, core)) for k in (1, 3, 2)],
        [
            pairs(lambda z, xh, y, core: (z, xh, y, 1 - core)),
            pairs(lambda z, xh, y, core: (z, 1 - xh, y, core)),
            pairs(lambda z, xh, y, core: (z, 1 - xh, y, 1 - core)),
        ],
        [
            pairs(lambda z, xh, y, core: (z ^ 1, xh, y, core)),
            pairs(lambda z, xh, y, core: ((z + 1 if z % 2 else z - 1) % 8, xh, y, core)),
        ],
        [
            pairs(lambda z, xh, y, core: ((z - 3 if z % 2 else z + 3) % 8, xh, y, core)),
            pairs(lambda z, xh, y, core: ((z + 3 if z % 2 else z - 3) % 8, xh, y, core)),
        ],
    ]


def summed(total, stage):
    for part in [lax.ppermute(total, "space", pairs) for pairs in stage]:
        total = total + part
    return total


def reduced(total, n, z_odd, gate, last_gate):
    todo = stages(n)
    if n != 128:
        total = gate(summed(total, todo[0]))
        for stage in todo[1:]:
            total = summed(total, stage)
        return last_gate(total)
    odd = z_odd == 1
    first, second = (lax.ppermute(total, "space", pairs) for pairs in todo[2])
    two = total + jnp.where(odd, first, second)
    three = total + (first + second)
    even_part, odd_part = jnp.where(odd, two, three), jnp.where(odd, three, two)
    plus = lax.ppermute(even_part, "space", todo[3][0])
    minus = lax.ppermute(odd_part, "space", todo[3][1])
    total = gate(three + (plus + minus))
    return summed(last_gate(summed(total, todo[0])), todo[1])


def per_device(pressure_now, pressure_old, auxiliary_now, auxiliary_old, velocity, epsilon_field, delta_field,
               active_blocks, source_cells, receiver_cells, wavelet):
    blocks = lax.axis_size("space")
    at = lax.axis_index("space").astype(jnp.int32).reshape(1)
    side = lax.axis_index("shot").astype(jnp.int32).reshape(1)
    fields = (2, ROWS, CZ)
    p_now, p_old, q_now, q_old = (a.reshape(fields) for a in (pressure_now, pressure_old, auxiliary_now, auxiliary_old))
    half = (ROWS // 2, CZ)
    speed, eps, delta = (a.reshape(half) for a in (velocity, epsilon_field, delta_field))
    field = shape(*fields)
    active = active_blocks.reshape(2)
    ints = [pltpu.SMEM((1,), jnp.int32), pltpu.SMEM((2,), jnp.int32), pltpu.SMEM((2,), jnp.int32)]

    own, p, odd, live, z_odd = call(
        begin_kernel, (at, side, active, source_cells, speed, eps, delta, p_now),
        (shape(3, *half), field, shape(8, CZ, dtype=jnp.int32), shape(16, CZ),
         shape(2, 8, receiver_cells.shape[1], dtype=jnp.int32)),
        10**6, "begin", far=range(8), scratch=ints + [pltpu.SemaphoreType.DMA((7,))])

    def exchange(values):
        return (lax.ppermute(values, "space", even_pairs(blocks)), lax.ppermute(values, "space", odd_pairs(blocks)))

    other = lax.ppermute(own, "shot", [(0, 1), (1, 0)])
    halos = exchange(p)
    base_p, base_q, q, hor, ver = call(
        ready_kernel, (at, active, source_cells, wavelet, p, p_old, q_now, q_old), (field,) * 5, 10**8, "ready",
        far=(5, 6, 7), scratch=[pltpu.SemaphoreType.DMA((3,))])
    po, qo = p, q
    pre_p, pre_q, c, cs, ck = call(
        first_kernel, (side, live, own, other, base_p, base_q, hor, ver), (field,) * 5, 2 * 10**10, "first")
    p, q = call(halo_kernel, (odd, *halos, pre_p, pre_q, cs, ck), (field, field), 10**6, "halo")
    halos = exchange(p)
    traced = shape(2, 8, receiver_cells.shape[1])
    for step in range(1, STEPS):
        now = (at, source_cells, wavelet, p, po, q, qo, c, cs, ck)
        if step == 1:
            pre_p, pre_q = call(functools.partial(local_kernel, step), now, (field, field), 10**8, "local")
        if step == 2:
            pre_p, pre_q, early = call(
                functools.partial(early_kernel, step), (*now, receiver_cells), (field, field, traced), 10**8, "local_early")
        if step == 3:
            break
        po, qo = p, q
        p, q = call(
            halo_kernel, (odd, *halos, pre_p, pre_q, cs, ck), (field, field), 10**6, f"halo{step}")
        if step < 2:
            halos = exchange(p)
    total, = call(late_kernel, (at, source_cells, wavelet, receiver_cells, early, p, q), (traced,), 10**8, "late")
    sent, total = lax.optimization_barrier((p, total))
    halos = exchange(sent)

    local = call(functools.partial(local_kernel, 3), now, (field, field), 10**8, "local3")

    def gate(total):
        nonlocal local
        total, local = lax.optimization_barrier((total, local))
        return total

    def last_gate(total):
        nonlocal halos
        total, halos = lax.optimization_barrier((total, halos))
        return total

    total = reduced(total, blocks, z_odd, gate, last_gate)
    p, q = call(halo_kernel, (odd, *halos, *local, cs, ck), (field, field), 2 * 10**10, "halo3")
    last = total[:, 4] + total[:, 0] * total[:, 5]
    traces = jnp.stack([total[:, 1], total[:, 2], total[:, 3], last], axis=1)
    return (p.reshape(pressure_now.shape), q.reshape(pressure_now.shape), traces)


def solution(mesh):
    grid = P("shot", "space", None, None, None)
    model = P("space", "shot", None, None)
    return jax.shard_map(
        per_device,
        mesh=mesh,
        in_specs=(grid, grid, grid, grid, model, model, model, P("shot", "space"), P("shot"), P("shot", None), P("shot", None)),
        out_specs=(grid, grid, P("shot", None, None)),
        check_vma=False,
    )
```

```python
import functools

import jax
import jax.numpy as jnp
from jax import lax
from jax.experimental import pallas as pl
from jax.experimental.pallas import tpu as pltpu
from jax.sharding import PartitionSpec as P

STEPS = 4
CX, CY, CZ = 4, 128, 128
ROWS = CX * CY
CELLS = ROWS * CZ

taps = (-205.0 / 72.0, 8.0 / 5.0, -1.0 / 5.0, 8.0 / 315.0, -1.0 / 560.0)
step_ratio = 0.08

VMEM = pl.BlockSpec(memory_space=pltpu.VMEM)
SMEM = pl.BlockSpec(memory_space=pltpu.SMEM)
FAR = pl.BlockSpec(memory_space=pltpu.HBM)
EXACT = lax.Precision.HIGHEST


def shape(*dims, dtype=jnp.float32):
    return jax.ShapeDtypeStruct(dims, dtype)


def call(kernel, ins, outs, flops, name, far=(), scratch=()):
    moved = 4 * sum(int(jnp.size(a)) for a in ins) + 4 * sum(o.size for o in outs)
    ins = [pltpu.with_memory_space_constraint(a, pltpu.HBM) if n in far else a for n, a in enumerate(ins)]
    specs = [FAR if n in far else SMEM if a.size <= 64 else VMEM for n, a in enumerate(ins)]
    return pl.pallas_call(
        kernel,
        out_shape=tuple(outs),
        in_specs=specs,
        out_specs=tuple(VMEM for _ in outs),
        scratch_shapes=scratch,
        compiler_params=pltpu.CompilerParams(vmem_limit_bytes=16 << 20),
        cost_estimate=pl.CostEstimate(flops=flops, bytes_accessed=moved, transcendentals=0),
        name=name,
    )(*ins)


def live_of(at_ref, active_ref, source_ref, s):
    here = source_ref[s] // CELLS == at_ref[0]
    return jnp.where(here | (active_ref[s] == 1), 1.0, 0.0)


def row(x):
    return pl.ds(x * CY, CY)


def begin_kernel(at_far, side_far, active_far, source_far, v_far, e_far, d_far, p_far,
                 own_ref, p0_ref, odd_ref, live_ref, z_odd_ref, at_ref, active_ref, source_ref, sems):
    pairs = (
        (v_far, own_ref.at[0]), (e_far, own_ref.at[1]), (d_far, own_ref.at[2]),
        (at_far, at_ref), (active_far, active_ref), (source_far, source_ref), (p_far, p0_ref))
    copies = [pltpu.make_async_copy(src, dst, sems.at[n]) for n, (src, dst) in enumerate(pairs)]
    for copy in copies:
        copy.start()
    for copy in copies[:3]:
        copy.wait()
    courant = (own_ref[0] * step_ratio) * (own_ref[0] * step_ratio)
    coupling = jnp.sqrt(1.0 + 2.0 * own_ref[2])
    own_ref[0] = courant
    own_ref[1] = courant * (1.0 + 2.0 * own_ref[1])
    own_ref[2] = courant * coupling
    for copy in copies[3:]:
        copy.wait()
    for s in range(2):
        live = live_of(at_ref, active_ref, source_ref, s)
        p0_ref[s] = p0_ref[s] * live
        live_ref[pl.ds(8 * s, 8), :] = jnp.full((8, CZ), live, jnp.float32)
    odd_ref[...] = jnp.full(odd_ref.shape, at_ref[0] & 1, jnp.int32)
    z_odd_ref[...] = jnp.full(z_odd_ref.shape, (at_ref[0] // 16) & 1, jnp.int32)


def band():
    apart = jnp.abs(lax.broadcasted_iota(jnp.int32, (CZ, CZ), 0) - lax.broadcasted_iota(jnp.int32, (CZ, CZ), 1))
    out = jnp.zeros((CZ, CZ), jnp.float32)
    for k in range(5):
        out = jnp.where(apart == k, taps[k], out)
    return out


def second_diffs(s, x, p, q, mat):
    hor = jnp.dot(mat, p[s, row(x), :], precision=EXACT, preferred_element_type=jnp.float32)
    for other in range(CX):
        hor = hor + taps[abs(other - x)] * p[s, row(other), :]
    ver = jnp.dot(q[s, row(x), :], mat, precision=EXACT, preferred_element_type=jnp.float32)
    return hor, ver


def add_source(s, step, at_ref, source_ref, wavelet_ref, *refs):
    cell = source_ref[s] % CELLS
    gain = jnp.where(source_ref[s] // CELLS == at_ref[0], wavelet_ref[s, step], 0.0)
    lane = lax.broadcasted_iota(jnp.int32, (1, CZ), 1)
    add = jnp.where(lane == cell % CZ, gain, 0.0)
    line = pl.ds(cell // CZ, 1)
    for ref in refs:
        ref[s, line, :] = ref[s, line, :] + add


def ready_kernel(at_ref, active_ref, source_ref, wavelet_ref, p0, po_far, q_far, qo_far,
                 base_p, base_q, q, hor_ref, ver_ref, sems):
    copies = [
        pltpu.make_async_copy(src, dst, sems.at[n])
        for n, (src, dst) in enumerate(((q_far, q), (po_far, base_p), (qo_far, base_q)))
    ]
    for copy in copies:
        copy.start()
    mat = band()
    for copy in copies:
        copy.wait()
    for s in range(2):
        live = live_of(at_ref, active_ref, source_ref, s)
        q[s] = q[s] * live
        base_p[s] = 2.0 * p0[s] - base_p[s] * live
        base_q[s] = 2.0 * q[s] - base_q[s] * live
        for x in range(CX):
            hor_ref[s, row(x), :], ver_ref[s, row(x), :] = second_diffs(s, x, p0, q, mat)
        add_source(s, 0, at_ref, source_ref, wavelet_ref, base_p, base_q)


def side_diff(x, rows, upper):
    above = below = taps[4] * rows[x]
    for k in range(1, 4):
        if x + k < CX:
            below = below + taps[4 - k] * rows[x + k]
        if x - k >= 0:
            above = above + taps[4 - k] * rows[x - k]
    return jnp.where(upper, above, below)


def tile_at(x, tile):
    return pl.ds(x * CY + tile * 8, 8)


def flat_at(s, x, tile):
    return pl.ds(s * ROWS + x * CY + tile * 8, 8)


def first_kernel(side_ref, live_ref, own, other, base_p, base_q, hor_ref, ver_ref, pre_p, pre_q, c_ref, cs_ref, ck_ref, extra_ref):
    extra_ref[pl.ds(ROWS, 16), :] = live_ref[...]

    def work(first, second):
        for tile in range(CY // 8):
            model = []
            for x in range(CX):
                half = (first, second)[x // 2]
                at = tile_at(x % 2, tile)
                model.append((half[0, at, :], half[1, at, :], half[2, at, :]))
                extra_ref[tile_at(x, tile), :] = model[x][1]
            for s in range(2):
                live = live_ref[pl.ds(8 * s, 8), :]
                for x in range(CX):
                    at = tile_at(x, tile)
                    c, cs, ck = (m * live for m in model[x])
                    c_ref[s, at, :], cs_ref[s, at, :], ck_ref[s, at, :] = c, cs, ck
                    hor, ver = hor_ref[s, at, :], ver_ref[s, at, :]
                    pre_p[s, at, :] = base_p[s, at, :] + (cs * hor + ck * ver)
                    pre_q[s, at, :] = base_q[s, at, :] + (ck * hor + c * ver)

    @pl.when(side_ref[0] == 0)
    def _():
        work(own, other)

    @pl.when(side_ref[0] == 1)
    def _():
        work(other, own)


def local_part(step, at_ref, source_ref, wavelet_ref, p, po, q, qo, c_ref, cs_ref, ck_ref, pre_p, pre_q):
    mat = band()
    for s in range(2):
        for x in range(CX):
            here = row(x)
            hor, ver = second_diffs(s, x, p, q, mat)
            pre_p[s, here, :] = 2.0 * p[s, here, :] - po[s, here, :] + (cs_ref[s, here, :] * hor + ck_ref[s, here, :] * ver)
            pre_q[s, here, :] = 2.0 * q[s, here, :] - qo[s, here, :] + (ck_ref[s, here, :] * hor + c_ref[s, here, :] * ver)
        add_source(s, step, at_ref, source_ref, wavelet_ref, pre_p, pre_q)


def chip_kernel(odd_ref, even_pair, pre_p, pre_q, cs_ref, ck_ref, *rest):
    extra, (out_p, out_q) = rest[:-2], rest[-2:]
    upper = odd_ref[...] == 0
    for ref in extra:
        out_p[pl.ds(2 * ROWS, ROWS + 16), :] = ref[...]
    for s in range(2):
        for tile in range(CY // 8):
            rows = [even_pair[s, tile_at(x, tile), :] for x in range(CX)]
            for x in range(CX):
                at = tile_at(x, tile)
                hor = side_diff(x, rows, upper)
                out_p[flat_at(s, x, tile), :] = pre_p[s, at, :] + cs_ref[s, at, :] * hor
                out_q[s, at, :] = pre_q[s, at, :] + ck_ref[s, at, :] * hor


def join(odd_ref, other_rows, part_p, part_q, cs_ref, ck_ref, p, q):
    upper = odd_ref[...] == 1
    for s in range(2):
        for tile in range(CY // 8):
            rows = other_rows(s, tile)
            for x in range(CX):
                at = tile_at(x, tile)
                hor = side_diff(x, rows, upper)
                p[s, at, :] = part_p[flat_at(s, x, tile), :] + cs_ref[s, at, :] * hor
                q[s, at, :] = part_q[s, at, :] + ck_ref[s, at, :] * hor


def first_join_kernel(odd_ref, got, part_p, part_q, cs_ref, ck_ref, p, q):
    def other_rows(s, tile):
        return [got[s, tile_at(x, tile), :] for x in range(CX)]

    join(odd_ref, other_rows, part_p, part_q, cs_ref, ck_ref, p, q)


def join_kernel(odd_ref, got, extra, before, part_p, part_q, cs_ref, ck_ref, p, q):
    upper = odd_ref[...] == 0

    def other_rows(s, tile):
        mine = [before[s, tile_at(x, tile), :] for x in range(CX)]
        live = extra[pl.ds(3 * ROWS + 8 * s, 8), :]
        out = []
        for x in range(CX):
            stretch = extra[pl.ds(2 * ROWS + x * CY + tile * 8, 8), :] * live
            out.append(got[flat_at(s, x, tile), :] + stretch * side_diff(x, mine, upper))
        return out

    join(odd_ref, other_rows, part_p, part_q, cs_ref, ck_ref, p, q)


def samples(field, s, pick_z, pick_y):
    out = []
    for x in range(CX):
        rest, spread = field[s, row(x), :], None
        for _ in range(3):
            part = rest.astype(jnp.bfloat16)
            rest = rest - part.astype(jnp.float32)
            picked = jnp.dot(part, pick_z, preferred_element_type=jnp.float32)
            spread = picked if spread is None else spread + picked
        out.append(jnp.sum(jnp.where(pick_y, spread, 0.0), axis=0, keepdims=True))
    return out


def picks(cells_ref, s):
    cells = cells_ref[pl.ds(s, 1), :]
    n = cells.shape[1]
    inside = cells % CELLS
    pick_z = jnp.where(lax.broadcasted_iota(jnp.int32, (CZ, n), 0) == inside % CZ, 1.0, 0.0).astype(jnp.bfloat16)
    pick_y = lax.broadcasted_iota(jnp.int32, (CY, n), 0) == (inside // CZ) % CY
    return cells // CELLS, inside // (CY * CZ), pick_z, pick_y


def own_sample(values, block, x_at, me):
    out = jnp.zeros(block.shape, jnp.float32)
    for x in range(CX):
        out = jnp.where((x_at == x) & (block == me), values[x], out)
    return out


def local_kernel(step, at_ref, source_ref, wavelet_ref, p, po, q, qo, c_ref, cs_ref, ck_ref, pre_p, pre_q):
    local_part(step, at_ref, source_ref, wavelet_ref, p, po, q, qo, c_ref, cs_ref, ck_ref, pre_p, pre_q)


def early_kernel(step, at_ref, source_ref, wavelet_ref, p, po, q, qo, c_ref, cs_ref, ck_ref, cells_ref, pre_p, pre_q, out_ref):
    local_part(step, at_ref, source_ref, wavelet_ref, p, po, q, qo, c_ref, cs_ref, ck_ref, pre_p, pre_q)
    out_ref[...] = jnp.zeros(out_ref.shape, jnp.float32)
    for s in range(2):
        block, x_at, pick_z, pick_y = picks(cells_ref, s)
        for n, field in ((0, cs_ref), (1, po), (2, p), (7, ck_ref)):
            out_ref[s, pl.ds(n, 1), :] = own_sample(samples(field, s, pick_z, pick_y), block, x_at, at_ref[0])


def weights(apart):
    out = jnp.zeros(apart.shape, jnp.float32)
    for k in range(5):
        out = jnp.where(apart == k, taps[k], out)
    return out


def late_kernel(at_ref, source_ref, wavelet_ref, cells_ref, early_ref, p, q, out_ref):
    me = at_ref[0]
    out_ref[...] = early_ref[...]
    for s in range(2):
        block, x_at, pick_z, pick_y = picks(cells_ref, s)
        cells = cells_ref[pl.ds(s, 1), :]
        n = cells.shape[1]
        band_z = weights(jnp.abs(lax.broadcasted_iota(jnp.int32, (CZ, n), 0) - cells % CZ))
        band_y = weights(jnp.abs(lax.broadcasted_iota(jnp.int32, (CY, n), 0) - (cells // CZ) % CY))
        here = jnp.zeros(block.shape, jnp.float32)
        hor, ver, across = here, here, here
        for x in range(CX):
            rest, spread = p[s, row(x), :], None
            for _ in range(3):
                part = rest.astype(jnp.bfloat16)
                rest = rest - part.astype(jnp.float32)
                picked = jnp.dot(part, pick_z, preferred_element_type=jnp.float32)
                spread = picked if spread is None else spread + picked
            value = jnp.sum(jnp.where(pick_y, spread, 0.0), axis=0, keepdims=True)
            along_y = jnp.sum(band_y * spread, axis=0, keepdims=True)
            along_z = jnp.dot(q[s, row(x), :], band_z, precision=EXACT, preferred_element_type=jnp.float32)
            along_z = jnp.sum(jnp.where(pick_y, along_z, 0.0), axis=0, keepdims=True)
            here = jnp.where(x_at == x, value, here)
            hor = hor + weights(jnp.abs(x_at - x)) * value + jnp.where(x_at == x, along_y, 0.0)
            ver = jnp.where(x_at == x, along_z, ver)
            apart = jnp.where(block == me + 1, x_at + 4 - x, jnp.where(block == me - 1, 4 + x - x_at, 9))
            for k in range(1, 5):
                across = across + jnp.where(apart == k, taps[k] * value, 0.0)
        mine = jnp.where(block == me, 1.0, 0.0)
        here = mine * here
        gain = mine * jnp.where(cells == source_ref[s], wavelet_ref[s, STEPS - 1], 0.0)
        early = [early_ref[s, pl.ds(k, 1), :] for k in (0, 2, 7)]
        out_ref[s, pl.ds(3, 1), :] = here
        out_ref[s, pl.ds(4, 1), :] = 2.0 * here - early[1] + (early[0] * hor + early[2] * ver) + gain
        out_ref[s, pl.ds(5, 1), :] = across


def even_pairs(n):
    return [(i, i ^ 1) for i in range(n)]


def odd_pairs(n):
    up = [(i, i + 1) for i in range(1, n - 1, 2)]
    return up + [(b, a) for a, b in up]


def stages(n):
    if n != 128:
        bit, out = 1, []
        while bit < n:
            out.append([[(i, i ^ bit) for i in range(n)]])
            bit *= 2
        return out

    def device(z, xh, y, core):
        return ((z * 2 + xh) * 4 + y) * 2 + core

    def pairs(move):
        return [
            (device(z, xh, y, core), device(*move(z, xh, y, core)))
            for z in range(8) for xh in range(2) for y in range(4) for core in range(2)
        ]

    return [
        [pairs(lambda z, xh, y, core, k=k: (z, xh, y ^ k, core)) for k in (1, 3, 2)],
        [
            pairs(lambda z, xh, y, core: (z, xh, y, 1 - core)),
            pairs(lambda z, xh, y, core: (z, 1 - xh, y, core)),
            pairs(lambda z, xh, y, core: (z, 1 - xh, y, 1 - core)),
        ],
        [
            pairs(lambda z, xh, y, core: (z ^ 1, xh, y, core)),
            pairs(lambda z, xh, y, core: ((z + 1 if z % 2 else z - 1) % 8, xh, y, core)),
        ],
        [
            pairs(lambda z, xh, y, core: ((z - 3 if z % 2 else z + 3) % 8, xh, y, core)),
            pairs(lambda z, xh, y, core: ((z + 3 if z % 2 else z - 3) % 8, xh, y, core)),
        ],
    ]


def summed(total, stage):
    for part in [lax.ppermute(total, "space", pairs) for pairs in stage]:
        total = total + part
    return total


def reduced(total, n, z_odd, gate, last_gate):
    todo = stages(n)
    if n != 128:
        total = gate(summed(total, todo[0]))
        for stage in todo[1:]:
            total = summed(total, stage)
        return last_gate(total)
    odd = z_odd == 1
    first, second = (lax.ppermute(total, "space", pairs) for pairs in todo[2])
    two = total + jnp.where(odd, first, second)
    three = total + (first + second)
    even_part, odd_part = jnp.where(odd, two, three), jnp.where(odd, three, two)
    plus = lax.ppermute(even_part, "space", todo[3][0])
    minus = lax.ppermute(odd_part, "space", todo[3][1])
    total = gate(three + (plus + minus))
    return summed(last_gate(summed(total, todo[0])), todo[1])


def per_device(pressure_now, pressure_old, auxiliary_now, auxiliary_old, velocity, epsilon_field, delta_field,
               active_blocks, source_cells, receiver_cells, wavelet):
    blocks = lax.axis_size("space")
    at = lax.axis_index("space").astype(jnp.int32).reshape(1)
    side = lax.axis_index("shot").astype(jnp.int32).reshape(1)
    fields = (2, ROWS, CZ)
    p_now, p_old, q_now, q_old = (a.reshape(fields) for a in (pressure_now, pressure_old, auxiliary_now, auxiliary_old))
    half = (ROWS // 2, CZ)
    speed, eps, delta = (a.reshape(half) for a in (velocity, epsilon_field, delta_field))
    field = shape(*fields)
    active = active_blocks.reshape(2)
    ints = [pltpu.SMEM((1,), jnp.int32), pltpu.SMEM((2,), jnp.int32), pltpu.SMEM((2,), jnp.int32)]

    own, p, odd, live, z_odd = call(
        begin_kernel, (at, side, active, source_cells, speed, eps, delta, p_now),
        (shape(3, *half), field, shape(8, CZ, dtype=jnp.int32), shape(16, CZ),
         shape(2, 8, receiver_cells.shape[1], dtype=jnp.int32)),
        10**6, "begin", far=range(8), scratch=ints + [pltpu.SemaphoreType.DMA((7,))])

    def on_chip(values):
        return lax.ppermute(values, "space", even_pairs(blocks))

    def off_chip(values):
        return lax.ppermute(values, "space", odd_pairs(blocks))

    other = lax.ppermute(own, "shot", [(0, 1), (1, 0)])
    got, pair = off_chip(p), on_chip(p)
    base_p, base_q, q, hor, ver = call(
        ready_kernel, (at, active, source_cells, wavelet, p, p_old, q_now, q_old), (field,) * 5, 10**8, "ready",
        far=(5, 6, 7), scratch=[pltpu.SemaphoreType.DMA((3,))])
    pre_p, pre_q, c, cs, ck, extra = call(
        first_kernel, (side, live, own, other, base_p, base_q, hor, ver), (*(field,) * 5, shape(ROWS + 16, CZ)),
        2 * 10**10, "first")
    part_p, part_q = call(
        chip_kernel, (odd, pair, pre_p, pre_q, cs, ck, extra), (shape(3 * ROWS + 16, CZ), field), 10**6, "chip0")
    coming = off_chip(part_p)
    po, qo = p, q
    p, q = call(first_join_kernel, (odd, got, part_p, part_q, cs, ck), (field, field), 10**6, "join0")
    extra = coming
    traced = shape(2, 8, receiver_cells.shape[1])
    for step in range(1, STEPS):
        got = coming
        pair = on_chip(p)
        now = (at, source_cells, wavelet, p, po, q, qo, c, cs, ck)
        if step == 2:
            pre_p, pre_q, early = call(
                functools.partial(early_kernel, step), (*now, receiver_cells), (field, field, traced), 10**6, "local_early")
        else:
            pre_p, pre_q = call(functools.partial(local_kernel, step), now, (field, field), 10**6, f"local{step}")
        if step == 3:
            total, = call(late_kernel, (at, source_cells, wavelet, receiver_cells, early, p, q), (traced,), 10**8, "late")
        part_p, part_q = call(
            chip_kernel, (odd, pair, pre_p, pre_q, cs, ck), (shape(2 * ROWS, CZ), field), 10**6, f"chip{step}")
        if step == 3:
            break
        coming = off_chip(part_p)
        if step == 1:
            got, coming = lax.optimization_barrier((got, coming))
            extra = got
        before, po, qo = po, p, q
        p, q = call(
            join_kernel, (odd, got, extra, before, part_p, part_q, cs, ck), (field, field), 10**6, f"join{step}")

    local = (got, part_p, part_q)

    def gate(total):
        nonlocal local
        total, local = lax.optimization_barrier((total, local))
        return total

    total = reduced(total, blocks, z_odd, lambda total: total, gate)
    got, part_p, part_q = local
    p, q = call(join_kernel, (odd, got, extra, po, part_p, part_q, cs, ck), (field, field), 2 * 10**10, "join3")
    last = total[:, 4] + total[:, 0] * total[:, 5]
    traces = jnp.stack([total[:, 1], total[:, 2], total[:, 3], last], axis=1)
    return (p.reshape(pressure_now.shape), q.reshape(pressure_now.shape), traces)


def solution(mesh):
    grid = P("shot", "space", None, None, None)
    model = P("space", "shot", None, None)
    return jax.shard_map(
        per_device,
        mesh=mesh,
        in_specs=(grid, grid, grid, grid, model, model, model, P("shot", "space"), P("shot"), P("shot", None), P("shot", None)),
        out_specs=(grid, grid, P("shot", None, None)),
        check_vma=False,
    )
```

```python
import functools

import jax
import jax.numpy as jnp
from jax import lax
from jax.experimental import pallas as pl
from jax.experimental.pallas import tpu as pltpu
from jax.sharding import PartitionSpec as P

STEPS = 4
CX, CY, CZ = 4, 128, 128
ROWS = CX * CY
CELLS = ROWS * CZ

taps = (-205.0 / 72.0, 8.0 / 5.0, -1.0 / 5.0, 8.0 / 315.0, -1.0 / 560.0)
step_ratio = 0.08

VMEM = pl.BlockSpec(memory_space=pltpu.VMEM)
SMEM = pl.BlockSpec(memory_space=pltpu.SMEM)
FAR = pl.BlockSpec(memory_space=pltpu.HBM)
EXACT = lax.Precision.HIGHEST


def shape(*dims, dtype=jnp.float32):
    return jax.ShapeDtypeStruct(dims, dtype)


def call(kernel, ins, outs, flops, name, far=(), scratch=()):
    moved = 4 * sum(int(jnp.size(a)) for a in ins) + 4 * sum(o.size for o in outs)
    ins = [pltpu.with_memory_space_constraint(a, pltpu.HBM) if n in far else a for n, a in enumerate(ins)]
    specs = [FAR if n in far else SMEM if a.size <= 64 else VMEM for n, a in enumerate(ins)]
    return pl.pallas_call(
        kernel,
        out_shape=tuple(outs),
        in_specs=specs,
        out_specs=tuple(VMEM for _ in outs),
        scratch_shapes=scratch,
        compiler_params=pltpu.CompilerParams(vmem_limit_bytes=16 << 20),
        cost_estimate=pl.CostEstimate(flops=flops, bytes_accessed=moved, transcendentals=0),
        name=name,
    )(*ins)


def live_of(at_ref, active_ref, source_ref, s):
    here = source_ref[s] // CELLS == at_ref[0]
    return jnp.where(here | (active_ref[s] == 1), 1.0, 0.0)


def row(x):
    return pl.ds(x * CY, CY)


def begin_kernel(at_far, side_far, active_far, source_far, v_far, e_far, d_far, p_far,
                 own_ref, p0_ref, odd_ref, live_ref, z_odd_ref, at_ref, active_ref, source_ref, sems):
    pairs = (
        (v_far, own_ref.at[0]), (e_far, own_ref.at[1]), (d_far, own_ref.at[2]),
        (at_far, at_ref), (active_far, active_ref), (source_far, source_ref), (p_far, p0_ref))
    copies = [pltpu.make_async_copy(src, dst, sems.at[n]) for n, (src, dst) in enumerate(pairs)]
    for copy in copies:
        copy.start()
    for copy in copies[:3]:
        copy.wait()
    courant = (own_ref[0] * step_ratio) * (own_ref[0] * step_ratio)
    coupling = jnp.sqrt(1.0 + 2.0 * own_ref[2])
    own_ref[0] = courant
    own_ref[1] = courant * (1.0 + 2.0 * own_ref[1])
    own_ref[2] = courant * coupling
    for copy in copies[3:]:
        copy.wait()
    for s in range(2):
        live = live_of(at_ref, active_ref, source_ref, s)
        p0_ref[s] = p0_ref[s] * live
        live_ref[pl.ds(8 * s, 8), :] = jnp.full((8, CZ), live, jnp.float32)
    odd_ref[...] = jnp.full(odd_ref.shape, at_ref[0] & 1, jnp.int32)
    z_odd_ref[...] = jnp.full(z_odd_ref.shape, (at_ref[0] // 16) & 1, jnp.int32)


def band():
    apart = jnp.abs(lax.broadcasted_iota(jnp.int32, (CZ, CZ), 0) - lax.broadcasted_iota(jnp.int32, (CZ, CZ), 1))
    out = jnp.zeros((CZ, CZ), jnp.float32)
    for k in range(5):
        out = jnp.where(apart == k, taps[k], out)
    return out


def second_diffs(s, x, p, q, mat):
    hor = jnp.dot(mat, p[s, row(x), :], precision=EXACT, preferred_element_type=jnp.float32)
    for other in range(CX):
        hor = hor + taps[abs(other - x)] * p[s, row(other), :]
    ver = jnp.dot(q[s, row(x), :], mat, precision=EXACT, preferred_element_type=jnp.float32)
    return hor, ver


def add_source(s, step, at_ref, source_ref, wavelet_ref, *refs):
    cell = source_ref[s] % CELLS
    gain = jnp.where(source_ref[s] // CELLS == at_ref[0], wavelet_ref[s, step], 0.0)
    lane = lax.broadcasted_iota(jnp.int32, (1, CZ), 1)
    add = jnp.where(lane == cell % CZ, gain, 0.0)
    line = pl.ds(cell // CZ, 1)
    for ref in refs:
        ref[s, line, :] = ref[s, line, :] + add


def ready_kernel(at_ref, active_ref, source_ref, wavelet_ref, p0, po_far, q_far, qo_far,
                 base_p, base_q, q, hor_ref, ver_ref, sems):
    copies = [
        pltpu.make_async_copy(src, dst, sems.at[n])
        for n, (src, dst) in enumerate(((q_far, q), (po_far, base_p), (qo_far, base_q)))
    ]
    for copy in copies:
        copy.start()
    mat = band()
    for copy in copies:
        copy.wait()
    for s in range(2):
        live = live_of(at_ref, active_ref, source_ref, s)
        q[s] = q[s] * live
        base_p[s] = 2.0 * p0[s] - base_p[s] * live
        base_q[s] = 2.0 * q[s] - base_q[s] * live
        for x in range(CX):
            hor_ref[s, row(x), :], ver_ref[s, row(x), :] = second_diffs(s, x, p0, q, mat)
        add_source(s, 0, at_ref, source_ref, wavelet_ref, base_p, base_q)


def side_diff(x, rows, upper):
    above = below = taps[4] * rows[x]
    for k in range(1, 4):
        if x + k < CX:
            below = below + taps[4 - k] * rows[x + k]
        if x - k >= 0:
            above = above + taps[4 - k] * rows[x - k]
    return jnp.where(upper, above, below)


def tile_at(x, tile):
    return pl.ds(x * CY + tile * 8, 8)


def flat_at(s, x, tile):
    return pl.ds(s * ROWS + x * CY + tile * 8, 8)


def first_kernel(side_ref, live_ref, own, other, base_p, base_q, hor_ref, ver_ref, pre_p, pre_q, c_ref, cs_ref, ck_ref, extra_ref):
    extra_ref[pl.ds(ROWS, 16), :] = live_ref[...]

    def work(first, second):
        for tile in range(CY // 8):
            model = []
            for x in range(CX):
                half = (first, second)[x // 2]
                at = tile_at(x % 2, tile)
                model.append((half[0, at, :], half[1, at, :], half[2, at, :]))
                extra_ref[tile_at(x, tile), :] = model[x][1]
            for s in range(2):
                live = live_ref[pl.ds(8 * s, 8), :]
                for x in range(CX):
                    at = tile_at(x, tile)
                    c, cs, ck = (m * live for m in model[x])
                    c_ref[s, at, :], cs_ref[s, at, :], ck_ref[s, at, :] = c, cs, ck
                    hor, ver = hor_ref[s, at, :], ver_ref[s, at, :]
                    pre_p[s, at, :] = base_p[s, at, :] + (cs * hor + ck * ver)
                    pre_q[s, at, :] = base_q[s, at, :] + (ck * hor + c * ver)

    @pl.when(side_ref[0] == 0)
    def _():
        work(own, other)

    @pl.when(side_ref[0] == 1)
    def _():
        work(other, own)


def local_part(step, at_ref, source_ref, wavelet_ref, p, po, q, qo, c_ref, cs_ref, ck_ref, pre_p, pre_q):
    mat = band()
    for s in range(2):
        for x in range(CX):
            here = row(x)
            hor, ver = second_diffs(s, x, p, q, mat)
            pre_p[s, here, :] = 2.0 * p[s, here, :] - po[s, here, :] + (cs_ref[s, here, :] * hor + ck_ref[s, here, :] * ver)
            pre_q[s, here, :] = 2.0 * q[s, here, :] - qo[s, here, :] + (ck_ref[s, here, :] * hor + c_ref[s, here, :] * ver)
        add_source(s, step, at_ref, source_ref, wavelet_ref, pre_p, pre_q)


def chip_kernel(odd_ref, even_pair, pre_p, pre_q, cs_ref, ck_ref, *rest):
    extra, (out_p, out_q) = rest[:-2], rest[-2:]
    upper = odd_ref[...] == 0
    for ref in extra:
        out_p[pl.ds(2 * ROWS, ROWS + 16), :] = ref[...]
    for s in range(2):
        for tile in range(CY // 8):
            rows = [even_pair[s, tile_at(x, tile), :] for x in range(CX)]
            for x in range(CX):
                at = tile_at(x, tile)
                hor = side_diff(x, rows, upper)
                out_p[flat_at(s, x, tile), :] = pre_p[s, at, :] + cs_ref[s, at, :] * hor
                out_q[s, at, :] = pre_q[s, at, :] + ck_ref[s, at, :] * hor


def join(odd_ref, other_rows, part_p, part_q, cs_ref, ck_ref, p, q):
    upper = odd_ref[...] == 1
    for s in range(2):
        for tile in range(CY // 8):
            rows = other_rows(s, tile)
            for x in range(CX):
                at = tile_at(x, tile)
                hor = side_diff(x, rows, upper)
                p[s, at, :] = part_p[flat_at(s, x, tile), :] + cs_ref[s, at, :] * hor
                q[s, at, :] = part_q[s, at, :] + ck_ref[s, at, :] * hor


def first_join_kernel(odd_ref, got, part_p, part_q, cs_ref, ck_ref, p, q):
    def other_rows(s, tile):
        return [got[s, tile_at(x, tile), :] for x in range(CX)]

    join(odd_ref, other_rows, part_p, part_q, cs_ref, ck_ref, p, q)


def join_kernel(odd_ref, got, extra, before, part_p, part_q, cs_ref, ck_ref, p, q):
    upper = odd_ref[...] == 0

    def other_rows(s, tile):
        mine = [before[s, tile_at(x, tile), :] for x in range(CX)]
        live = extra[pl.ds(3 * ROWS + 8 * s, 8), :]
        out = []
        for x in range(CX):
            stretch = extra[pl.ds(2 * ROWS + x * CY + tile * 8, 8), :] * live
            out.append(got[flat_at(s, x, tile), :] + stretch * side_diff(x, mine, upper))
        return out

    join(odd_ref, other_rows, part_p, part_q, cs_ref, ck_ref, p, q)


def samples(field, s, pick_z, pick_y):
    out = []
    for x in range(CX):
        rest, spread = field[s, row(x), :], None
        for _ in range(3):
            part = rest.astype(jnp.bfloat16)
            rest = rest - part.astype(jnp.float32)
            picked = jnp.dot(part, pick_z, preferred_element_type=jnp.float32)
            spread = picked if spread is None else spread + picked
        out.append(jnp.sum(jnp.where(pick_y, spread, 0.0), axis=0, keepdims=True))
    return out


def picks(cells_ref, s):
    cells = cells_ref[pl.ds(s, 1), :]
    n = cells.shape[1]
    inside = cells % CELLS
    pick_z = jnp.where(lax.broadcasted_iota(jnp.int32, (CZ, n), 0) == inside % CZ, 1.0, 0.0).astype(jnp.bfloat16)
    pick_y = lax.broadcasted_iota(jnp.int32, (CY, n), 0) == (inside // CZ) % CY
    return cells // CELLS, inside // (CY * CZ), pick_z, pick_y


def own_sample(values, block, x_at, me):
    out = jnp.zeros(block.shape, jnp.float32)
    for x in range(CX):
        out = jnp.where((x_at == x) & (block == me), values[x], out)
    return out


def local_kernel(step, at_ref, source_ref, wavelet_ref, p, po, q, qo, c_ref, cs_ref, ck_ref, pre_p, pre_q):
    local_part(step, at_ref, source_ref, wavelet_ref, p, po, q, qo, c_ref, cs_ref, ck_ref, pre_p, pre_q)


def early_kernel(at_ref, source_ref, wavelet_ref, p, po, q, qo, c_ref, cs_ref, ck_ref, cells_ref, pre_p, pre_q, out_ref):
    local_part(1, at_ref, source_ref, wavelet_ref, p, po, q, qo, c_ref, cs_ref, ck_ref, pre_p, pre_q)
    out_ref[...] = jnp.zeros(out_ref.shape, jnp.float32)
    for s in range(2):
        block, x_at, pick_z, pick_y = picks(cells_ref, s)
        for n, field in ((0, cs_ref), (1, p), (7, ck_ref)):
            out_ref[s, pl.ds(n, 1), :] = own_sample(samples(field, s, pick_z, pick_y), block, x_at, at_ref[0])


def middle_kernel(at_ref, source_ref, wavelet_ref, p, po, q, qo, c_ref, cs_ref, ck_ref, cells_ref, early_ref,
                  pre_p, pre_q, out_ref):
    local_part(2, at_ref, source_ref, wavelet_ref, p, po, q, qo, c_ref, cs_ref, ck_ref, pre_p, pre_q)
    out_ref[...] = early_ref[...]
    for s in range(2):
        block, x_at, pick_z, pick_y = picks(cells_ref, s)
        out_ref[s, pl.ds(2, 1), :] = own_sample(samples(p, s, pick_z, pick_y), block, x_at, at_ref[0])


def weights(apart):
    out = jnp.zeros(apart.shape, jnp.float32)
    for k in range(5):
        out = jnp.where(apart == k, taps[k], out)
    return out


def late_kernel(at_ref, source_ref, wavelet_ref, cells_ref, early_ref, p, q, out_ref):
    me = at_ref[0]
    out_ref[...] = early_ref[...]
    for s in range(2):
        block, x_at, pick_z, pick_y = picks(cells_ref, s)
        cells = cells_ref[pl.ds(s, 1), :]
        n = cells.shape[1]
        band_z = weights(jnp.abs(lax.broadcasted_iota(jnp.int32, (CZ, n), 0) - cells % CZ))
        band_y = weights(jnp.abs(lax.broadcasted_iota(jnp.int32, (CY, n), 0) - (cells // CZ) % CY))
        here = jnp.zeros(block.shape, jnp.float32)
        hor, ver, across = here, here, here
        for x in range(CX):
            rest, spread = p[s, row(x), :], None
            for _ in range(3):
                part = rest.astype(jnp.bfloat16)
                rest = rest - part.astype(jnp.float32)
                picked = jnp.dot(part, pick_z, preferred_element_type=jnp.float32)
                spread = picked if spread is None else spread + picked
            value = jnp.sum(jnp.where(pick_y, spread, 0.0), axis=0, keepdims=True)
            along_y = jnp.sum(band_y * spread, axis=0, keepdims=True)
            along_z = jnp.dot(q[s, row(x), :], band_z, precision=EXACT, preferred_element_type=jnp.float32)
            along_z = jnp.sum(jnp.where(pick_y, along_z, 0.0), axis=0, keepdims=True)
            here = jnp.where(x_at == x, value, here)
            hor = hor + weights(jnp.abs(x_at - x)) * value + jnp.where(x_at == x, along_y, 0.0)
            ver = jnp.where(x_at == x, along_z, ver)
            apart = jnp.where(block == me + 1, x_at + 4 - x, jnp.where(block == me - 1, 4 + x - x_at, 9))
            for k in range(1, 5):
                across = across + jnp.where(apart == k, taps[k] * value, 0.0)
        mine = jnp.where(block == me, 1.0, 0.0)
        here = mine * here
        gain = mine * jnp.where(cells == source_ref[s], wavelet_ref[s, STEPS - 1], 0.0)
        early = [early_ref[s, pl.ds(k, 1), :] for k in (0, 2, 7)]
        out_ref[s, pl.ds(3, 1), :] = here
        out_ref[s, pl.ds(4, 1), :] = 2.0 * here - early[1] + (early[0] * hor + early[2] * ver) + gain
        out_ref[s, pl.ds(5, 1), :] = across


def even_pairs(n):
    return [(i, i ^ 1) for i in range(n)]


def odd_pairs(n):
    up = [(i, i + 1) for i in range(1, n - 1, 2)]
    return up + [(b, a) for a, b in up]


def stages(n):
    if n != 128:
        bit, out = 1, []
        while bit < n:
            out.append([[(i, i ^ bit) for i in range(n)]])
            bit *= 2
        return out

    def device(z, xh, y, core):
        return ((z * 2 + xh) * 4 + y) * 2 + core

    def pairs(move):
        return [
            (device(z, xh, y, core), device(*move(z, xh, y, core)))
            for z in range(8) for xh in range(2) for y in range(4) for core in range(2)
        ]

    return [
        [pairs(lambda z, xh, y, core, k=k: (z, xh, y ^ k, core)) for k in (1, 3, 2)],
        [
            pairs(lambda z, xh, y, core: (z, xh, y, 1 - core)),
            pairs(lambda z, xh, y, core: (z, 1 - xh, y, core)),
            pairs(lambda z, xh, y, core: (z, 1 - xh, y, 1 - core)),
        ],
        [
            pairs(lambda z, xh, y, core: (z ^ 1, xh, y, core)),
            pairs(lambda z, xh, y, core: ((z + 1 if z % 2 else z - 1) % 8, xh, y, core)),
        ],
        [
            pairs(lambda z, xh, y, core: ((z - 3 if z % 2 else z + 3) % 8, xh, y, core)),
            pairs(lambda z, xh, y, core: ((z + 3 if z % 2 else z - 3) % 8, xh, y, core)),
        ],
    ]


def summed(total, stage):
    for part in [lax.ppermute(total, "space", pairs) for pairs in stage]:
        total = total + part
    return total


def reduced(total, n, z_odd, gate, last_gate):
    todo = stages(n)
    if n != 128:
        total = gate(summed(total, todo[0]))
        for stage in todo[1:]:
            total = summed(total, stage)
        return last_gate(total)
    odd = z_odd == 1
    first, second = (lax.ppermute(total, "space", pairs) for pairs in todo[2])
    two = total + jnp.where(odd, first, second)
    three = total + (first + second)
    even_part, odd_part = jnp.where(odd, two, three), jnp.where(odd, three, two)
    plus = lax.ppermute(even_part, "space", todo[3][0])
    minus = lax.ppermute(odd_part, "space", todo[3][1])
    total = gate(three + (plus + minus))
    return summed(last_gate(summed(total, todo[0])), todo[1])


def per_device(pressure_now, pressure_old, auxiliary_now, auxiliary_old, velocity, epsilon_field, delta_field,
               active_blocks, source_cells, receiver_cells, wavelet):
    blocks = lax.axis_size("space")
    at = lax.axis_index("space").astype(jnp.int32).reshape(1)
    side = lax.axis_index("shot").astype(jnp.int32).reshape(1)
    fields = (2, ROWS, CZ)
    p_now, p_old, q_now, q_old = (a.reshape(fields) for a in (pressure_now, pressure_old, auxiliary_now, auxiliary_old))
    half = (ROWS // 2, CZ)
    speed, eps, delta = (a.reshape(half) for a in (velocity, epsilon_field, delta_field))
    field = shape(*fields)
    active = active_blocks.reshape(2)
    ints = [pltpu.SMEM((1,), jnp.int32), pltpu.SMEM((2,), jnp.int32), pltpu.SMEM((2,), jnp.int32)]

    own, p, odd, live, z_odd = call(
        begin_kernel, (at, side, active, source_cells, speed, eps, delta, p_now),
        (shape(3, *half), field, shape(8, CZ, dtype=jnp.int32), shape(16, CZ),
         shape(2, 8, receiver_cells.shape[1], dtype=jnp.int32)),
        10**6, "begin", far=range(8), scratch=ints + [pltpu.SemaphoreType.DMA((7,))])

    def on_chip(values):
        return lax.ppermute(values, "space", even_pairs(blocks))

    def off_chip(values):
        return lax.ppermute(values, "space", odd_pairs(blocks))

    other = lax.ppermute(own, "shot", [(0, 1), (1, 0)])
    got, pair = off_chip(p), on_chip(p)
    base_p, base_q, q, hor, ver = call(
        ready_kernel, (at, active, source_cells, wavelet, p, p_old, q_now, q_old), (field,) * 5, 10**8, "ready",
        far=(5, 6, 7), scratch=[pltpu.SemaphoreType.DMA((3,))])
    pre_p, pre_q, c, cs, ck, extra = call(
        first_kernel, (side, live, own, other, base_p, base_q, hor, ver), (*(field,) * 5, shape(ROWS + 16, CZ)),
        2 * 10**10, "first")
    part_p, part_q = call(
        chip_kernel, (odd, pair, pre_p, pre_q, cs, ck, extra), (shape(3 * ROWS + 16, CZ), field), 10**6, "chip0")
    coming = off_chip(part_p)
    po, qo = p, q
    p, q = call(first_join_kernel, (odd, got, part_p, part_q, cs, ck), (field, field), 10**6, "join0")
    extra = coming
    traced = shape(2, 8, receiver_cells.shape[1])
    for step in range(1, STEPS):
        got = coming
        pair = on_chip(p)
        now = (at, source_cells, wavelet, p, po, q, qo, c, cs, ck)
        if step == 1:
            pre_p, pre_q, early = call(
                early_kernel, (*now, receiver_cells), (field, field, traced), 2*10**10, "local1")
        elif step == 2:
            pre_p, pre_q, early = call(
                middle_kernel, (*now, receiver_cells, early), (field, field, traced), 10**6, "local2")
        else:
            pre_p, pre_q = call(functools.partial(local_kernel, step), now, (field, field), 10**6, "local3")
        if step == 3:
            total, = call(late_kernel, (at, source_cells, wavelet, receiver_cells, early, p, q), (traced,), 10**8, "late")
        part_p, part_q = call(
            chip_kernel, (odd, pair, pre_p, pre_q, cs, ck), (shape(2 * ROWS, CZ), field), 10**6, f"chip{step}")
        if step == 3:
            break
        coming = off_chip(part_p)
        if step == 1:
            got, coming = lax.optimization_barrier((got, coming))
            extra = got
        before, po, qo = po, p, q
        p, q = call(
            join_kernel, (odd, got, extra, before, part_p, part_q, cs, ck), (field, field), 10**6, f"join{step}")

    local = (got, part_p, part_q)

    def gate(total):
        nonlocal local
        total, local = lax.optimization_barrier((total, local))
        return total

    total = reduced(total, blocks, z_odd, lambda total: total, gate)
    got, part_p, part_q = local
    p, q = call(join_kernel, (odd, got, extra, po, part_p, part_q, cs, ck), (field, field), 2 * 10**10, "join3")
    last = total[:, 4] + total[:, 0] * total[:, 5]
    traces = jnp.stack([total[:, 1], total[:, 2], total[:, 3], last], axis=1)
    return (p.reshape(pressure_now.shape), q.reshape(pressure_now.shape), traces)


def solution(mesh):
    grid = P("shot", "space", None, None, None)
    model = P("space", "shot", None, None)
    return jax.shard_map(
        per_device,
        mesh=mesh,
        in_specs=(grid, grid, grid, grid, model, model, model, P("shot", "space"), P("shot"), P("shot", None), P("shot", None)),
        out_specs=(grid, grid, P("shot", None, None)),
        check_vma=False,
    )
```

```python
import functools

import jax
import jax.numpy as jnp
from jax import lax
from jax.experimental import pallas as pl
from jax.experimental.pallas import tpu as pltpu
from jax.sharding import PartitionSpec as P

STEPS = 4
CX, CY, CZ = 4, 128, 128
ROWS = CX * CY
CELLS = ROWS * CZ

taps = (-205.0 / 72.0, 8.0 / 5.0, -1.0 / 5.0, 8.0 / 315.0, -1.0 / 560.0)
step_ratio = 0.08

VMEM = pl.BlockSpec(memory_space=pltpu.VMEM)
SMEM = pl.BlockSpec(memory_space=pltpu.SMEM)
FAR = pl.BlockSpec(memory_space=pltpu.HBM)
EXACT = lax.Precision.HIGHEST


def shape(*dims, dtype=jnp.float32):
    return jax.ShapeDtypeStruct(dims, dtype)


def call(kernel, ins, outs, flops, name, far=(), scratch=()):
    moved = 4 * sum(int(jnp.size(a)) for a in ins) + 4 * sum(o.size for o in outs)
    ins = [pltpu.with_memory_space_constraint(a, pltpu.HBM) if n in far else a for n, a in enumerate(ins)]
    specs = [FAR if n in far else SMEM if a.size <= 64 else VMEM for n, a in enumerate(ins)]
    return pl.pallas_call(
        kernel,
        out_shape=tuple(outs),
        in_specs=specs,
        out_specs=tuple(VMEM for _ in outs),
        scratch_shapes=scratch,
        compiler_params=pltpu.CompilerParams(vmem_limit_bytes=16 << 20),
        cost_estimate=pl.CostEstimate(flops=flops, bytes_accessed=moved, transcendentals=0),
        name=name,
    )(*ins)


def live_of(at_ref, active_ref, source_ref, s):
    here = source_ref[s] // CELLS == at_ref[0]
    return jnp.where(here | (active_ref[s] == 1), 1.0, 0.0)


def row(x):
    return pl.ds(x * CY, CY)


def begin_kernel(at_far, side_far, active_far, source_far, v_far, e_far, d_far, p_far,
                 own_ref, p0_ref, odd_ref, live_ref, z_odd_ref, at_ref, active_ref, source_ref, sems):
    pairs = (
        (v_far, own_ref.at[0]), (e_far, own_ref.at[1]), (d_far, own_ref.at[2]),
        (at_far, at_ref), (active_far, active_ref), (source_far, source_ref), (p_far, p0_ref))
    copies = [pltpu.make_async_copy(src, dst, sems.at[n]) for n, (src, dst) in enumerate(pairs)]
    for copy in copies:
        copy.start()
    for copy in copies[:3]:
        copy.wait()
    courant = (own_ref[0] * step_ratio) * (own_ref[0] * step_ratio)
    coupling = jnp.sqrt(1.0 + 2.0 * own_ref[2])
    own_ref[0] = courant
    own_ref[1] = courant * (1.0 + 2.0 * own_ref[1])
    own_ref[2] = courant * coupling
    for copy in copies[3:]:
        copy.wait()
    for s in range(2):
        live = live_of(at_ref, active_ref, source_ref, s)
        p0_ref[s] = p0_ref[s] * live
        live_ref[pl.ds(8 * s, 8), :] = jnp.full((8, CZ), live, jnp.float32)
    odd_ref[...] = jnp.full(odd_ref.shape, at_ref[0] & 1, jnp.int32)
    z_odd_ref[...] = jnp.full(z_odd_ref.shape, (at_ref[0] // 16) & 1, jnp.int32)


def band():
    apart = jnp.abs(lax.broadcasted_iota(jnp.int32, (CZ, CZ), 0) - lax.broadcasted_iota(jnp.int32, (CZ, CZ), 1))
    out = jnp.zeros((CZ, CZ), jnp.float32)
    for k in range(5):
        out = jnp.where(apart == k, taps[k], out)
    return out


def second_diffs(s, x, p, q, mat):
    hor = jnp.dot(mat, p[s, row(x), :], precision=EXACT, preferred_element_type=jnp.float32)
    for other in range(CX):
        hor = hor + taps[abs(other - x)] * p[s, row(other), :]
    ver = jnp.dot(q[s, row(x), :], mat, precision=EXACT, preferred_element_type=jnp.float32)
    return hor, ver


def add_source(s, step, at_ref, source_ref, wavelet_ref, *refs):
    cell = source_ref[s] % CELLS
    gain = jnp.where(source_ref[s] // CELLS == at_ref[0], wavelet_ref[s, step], 0.0)
    lane = lax.broadcasted_iota(jnp.int32, (1, CZ), 1)
    add = jnp.where(lane == cell % CZ, gain, 0.0)
    line = pl.ds(cell // CZ, 1)
    for ref in refs:
        ref[s, line, :] = ref[s, line, :] + add


def ready_kernel(at_ref, active_ref, source_ref, wavelet_ref, p0, po_far, q_far, qo_far,
                 base_p, base_q, q, hor_ref, ver_ref, sems):
    copies = [
        pltpu.make_async_copy(src, dst, sems.at[n])
        for n, (src, dst) in enumerate(((q_far, q), (po_far, base_p), (qo_far, base_q)))
    ]
    for copy in copies:
        copy.start()
    mat = band()
    for copy in copies:
        copy.wait()
    for s in range(2):
        live = live_of(at_ref, active_ref, source_ref, s)
        q[s] = q[s] * live
        base_p[s] = 2.0 * p0[s] - base_p[s] * live
        base_q[s] = 2.0 * q[s] - base_q[s] * live
        for x in range(CX):
            hor_ref[s, row(x), :], ver_ref[s, row(x), :] = second_diffs(s, x, p0, q, mat)
        add_source(s, 0, at_ref, source_ref, wavelet_ref, base_p, base_q)


def side_diff(x, rows, upper):
    above = below = taps[4] * rows[x]
    for k in range(1, 4):
        if x + k < CX:
            below = below + taps[4 - k] * rows[x + k]
        if x - k >= 0:
            above = above + taps[4 - k] * rows[x - k]
    return jnp.where(upper, above, below)


def tile_at(x, tile):
    return pl.ds(x * CY + tile * 8, 8)


def flat_at(s, x, tile):
    return pl.ds(s * ROWS + x * CY + tile * 8, 8)


def first_kernel(side_ref, live_ref, own, other, base_p, base_q, hor_ref, ver_ref, pre_p, pre_q, c_ref, cs_ref, ck_ref, extra_ref):
    extra_ref[pl.ds(ROWS, 16), :] = live_ref[...]

    def work(first, second):
        for tile in range(CY // 8):
            model = []
            for x in range(CX):
                half = (first, second)[x // 2]
                at = tile_at(x % 2, tile)
                model.append((half[0, at, :], half[1, at, :], half[2, at, :]))
                extra_ref[tile_at(x, tile), :] = model[x][1]
            for s in range(2):
                live = live_ref[pl.ds(8 * s, 8), :]
                for x in range(CX):
                    at = tile_at(x, tile)
                    c, cs, ck = (m * live for m in model[x])
                    c_ref[s, at, :], cs_ref[s, at, :], ck_ref[s, at, :] = c, cs, ck
                    hor, ver = hor_ref[s, at, :], ver_ref[s, at, :]
                    pre_p[s, at, :] = base_p[s, at, :] + (cs * hor + ck * ver)
                    pre_q[s, at, :] = base_q[s, at, :] + (ck * hor + c * ver)

    @pl.when(side_ref[0] == 0)
    def _():
        work(own, other)

    @pl.when(side_ref[0] == 1)
    def _():
        work(other, own)


def local_part(step, at_ref, source_ref, wavelet_ref, p, po, q, qo, c_ref, cs_ref, ck_ref, pre_p, pre_q):
    mat = band()
    for s in range(2):
        for x in range(CX):
            here = row(x)
            hor, ver = second_diffs(s, x, p, q, mat)
            pre_p[s, here, :] = 2.0 * p[s, here, :] - po[s, here, :] + (cs_ref[s, here, :] * hor + ck_ref[s, here, :] * ver)
            pre_q[s, here, :] = 2.0 * q[s, here, :] - qo[s, here, :] + (ck_ref[s, here, :] * hor + c_ref[s, here, :] * ver)
        add_source(s, step, at_ref, source_ref, wavelet_ref, pre_p, pre_q)


def chip_kernel(odd_ref, even_pair, pre_p, pre_q, cs_ref, ck_ref, *rest):
    extra, (out_p, out_q) = rest[:-2], rest[-2:]
    upper = odd_ref[...] == 0
    for ref in extra:
        out_p[pl.ds(2 * ROWS, ROWS + 16), :] = ref[...]
    for s in range(2):
        for tile in range(CY // 8):
            rows = [even_pair[s, tile_at(x, tile), :] for x in range(CX)]
            for x in range(CX):
                at = tile_at(x, tile)
                hor = side_diff(x, rows, upper)
                out_p[flat_at(s, x, tile), :] = pre_p[s, at, :] + cs_ref[s, at, :] * hor
                out_q[s, at, :] = pre_q[s, at, :] + ck_ref[s, at, :] * hor


def join(odd_ref, other_rows, part_p, part_q, cs_ref, ck_ref, p, q):
    upper = odd_ref[...] == 1
    for s in range(2):
        for tile in range(CY // 8):
            rows = other_rows(s, tile)
            for x in range(CX):
                at = tile_at(x, tile)
                hor = side_diff(x, rows, upper)
                p[s, at, :] = part_p[flat_at(s, x, tile), :] + cs_ref[s, at, :] * hor
                q[s, at, :] = part_q[s, at, :] + ck_ref[s, at, :] * hor


def first_join_kernel(odd_ref, got, part_p, part_q, cs_ref, ck_ref, p, q):
    def other_rows(s, tile):
        return [got[s, tile_at(x, tile), :] for x in range(CX)]

    join(odd_ref, other_rows, part_p, part_q, cs_ref, ck_ref, p, q)


def join_kernel(odd_ref, got, extra, before, part_p, part_q, cs_ref, ck_ref, p, q):
    upper = odd_ref[...] == 0

    def other_rows(s, tile):
        mine = [before[s, tile_at(x, tile), :] for x in range(CX)]
        live = extra[pl.ds(3 * ROWS + 8 * s, 8), :]
        out = []
        for x in range(CX):
            stretch = extra[pl.ds(2 * ROWS + x * CY + tile * 8, 8), :] * live
            out.append(got[flat_at(s, x, tile), :] + stretch * side_diff(x, mine, upper))
        return out

    join(odd_ref, other_rows, part_p, part_q, cs_ref, ck_ref, p, q)


def samples(field, s, pick_z, pick_y):
    out = []
    for x in range(CX):
        rest, spread = field[s, row(x), :], None
        for _ in range(3):
            part = rest.astype(jnp.bfloat16)
            rest = rest - part.astype(jnp.float32)
            picked = jnp.dot(part, pick_z, preferred_element_type=jnp.float32)
            spread = picked if spread is None else spread + picked
        out.append(jnp.sum(jnp.where(pick_y, spread, 0.0), axis=0, keepdims=True))
    return out


def picks(cells_ref, s):
    cells = cells_ref[pl.ds(s, 1), :]
    n = cells.shape[1]
    inside = cells % CELLS
    pick_z = jnp.where(lax.broadcasted_iota(jnp.int32, (CZ, n), 0) == inside % CZ, 1.0, 0.0).astype(jnp.bfloat16)
    pick_y = lax.broadcasted_iota(jnp.int32, (CY, n), 0) == (inside // CZ) % CY
    return cells // CELLS, inside // (CY * CZ), pick_z, pick_y


def own_sample(values, block, x_at, me):
    out = jnp.zeros(block.shape, jnp.float32)
    for x in range(CX):
        out = jnp.where((x_at == x) & (block == me), values[x], out)
    return out


def local_kernel(step, at_ref, source_ref, wavelet_ref, p, po, q, qo, c_ref, cs_ref, ck_ref, pre_p, pre_q):
    local_part(step, at_ref, source_ref, wavelet_ref, p, po, q, qo, c_ref, cs_ref, ck_ref, pre_p, pre_q)


def early_kernel(at_ref, cells_ref, p, cs_ref, ck_ref, out_ref):
    out_ref[...] = jnp.zeros(out_ref.shape, jnp.float32)
    for s in range(2):
        block, x_at, pick_z, pick_y = picks(cells_ref, s)
        for n, field in ((0, cs_ref), (1, p), (7, ck_ref)):
            out_ref[s, pl.ds(n, 1), :] = own_sample(samples(field, s, pick_z, pick_y), block, x_at, at_ref[0])


def middle_kernel(at_ref, source_ref, wavelet_ref, p, po, q, qo, c_ref, cs_ref, ck_ref, cells_ref, early_ref,
                  pre_p, pre_q, out_ref):
    local_part(2, at_ref, source_ref, wavelet_ref, p, po, q, qo, c_ref, cs_ref, ck_ref, pre_p, pre_q)
    out_ref[...] = early_ref[...]
    for s in range(2):
        block, x_at, pick_z, pick_y = picks(cells_ref, s)
        out_ref[s, pl.ds(2, 1), :] = own_sample(samples(p, s, pick_z, pick_y), block, x_at, at_ref[0])


def weights(apart):
    out = jnp.zeros(apart.shape, jnp.float32)
    for k in range(5):
        out = jnp.where(apart == k, taps[k], out)
    return out


def late_kernel(at_ref, source_ref, wavelet_ref, cells_ref, early_ref, p, q, out_ref):
    me = at_ref[0]
    out_ref[...] = early_ref[...]
    for s in range(2):
        block, x_at, pick_z, pick_y = picks(cells_ref, s)
        cells = cells_ref[pl.ds(s, 1), :]
        n = cells.shape[1]
        band_z = weights(jnp.abs(lax.broadcasted_iota(jnp.int32, (CZ, n), 0) - cells % CZ))
        band_y = weights(jnp.abs(lax.broadcasted_iota(jnp.int32, (CY, n), 0) - (cells // CZ) % CY))
        here = jnp.zeros(block.shape, jnp.float32)
        hor, ver, across = here, here, here
        for x in range(CX):
            rest, spread = p[s, row(x), :], None
            for _ in range(3):
                part = rest.astype(jnp.bfloat16)
                rest = rest - part.astype(jnp.float32)
                picked = jnp.dot(part, pick_z, preferred_element_type=jnp.float32)
                spread = picked if spread is None else spread + picked
            value = jnp.sum(jnp.where(pick_y, spread, 0.0), axis=0, keepdims=True)
            along_y = jnp.sum(band_y * spread, axis=0, keepdims=True)
            along_z = jnp.dot(q[s, row(x), :], band_z, precision=EXACT, preferred_element_type=jnp.float32)
            along_z = jnp.sum(jnp.where(pick_y, along_z, 0.0), axis=0, keepdims=True)
            here = jnp.where(x_at == x, value, here)
            hor = hor + weights(jnp.abs(x_at - x)) * value + jnp.where(x_at == x, along_y, 0.0)
            ver = jnp.where(x_at == x, along_z, ver)
            apart = jnp.where(block == me + 1, x_at + 4 - x, jnp.where(block == me - 1, 4 + x - x_at, 9))
            for k in range(1, 5):
                across = across + jnp.where(apart == k, taps[k] * value, 0.0)
        mine = jnp.where(block == me, 1.0, 0.0)
        here = mine * here
        gain = mine * jnp.where(cells == source_ref[s], wavelet_ref[s, STEPS - 1], 0.0)
        early = [early_ref[s, pl.ds(k, 1), :] for k in (0, 2, 7)]
        out_ref[s, pl.ds(3, 1), :] = here
        out_ref[s, pl.ds(4, 1), :] = 2.0 * here - early[1] + (early[0] * hor + early[2] * ver) + gain
        out_ref[s, pl.ds(5, 1), :] = across


def even_pairs(n):
    return [(i, i ^ 1) for i in range(n)]


def odd_pairs(n):
    up = [(i, i + 1) for i in range(1, n - 1, 2)]
    return up + [(b, a) for a, b in up]


def stages(n):
    if n != 128:
        bit, out = 1, []
        while bit < n:
            out.append([[(i, i ^ bit) for i in range(n)]])
            bit *= 2
        return out

    def device(z, xh, y, core):
        return ((z * 2 + xh) * 4 + y) * 2 + core

    def pairs(move):
        return [
            (device(z, xh, y, core), device(*move(z, xh, y, core)))
            for z in range(8) for xh in range(2) for y in range(4) for core in range(2)
        ]

    return [
        [pairs(lambda z, xh, y, core, k=k: (z, xh, y ^ k, core)) for k in (1, 3, 2)],
        [
            pairs(lambda z, xh, y, core: (z, xh, y, 1 - core)),
            pairs(lambda z, xh, y, core: (z, 1 - xh, y, core)),
            pairs(lambda z, xh, y, core: (z, 1 - xh, y, 1 - core)),
        ],
        [
            pairs(lambda z, xh, y, core: (z ^ 1, xh, y, core)),
            pairs(lambda z, xh, y, core: ((z + 1 if z % 2 else z - 1) % 8, xh, y, core)),
        ],
        [
            pairs(lambda z, xh, y, core: ((z - 3 if z % 2 else z + 3) % 8, xh, y, core)),
            pairs(lambda z, xh, y, core: ((z + 3 if z % 2 else z - 3) % 8, xh, y, core)),
        ],
    ]


def summed(total, stage):
    for part in [lax.ppermute(total, "space", pairs) for pairs in stage]:
        total = total + part
    return total


def reduced(total, n, z_odd, gate, last_gate):
    todo = stages(n)
    if n != 128:
        total = gate(summed(total, todo[0]))
        for stage in todo[1:]:
            total = summed(total, stage)
        return last_gate(total)
    odd = z_odd == 1
    first, second = (lax.ppermute(total, "space", pairs) for pairs in todo[2])
    two = total + jnp.where(odd, first, second)
    three = total + (first + second)
    even_part, odd_part = jnp.where(odd, two, three), jnp.where(odd, three, two)
    plus = lax.ppermute(even_part, "space", todo[3][0])
    minus = lax.ppermute(odd_part, "space", todo[3][1])
    total = gate(three + (plus + minus))
    return summed(last_gate(summed(total, todo[0])), todo[1])


def per_device(pressure_now, pressure_old, auxiliary_now, auxiliary_old, velocity, epsilon_field, delta_field,
               active_blocks, source_cells, receiver_cells, wavelet):
    blocks = lax.axis_size("space")
    at = lax.axis_index("space").astype(jnp.int32).reshape(1)
    side = lax.axis_index("shot").astype(jnp.int32).reshape(1)
    fields = (2, ROWS, CZ)
    p_now, p_old, q_now, q_old = (a.reshape(fields) for a in (pressure_now, pressure_old, auxiliary_now, auxiliary_old))
    half = (ROWS // 2, CZ)
    speed, eps, delta = (a.reshape(half) for a in (velocity, epsilon_field, delta_field))
    field = shape(*fields)
    active = active_blocks.reshape(2)
    ints = [pltpu.SMEM((1,), jnp.int32), pltpu.SMEM((2,), jnp.int32), pltpu.SMEM((2,), jnp.int32)]

    own, p, odd, live, z_odd = call(
        begin_kernel, (at, side, active, source_cells, speed, eps, delta, p_now),
        (shape(3, *half), field, shape(8, CZ, dtype=jnp.int32), shape(16, CZ),
         shape(2, 8, receiver_cells.shape[1], dtype=jnp.int32)),
        10**6, "begin", far=range(8), scratch=ints + [pltpu.SemaphoreType.DMA((7,))])

    def on_chip(values):
        return lax.ppermute(values, "space", even_pairs(blocks))

    def off_chip(values):
        return lax.ppermute(values, "space", odd_pairs(blocks))

    other = lax.ppermute(own, "shot", [(0, 1), (1, 0)])
    got, pair = off_chip(p), on_chip(p)
    base_p, base_q, q, hor, ver = call(
        ready_kernel, (at, active, source_cells, wavelet, p, p_old, q_now, q_old), (field,) * 5, 10**8, "ready",
        far=(5, 6, 7), scratch=[pltpu.SemaphoreType.DMA((3,))])
    pre_p, pre_q, c, cs, ck, extra = call(
        first_kernel, (side, live, own, other, base_p, base_q, hor, ver), (*(field,) * 5, shape(ROWS + 16, CZ)),
        2 * 10**10, "first")
    part_p, part_q = call(
        chip_kernel, (odd, pair, pre_p, pre_q, cs, ck, extra), (shape(3 * ROWS + 16, CZ), field), 10**6, "chip0")
    coming = off_chip(part_p)
    po, qo = p, q
    p, q = call(first_join_kernel, (odd, got, part_p, part_q, cs, ck), (field, field), 10**6, "join0")
    extra = coming
    traced = shape(2, 8, receiver_cells.shape[1])
    for step in range(1, STEPS):
        got = coming
        pair = on_chip(p)
        now = (at, source_cells, wavelet, p, po, q, qo, c, cs, ck)
        if step == 1:
            pre_p, pre_q = call(functools.partial(local_kernel, step), now, (field, field), 2 * 10**10, "local1")
            early, = call(early_kernel, (at, receiver_cells, p, cs, ck), (traced,), 10**6, "early")
        elif step == 2:
            pre_p, pre_q, early = call(
                middle_kernel, (*now, receiver_cells, early), (field, field, traced), 10**6, "local2")
        else:
            pre_p, pre_q = call(functools.partial(local_kernel, step), now, (field, field), 10**6, "local3")
        if step == 3:
            total, = call(late_kernel, (at, source_cells, wavelet, receiver_cells, early, p, q), (traced,), 10**8, "late")
        part_p, part_q = call(
            chip_kernel, (odd, pair, pre_p, pre_q, cs, ck), (shape(2 * ROWS, CZ), field), 10**6, f"chip{step}")
        if step == 3:
            break
        coming = off_chip(part_p)
        if step == 1:
            got, coming, early = lax.optimization_barrier((got, coming, early))
            extra = got
        before, po, qo = po, p, q
        p, q = call(
            join_kernel, (odd, got, extra, before, part_p, part_q, cs, ck), (field, field), 10**6, f"join{step}")

    local = (got, part_p, part_q)

    def gate(total):
        nonlocal local
        total, local = lax.optimization_barrier((total, local))
        return total

    total = reduced(total, blocks, z_odd, lambda total: total, gate)
    got, part_p, part_q = local
    p, q = call(join_kernel, (odd, got, extra, po, part_p, part_q, cs, ck), (field, field), 2 * 10**10, "join3")
    last = total[:, 4] + total[:, 0] * total[:, 5]
    traces = jnp.stack([total[:, 1], total[:, 2], total[:, 3], last], axis=1)
    return (p.reshape(pressure_now.shape), q.reshape(pressure_now.shape), traces)


def solution(mesh):
    grid = P("shot", "space", None, None, None)
    model = P("space", "shot", None, None)
    return jax.shard_map(
        per_device,
        mesh=mesh,
        in_specs=(grid, grid, grid, grid, model, model, model, P("shot", "space"), P("shot"), P("shot", None), P("shot", None)),
        out_specs=(grid, grid, P("shot", None, None)),
        check_vma=False,
    )
```

```python
import functools

import jax
import jax.numpy as jnp
from jax import lax
from jax.experimental import pallas as pl
from jax.experimental.pallas import tpu as pltpu
from jax.sharding import PartitionSpec as P

STEPS = 4
CX, CY, CZ = 4, 128, 128
ROWS = CX * CY
CELLS = ROWS * CZ

taps = (-205.0 / 72.0, 8.0 / 5.0, -1.0 / 5.0, 8.0 / 315.0, -1.0 / 560.0)
step_ratio = 0.08

VMEM = pl.BlockSpec(memory_space=pltpu.VMEM)
SMEM = pl.BlockSpec(memory_space=pltpu.SMEM)
FAR = pl.BlockSpec(memory_space=pltpu.HBM)
EXACT = lax.Precision.HIGHEST


def shape(*dims, dtype=jnp.float32):
    return jax.ShapeDtypeStruct(dims, dtype)


def call(kernel, ins, outs, flops, name, far=(), scratch=()):
    moved = 4 * sum(int(jnp.size(a)) for a in ins) + 4 * sum(o.size for o in outs)
    ins = [pltpu.with_memory_space_constraint(a, pltpu.HBM) if n in far else a for n, a in enumerate(ins)]
    specs = [FAR if n in far else SMEM if a.size <= 64 else VMEM for n, a in enumerate(ins)]
    return pl.pallas_call(
        kernel,
        out_shape=tuple(outs),
        in_specs=specs,
        out_specs=tuple(VMEM for _ in outs),
        scratch_shapes=scratch,
        compiler_params=pltpu.CompilerParams(vmem_limit_bytes=16 << 20),
        cost_estimate=pl.CostEstimate(flops=flops, bytes_accessed=moved, transcendentals=0),
        name=name,
    )(*ins)


def live_of(at_ref, active_ref, source_ref, s):
    here = source_ref[s] // CELLS == at_ref[0]
    return jnp.where(here | (active_ref[s] == 1), 1.0, 0.0)


def row(x):
    return pl.ds(x * CY, CY)


def begin_kernel(at_far, side_far, active_far, source_far, v_far, e_far, d_far, p_far,
                 own_ref, p0_ref, odd_ref, live_ref, z_odd_ref, at_ref, active_ref, source_ref, sems):
    pairs = (
        (v_far, own_ref.at[0]), (e_far, own_ref.at[1]), (d_far, own_ref.at[2]),
        (at_far, at_ref), (active_far, active_ref), (source_far, source_ref), (p_far, p0_ref))
    copies = [pltpu.make_async_copy(src, dst, sems.at[n]) for n, (src, dst) in enumerate(pairs)]
    for copy in copies:
        copy.start()
    for copy in copies[:3]:
        copy.wait()
    courant = (own_ref[0] * step_ratio) * (own_ref[0] * step_ratio)
    coupling = jnp.sqrt(1.0 + 2.0 * own_ref[2])
    own_ref[0] = courant
    own_ref[1] = courant * (1.0 + 2.0 * own_ref[1])
    own_ref[2] = courant * coupling
    for copy in copies[3:]:
        copy.wait()
    for s in range(2):
        live = live_of(at_ref, active_ref, source_ref, s)
        p0_ref[s] = p0_ref[s] * live
        live_ref[pl.ds(8 * s, 8), :] = jnp.full((8, CZ), live, jnp.float32)
    odd_ref[...] = jnp.full(odd_ref.shape, at_ref[0] & 1, jnp.int32)
    z_odd_ref[...] = jnp.full(z_odd_ref.shape, (at_ref[0] // 16) & 1, jnp.int32)


def band():
    apart = jnp.abs(lax.broadcasted_iota(jnp.int32, (CZ, CZ), 0) - lax.broadcasted_iota(jnp.int32, (CZ, CZ), 1))
    out = jnp.zeros((CZ, CZ), jnp.float32)
    for k in range(5):
        out = jnp.where(apart == k, taps[k], out)
    return out


def vertical(s, q, mat):
    return jnp.dot(q[s], mat, precision=EXACT, preferred_element_type=jnp.float32)


def horizontal(s, x, p, mat):
    hor = jnp.dot(mat, p[s, row(x), :], precision=EXACT, preferred_element_type=jnp.float32)
    for other in range(CX):
        hor = hor + taps[abs(other - x)] * p[s, row(other), :]
    return hor


def add_source(s, step, at_ref, source_ref, wavelet_ref, *refs):
    cell = source_ref[s] % CELLS
    gain = jnp.where(source_ref[s] // CELLS == at_ref[0], wavelet_ref[s, step], 0.0)
    lane = lax.broadcasted_iota(jnp.int32, (1, CZ), 1)
    add = jnp.where(lane == cell % CZ, gain, 0.0)
    line = pl.ds(cell // CZ, 1)
    for ref in refs:
        ref[s, line, :] = ref[s, line, :] + add


def ready_kernel(at_ref, active_ref, source_ref, wavelet_ref, p0, po_far, q_far, qo_far,
                 base_p, base_q, q, hor_ref, ver_ref, sems):
    copies = [
        pltpu.make_async_copy(src, dst, sems.at[n])
        for n, (src, dst) in enumerate(((q_far, q), (po_far, base_p), (qo_far, base_q)))
    ]
    for copy in copies:
        copy.start()
    mat = band()
    for copy in copies:
        copy.wait()
    for s in range(2):
        live = live_of(at_ref, active_ref, source_ref, s)
        q[s] = q[s] * live
        base_p[s] = 2.0 * p0[s] - base_p[s] * live
        base_q[s] = 2.0 * q[s] - base_q[s] * live
        ver_ref[s] = vertical(s, q, mat)
        for x in range(CX):
            hor_ref[s, row(x), :] = horizontal(s, x, p0, mat)
        add_source(s, 0, at_ref, source_ref, wavelet_ref, base_p, base_q)


def side_diff(x, rows, upper):
    above = below = taps[4] * rows[x]
    for k in range(1, 4):
        if x + k < CX:
            below = below + taps[4 - k] * rows[x + k]
        if x - k >= 0:
            above = above + taps[4 - k] * rows[x - k]
    return jnp.where(upper, above, below)


def tile_at(x, tile):
    return pl.ds(x * CY + tile * 8, 8)


def flat_at(s, x, tile):
    return pl.ds(s * ROWS + x * CY + tile * 8, 8)


def first_kernel(side_ref, live_ref, own, other, base_p, base_q, hor_ref, ver_ref, pre_p, pre_q, c_ref, cs_ref, ck_ref, extra_ref):
    extra_ref[pl.ds(ROWS, 16), :] = live_ref[...]

    def work(first, second):
        for tile in range(CY // 8):
            model = []
            for x in range(CX):
                half = (first, second)[x // 2]
                at = tile_at(x % 2, tile)
                model.append((half[0, at, :], half[1, at, :], half[2, at, :]))
                extra_ref[tile_at(x, tile), :] = model[x][1]
            for s in range(2):
                live = live_ref[pl.ds(8 * s, 8), :]
                for x in range(CX):
                    at = tile_at(x, tile)
                    c, cs, ck = (m * live for m in model[x])
                    c_ref[s, at, :], cs_ref[s, at, :], ck_ref[s, at, :] = c, cs, ck
                    hor, ver = hor_ref[s, at, :], ver_ref[s, at, :]
                    pre_p[s, at, :] = base_p[s, at, :] + (cs * hor + ck * ver)
                    pre_q[s, at, :] = base_q[s, at, :] + (ck * hor + c * ver)

    @pl.when(side_ref[0] == 0)
    def _():
        work(own, other)

    @pl.when(side_ref[0] == 1)
    def _():
        work(other, own)


def local_part(step, at_ref, source_ref, wavelet_ref, p, po, q, qo, c_ref, cs_ref, ck_ref, pre_p, pre_q):
    mat = band()
    for s in range(2):
        all_ver = vertical(s, q, mat)
        for x in range(CX):
            here = row(x)
            hor, ver = horizontal(s, x, p, mat), all_ver[x * CY:(x + 1) * CY]
            pre_p[s, here, :] = 2.0 * p[s, here, :] - po[s, here, :] + (cs_ref[s, here, :] * hor + ck_ref[s, here, :] * ver)
            pre_q[s, here, :] = 2.0 * q[s, here, :] - qo[s, here, :] + (ck_ref[s, here, :] * hor + c_ref[s, here, :] * ver)
        add_source(s, step, at_ref, source_ref, wavelet_ref, pre_p, pre_q)


def chip_kernel(odd_ref, even_pair, pre_p, pre_q, cs_ref, ck_ref, *rest):
    extra, (out_p, out_q) = rest[:-2], rest[-2:]
    upper = odd_ref[...] == 0
    for ref in extra:
        out_p[pl.ds(2 * ROWS, ROWS + 16), :] = ref[...]
    for s in range(2):
        for tile in range(CY // 8):
            rows = [even_pair[s, tile_at(x, tile), :] for x in range(CX)]
            for x in range(CX):
                at = tile_at(x, tile)
                hor = side_diff(x, rows, upper)
                out_p[flat_at(s, x, tile), :] = pre_p[s, at, :] + cs_ref[s, at, :] * hor
                out_q[s, at, :] = pre_q[s, at, :] + ck_ref[s, at, :] * hor


def join(odd_ref, other_rows, part_p, part_q, cs_ref, ck_ref, p, q):
    upper = odd_ref[...] == 1
    for s in range(2):
        for tile in range(CY // 8):
            rows = other_rows(s, tile)
            for x in range(CX):
                at = tile_at(x, tile)
                hor = side_diff(x, rows, upper)
                p[s, at, :] = part_p[flat_at(s, x, tile), :] + cs_ref[s, at, :] * hor
                q[s, at, :] = part_q[s, at, :] + ck_ref[s, at, :] * hor


def first_join_kernel(odd_ref, got, part_p, part_q, cs_ref, ck_ref, p, q):
    def other_rows(s, tile):
        return [got[s, tile_at(x, tile), :] for x in range(CX)]

    join(odd_ref, other_rows, part_p, part_q, cs_ref, ck_ref, p, q)


def join_kernel(odd_ref, got, extra, before, part_p, part_q, cs_ref, ck_ref, p, q):
    upper = odd_ref[...] == 0

    def other_rows(s, tile):
        mine = [before[s, tile_at(x, tile), :] for x in range(CX)]
        live = extra[pl.ds(3 * ROWS + 8 * s, 8), :]
        out = []
        for x in range(CX):
            stretch = extra[pl.ds(2 * ROWS + x * CY + tile * 8, 8), :] * live
            out.append(got[flat_at(s, x, tile), :] + stretch * side_diff(x, mine, upper))
        return out

    join(odd_ref, other_rows, part_p, part_q, cs_ref, ck_ref, p, q)


def spread_rows(field, s, pick_z):
    rest, spread = field[s], None
    for _ in range(3):
        part = rest.astype(jnp.bfloat16)
        rest = rest - part.astype(jnp.float32)
        picked = jnp.dot(part, pick_z, preferred_element_type=jnp.float32)
        spread = picked if spread is None else spread + picked
    return [spread[x * CY:(x + 1) * CY] for x in range(CX)]


def samples(field, s, pick_z, pick_y):
    out = []
    for spread in spread_rows(field, s, pick_z):
        out.append(jnp.sum(jnp.where(pick_y, spread, 0.0), axis=0, keepdims=True))
    return out


def picks(cells_ref, s):
    cells = cells_ref[pl.ds(s, 1), :]
    n = cells.shape[1]
    inside = cells % CELLS
    pick_z = jnp.where(lax.broadcasted_iota(jnp.int32, (CZ, n), 0) == inside % CZ, 1.0, 0.0).astype(jnp.bfloat16)
    pick_y = lax.broadcasted_iota(jnp.int32, (CY, n), 0) == (inside // CZ) % CY
    return cells // CELLS, inside // (CY * CZ), pick_z, pick_y


def own_sample(values, block, x_at, me):
    out = jnp.zeros(block.shape, jnp.float32)
    for x in range(CX):
        out = jnp.where((x_at == x) & (block == me), values[x], out)
    return out


def local_kernel(step, at_ref, source_ref, wavelet_ref, p, po, q, qo, c_ref, cs_ref, ck_ref, pre_p, pre_q):
    local_part(step, at_ref, source_ref, wavelet_ref, p, po, q, qo, c_ref, cs_ref, ck_ref, pre_p, pre_q)


def early_kernel(at_ref, cells_ref, p, cs_ref, ck_ref, out_ref):
    out_ref[...] = jnp.zeros(out_ref.shape, jnp.float32)
    for s in range(2):
        block, x_at, pick_z, pick_y = picks(cells_ref, s)
        for n, field in ((0, cs_ref), (1, p), (7, ck_ref)):
            out_ref[s, pl.ds(n, 1), :] = own_sample(samples(field, s, pick_z, pick_y), block, x_at, at_ref[0])


def middle_kernel(at_ref, source_ref, wavelet_ref, p, po, q, qo, c_ref, cs_ref, ck_ref, cells_ref, early_ref,
                  pre_p, pre_q, out_ref):
    local_part(2, at_ref, source_ref, wavelet_ref, p, po, q, qo, c_ref, cs_ref, ck_ref, pre_p, pre_q)
    out_ref[...] = early_ref[...]
    for s in range(2):
        block, x_at, pick_z, pick_y = picks(cells_ref, s)
        out_ref[s, pl.ds(2, 1), :] = own_sample(samples(p, s, pick_z, pick_y), block, x_at, at_ref[0])


def weights(apart):
    out = jnp.zeros(apart.shape, jnp.float32)
    for k in range(5):
        out = jnp.where(apart == k, taps[k], out)
    return out


def late_kernel(at_ref, source_ref, wavelet_ref, cells_ref, early_ref, p, q, out_ref):
    me = at_ref[0]
    out_ref[...] = early_ref[...]
    for s in range(2):
        block, x_at, pick_z, pick_y = picks(cells_ref, s)
        cells = cells_ref[pl.ds(s, 1), :]
        n = cells.shape[1]
        band_z = weights(jnp.abs(lax.broadcasted_iota(jnp.int32, (CZ, n), 0) - cells % CZ))
        band_y = weights(jnp.abs(lax.broadcasted_iota(jnp.int32, (CY, n), 0) - (cells // CZ) % CY))
        here = jnp.zeros(block.shape, jnp.float32)
        hor, ver, across = here, here, here
        all_z = jnp.dot(q[s], band_z, precision=EXACT, preferred_element_type=jnp.float32)
        for x, spread in enumerate(spread_rows(p, s, pick_z)):
            value = jnp.sum(jnp.where(pick_y, spread, 0.0), axis=0, keepdims=True)
            along_y = jnp.sum(band_y * spread, axis=0, keepdims=True)
            along_z = jnp.sum(jnp.where(pick_y, all_z[x * CY:(x + 1) * CY], 0.0), axis=0, keepdims=True)
            here = jnp.where(x_at == x, value, here)
            hor = hor + weights(jnp.abs(x_at - x)) * value + jnp.where(x_at == x, along_y, 0.0)
            ver = jnp.where(x_at == x, along_z, ver)
            apart = jnp.where(block == me + 1, x_at + 4 - x, jnp.where(block == me - 1, 4 + x - x_at, 9))
            for k in range(1, 5):
                across = across + jnp.where(apart == k, taps[k] * value, 0.0)
        mine = jnp.where(block == me, 1.0, 0.0)
        here = mine * here
        gain = mine * jnp.where(cells == source_ref[s], wavelet_ref[s, STEPS - 1], 0.0)
        early = [early_ref[s, pl.ds(k, 1), :] for k in (0, 2, 7)]
        out_ref[s, pl.ds(3, 1), :] = here
        out_ref[s, pl.ds(4, 1), :] = 2.0 * here - early[1] + (early[0] * hor + early[2] * ver) + gain
        out_ref[s, pl.ds(5, 1), :] = across


def even_pairs(n):
    return [(i, i ^ 1) for i in range(n)]


def odd_pairs(n):
    up = [(i, i + 1) for i in range(1, n - 1, 2)]
    return up + [(b, a) for a, b in up]


def stages(n):
    if n != 128:
        bit, out = 1, []
        while bit < n:
            out.append([[(i, i ^ bit) for i in range(n)]])
            bit *= 2
        return out

    def device(z, xh, y, core):
        return ((z * 2 + xh) * 4 + y) * 2 + core

    def pairs(move):
        return [
            (device(z, xh, y, core), device(*move(z, xh, y, core)))
            for z in range(8) for xh in range(2) for y in range(4) for core in range(2)
        ]

    return [
        [pairs(lambda z, xh, y, core, k=k: (z, xh, y ^ k, core)) for k in (1, 3, 2)],
        [
            pairs(lambda z, xh, y, core: (z, xh, y, 1 - core)),
            pairs(lambda z, xh, y, core: (z, 1 - xh, y, core)),
            pairs(lambda z, xh, y, core: (z, 1 - xh, y, 1 - core)),
        ],
        [
            pairs(lambda z, xh, y, core: (z ^ 1, xh, y, core)),
            pairs(lambda z, xh, y, core: ((z + 1 if z % 2 else z - 1) % 8, xh, y, core)),
        ],
        [
            pairs(lambda z, xh, y, core: ((z - 3 if z % 2 else z + 3) % 8, xh, y, core)),
            pairs(lambda z, xh, y, core: ((z + 3 if z % 2 else z - 3) % 8, xh, y, core)),
        ],
    ]


def summed(total, stage):
    for part in [lax.ppermute(total, "space", pairs) for pairs in stage]:
        total = total + part
    return total


def reduced(total, n, z_odd, gate, last_gate):
    todo = stages(n)
    if n != 128:
        total = gate(summed(total, todo[0]))
        for stage in todo[1:]:
            total = summed(total, stage)
        return last_gate(total)
    odd = z_odd == 1
    first, second = (lax.ppermute(total, "space", pairs) for pairs in todo[2])
    two = total + jnp.where(odd, first, second)
    three = total + (first + second)
    even_part, odd_part = jnp.where(odd, two, three), jnp.where(odd, three, two)
    plus = lax.ppermute(even_part, "space", todo[3][0])
    minus = lax.ppermute(odd_part, "space", todo[3][1])
    total = gate(three + (plus + minus))
    return summed(last_gate(summed(total, todo[0])), todo[1])


def per_device(pressure_now, pressure_old, auxiliary_now, auxiliary_old, velocity, epsilon_field, delta_field,
               active_blocks, source_cells, receiver_cells, wavelet):
    blocks = lax.axis_size("space")
    at = lax.axis_index("space").astype(jnp.int32).reshape(1)
    side = lax.axis_index("shot").astype(jnp.int32).reshape(1)
    fields = (2, ROWS, CZ)
    p_now, p_old, q_now, q_old = (a.reshape(fields) for a in (pressure_now, pressure_old, auxiliary_now, auxiliary_old))
    half = (ROWS // 2, CZ)
    speed, eps, delta = (a.reshape(half) for a in (velocity, epsilon_field, delta_field))
    field = shape(*fields)
    active = active_blocks.reshape(2)
    ints = [pltpu.SMEM((1,), jnp.int32), pltpu.SMEM((2,), jnp.int32), pltpu.SMEM((2,), jnp.int32)]

    own, p, odd, live, z_odd = call(
        begin_kernel, (at, side, active, source_cells, speed, eps, delta, p_now),
        (shape(3, *half), field, shape(8, CZ, dtype=jnp.int32), shape(16, CZ),
         shape(2, 8, receiver_cells.shape[1], dtype=jnp.int32)),
        10**6, "begin", far=range(8), scratch=ints + [pltpu.SemaphoreType.DMA((7,))])

    def on_chip(values):
        return lax.ppermute(values, "space", even_pairs(blocks))

    def off_chip(values):
        return lax.ppermute(values, "space", odd_pairs(blocks))

    other = lax.ppermute(own, "shot", [(0, 1), (1, 0)])
    got, pair = off_chip(p), on_chip(p)
    base_p, base_q, q, hor, ver = call(
        ready_kernel, (at, active, source_cells, wavelet, p, p_old, q_now, q_old), (field,) * 5, 10**8, "ready",
        far=(5, 6, 7), scratch=[pltpu.SemaphoreType.DMA((3,))])
    pre_p, pre_q, c, cs, ck, extra = call(
        first_kernel, (side, live, own, other, base_p, base_q, hor, ver), (*(field,) * 5, shape(ROWS + 16, CZ)),
        2 * 10**10, "first")
    part_p, part_q = call(
        chip_kernel, (odd, pair, pre_p, pre_q, cs, ck, extra), (shape(3 * ROWS + 16, CZ), field), 10**6, "chip0")
    coming = off_chip(part_p)
    po, qo = p, q
    p, q = call(first_join_kernel, (odd, got, part_p, part_q, cs, ck), (field, field), 10**6, "join0")
    extra = coming
    traced = shape(2, 8, receiver_cells.shape[1])
    for step in range(1, STEPS):
        got = coming
        pair = on_chip(p)
        now = (at, source_cells, wavelet, p, po, q, qo, c, cs, ck)
        if step == 1:
            pre_p, pre_q = call(functools.partial(local_kernel, step), now, (field, field), 2 * 10**10, "local1")
            early, = call(early_kernel, (at, receiver_cells, p, cs, ck), (traced,), 10**6, "early")
        elif step == 2:
            pre_p, pre_q, early = call(
                middle_kernel, (*now, receiver_cells, early), (field, field, traced), 10**6, "local2")
        else:
            pre_p, pre_q = call(functools.partial(local_kernel, step), now, (field, field), 10**6, "local3")
        if step == 3:
            total, = call(late_kernel, (at, source_cells, wavelet, receiver_cells, early, p, q), (traced,), 10**8, "late")
        part_p, part_q = call(
            chip_kernel, (odd, pair, pre_p, pre_q, cs, ck), (shape(2 * ROWS, CZ), field), 10**6, f"chip{step}")
        if step == 3:
            break
        coming = off_chip(part_p)
        if step == 1:
            got, coming, early = lax.optimization_barrier((got, coming, early))
            extra = got
        before, po, qo = po, p, q
        p, q = call(
            join_kernel, (odd, got, extra, before, part_p, part_q, cs, ck), (field, field), 10**6, f"join{step}")

    local = (got, part_p, part_q)

    def gate(total):
        nonlocal local
        total, local = lax.optimization_barrier((total, local))
        return total

    total = reduced(total, blocks, z_odd, lambda total: total, gate)
    got, part_p, part_q = local
    p, q = call(join_kernel, (odd, got, extra, po, part_p, part_q, cs, ck), (field, field), 2 * 10**10, "join3")
    last = total[:, 4] + total[:, 0] * total[:, 5]
    traces = jnp.stack([total[:, 1], total[:, 2], total[:, 3], last], axis=1)
    return (p.reshape(pressure_now.shape), q.reshape(pressure_now.shape), traces)


def solution(mesh):
    grid = P("shot", "space", None, None, None)
    model = P("space", "shot", None, None)
    return jax.shard_map(
        per_device,
        mesh=mesh,
        in_specs=(grid, grid, grid, grid, model, model, model, P("shot", "space"), P("shot"), P("shot", None), P("shot", None)),
        out_specs=(grid, grid, P("shot", None, None)),
        check_vma=False,
    )
```
